32 devices in a mesh: ang: 8 (over z, y), row: 4 (over x, core).
Axes of the slice: x: 2, y: 2, z: 4, core: 2. Of those that a mesh axis runs over, the one named last changes fastest.
Arguments:
- raw: bfloat16 [2304, 2048], P(('row', 'ang')), parts along dimension 0, may hold values from 6e-05 to 1, as said below
- block_dest: int32 [576], P('ang'), may hold values from 0 to 575, as said below
- section_offset: int32 [64, 9], P('ang'), may hold values from 0 to 14336, as said below
- ramp_length: int32 [9], replicated, may hold values from 16 to 256
- module_width: int32 [8], replicated, may hold values from 1 to 4096, 16384 in all
Outputs:
- filtered: float32 [256, 16384], P(('row', 'ang')), parts along dimension 0
The draws below stay inside these ranges and needn't reach their ends.
There are 4 independent parts, one for each index of `row`. The reference program is written for one: setup_inputs(seed, part) draws one part's arguments, and reference() takes and returns one part's arrays. A program takes and returns all parts, laid end to end along the dimension named above; an argument that names none is the same for every part. Nothing has to cross between parts.
Inputs may be any that keep to these rules, and one draw needn't show every extreme that they name: `block_dest`: A permutation of the tile rows. Each index of ang holds 72 of them, at most 9 for any one index of ang that owns their angle (angle a is owned by index a // 8), and in every draw some index holds exactly 9 for some owner. `section_offset`: tile 0 starts at column 0 and the last tile at 14336 at every angle; tile t otherwise lies within 64 columns of t * 1792. `module_width`: the widths sum to 16384; the widest module has exactly 4096 columns. `raw`: positive intensities.
All inputs are finite; a program needn't handle non-finite values.
Results may differ from the reference program's by a relative error of at most 0.0014.
Values may be sent and summed in bfloat16 or wider, within the bound.
A program may use at most 64 MiB of HBM per device.

```python
import math
import jax
import jax.numpy as jnp
import numpy as np
from jax import lax

ANG_DEV = 8
W = 16384
TW = 2048
NT = 9
JITTER = 64
RAMP_HALF = 128
ANGLES = 64
STEP = 1792
BLOCKS = 576
NSEG = 8
WMAX = 4096
N_ANG = 8


def draw_raw(key, part):
    key_scale, key_depth, key_rows = jax.random.split(key, 3)
    col_scale = jnp.exp(jax.random.uniform(key_scale, (TW,), jnp.float32, 0.0, math.log(10.0)))
    depths = jnp.minimum(jnp.abs(jax.random.normal(key_depth, (BLOCKS, TW), jnp.float32)) * 0.1, 0.3)
    row_scale = jnp.exp(jax.random.uniform(key_rows, (BLOCKS, 1), jnp.float32, math.log(0.5), math.log(2.0)))
    return jnp.exp(-col_scale[None, :] * depths * row_scale).astype(jnp.bfloat16)


def draw_block_dest(key, part):
    per_owner = ANG_DEV * NT
    key_owner, key_source, key_local, key_order = jax.random.split(key, 4)
    owner_perm = jax.random.permutation(key_owner, N_ANG).astype(jnp.int32)
    source_perm = jax.random.permutation(key_source, N_ANG).astype(jnp.int32)
    local_keys = jax.random.split(key_local, N_ANG)
    local_perm = jax.vmap(lambda single: jax.random.permutation(single, per_owner))(local_keys).astype(jnp.int32)
    linear = jnp.arange(N_ANG, dtype=jnp.int32)[:, None] * per_owner + jnp.arange(per_owner, dtype=jnp.int32)[None, :]
    sources = source_perm[linear % N_ANG]
    block_ids = owner_perm[:, None] * per_owner + local_perm
    tie_break = jax.random.permutation(key_order, N_ANG * per_owner).astype(jnp.int32)
    sort_keys = sources.reshape(-1) * (N_ANG * per_owner) + tie_break
    order = jnp.argsort(sort_keys)
    return block_ids.reshape(-1)[order].astype(jnp.int32)


def draw_section_offset(key, part):
    jitter = jax.random.randint(key, (ANGLES, NT), -JITTER, JITTER + 1, dtype=jnp.int32)
    tile_index = jnp.arange(NT, dtype=jnp.int32)[None, :]
    interior = (tile_index > 0) & (tile_index < NT - 1)
    nominal = jnp.where(tile_index == NT - 1, W - TW, tile_index * STEP)
    return (nominal + jnp.where(interior, jitter, 0)).astype(jnp.int32)


def place_ends(array, own_key, least, largest):
    longest = array.shape.index(max(array.shape))
    spots = []
    for shift in (0, 1):
        where = [jax.random.randint(jax.random.fold_in(own_key, axis), (), 0, length) for axis, length in enumerate(array.shape)]
        where[longest] = (where[longest] + shift) % array.shape[longest]
        spots.append(tuple(where))
    return array.at[spots[0]].set(least).at[spots[1]].set(largest)


def split_up(number_of, total, most, skew):
    portions = [(1 << 20) // math.isqrt(rank ** skew) + 1 for rank in range(2, number_of + 1)]
    spare, holding = total - most - (number_of - 1), [1] * (number_of - 1)
    while spare > 0:
        free = [i for i in range(number_of - 1) if holding[i] < most]
        pool, left = sum([portions[i] for i in free]), spare
        for i in free:
            more = min(most - holding[i], max(1, left * portions[i] // pool), spare)
            holding[i] = holding[i] + more
            spare = spare - more
    return np.array([most] + holding)


def uneven(stream_key, count, total, most, slope):
    if count == 2:
        one = jax.random.randint(stream_key, (), max(1, total - most), min(most, total - 1) + 1)
        return jnp.stack([one, total - one])
    sizes = jnp.asarray(split_up(count, total, most, slope), jnp.int32)
    couples = (count - 1) // 2
    giver, receiver = sizes[1:1 + 2 * couples:2], sizes[2:2 + 2 * couples:2]
    margin = jnp.minimum(giver - 1, most - receiver)
    moved = jax.random.randint(jax.random.fold_in(stream_key, 1), (couples,), 0, 1 << 20) % (margin + 1)
    sizes = sizes.at[1:1 + 2 * couples:2].set(giver - moved).at[2:2 + 2 * couples:2].set(receiver + moved)
    return sizes[jax.random.permutation(jax.random.fold_in(stream_key, 2), count)]


def setup_inputs(seed: int = 0, part: int = 0) -> dict:
    key_of = jax.random.split(jax.random.key(seed), 6)
    own_keys = jax.random.split(jax.random.fold_in(key_of[5], part), 6)
    raw = draw_raw(jax.random.fold_in(jax.random.fold_in(key_of[5], part), 71), part)
    block_dest = draw_block_dest(jax.random.fold_in(key_of[5], 71), part)
    section_offset = draw_section_offset(jax.random.fold_in(key_of[5], 71), part)
    ramp_length = place_ends(jax.random.randint(key_of[3], (NT,), 16, TW - STEP + 1), jax.random.fold_in(key_of[3], 1), 16, TW - STEP).astype(jnp.int32)
    module_width = uneven(key_of[4], NSEG, W, WMAX, 2).astype(jnp.int32)
    return {"raw": raw, "block_dest": block_dest, "section_offset": section_offset, "ramp_length": ramp_length, "module_width": module_width}


SHRINK_SCALE = 1.0
EPSILON = 1e-6


def ramp_taps(offsets):
    values = offsets.astype(jnp.float32)
    nonzero = jnp.where(offsets == 0, jnp.float32(1.0), values)
    odd_mask = (offsets % 2) != 0
    taps = jnp.where(odd_mask, -1.0 / (math.pi * math.pi * nonzero * nonzero), jnp.float32(0.0))
    taps = jnp.where(offsets == 0, jnp.float32(0.25), taps)
    return jnp.where(jnp.abs(offsets) <= RAMP_HALF, taps, jnp.float32(0.0))


def reference(raw, block_dest, section_offset, ramp_length, module_width):
    tile_grid = jnp.zeros((ANGLES * NT, TW), jnp.float32).at[block_dest].set(raw.astype(jnp.float32))
    tile_grid = tile_grid.reshape(ANGLES, NT, TW)
    columns = jnp.arange(W, dtype=jnp.int32)
    weighted_sum = jnp.zeros((ANGLES, W), jnp.float32)
    weight_sum = jnp.zeros((ANGLES, W), jnp.float32)
    for tile in range(NT):
        position = columns[None, :] - section_offset[:, tile][:, None]
        inside = (position >= 0) & (position < TW)
        clipped = jnp.clip(position, 0, TW - 1).astype(jnp.int32)
        values = jnp.take_along_axis(tile_grid[:, tile, :], clipped, axis=1)
        ramp = (jnp.minimum(clipped, TW - 1 - clipped) + 1).astype(jnp.float32) / ramp_length[tile].astype(jnp.float32)
        feather = jnp.where(inside, jnp.minimum(jnp.float32(1.0), ramp), jnp.float32(0.0))
        weighted_sum = weighted_sum + feather * values
        weight_sum = weight_sum + feather
    projection = -jnp.log(weighted_sum / weight_sum)
    bounds = jnp.cumsum(module_width).astype(jnp.int32)
    starts = bounds - module_width
    member = ((columns[:, None] >= starts[None, :]) & (columns[:, None] < bounds[None, :])).astype(jnp.float32)
    widths = module_width.astype(jnp.float32)
    module_mean = jnp.dot(projection, member, precision=lax.Precision.HIGHEST) / widths[None, :]
    centered = projection - jnp.dot(module_mean, member.T, precision=lax.Precision.HIGHEST)
    spectrum = jnp.fft.fft(centered, axis=0)
    magnitude = jnp.abs(spectrum)
    totals = jnp.dot(jnp.sum(magnitude, axis=0), member, precision=lax.Precision.HIGHEST)
    level = SHRINK_SCALE * (totals / (ANGLES * widths) + EPSILON)
    level_col = jnp.dot(member, level, precision=lax.Precision.HIGHEST)
    freqs = jnp.arange(ANGLES, dtype=jnp.int32)
    wrapped = jnp.minimum(freqs, ANGLES - freqs).astype(jnp.float32)
    band_weight = jnp.exp(-wrapped / (ANGLES // 8))
    factor = jnp.maximum(magnitude - level_col[None, :], 0.0) / jnp.maximum(magnitude, level_col[None, :])
    shrunk = spectrum * (factor * band_weight[:, None])
    stripe = jnp.real(jnp.fft.ifft(shrunk, axis=0))
    clean = projection - stripe
    taps = ramp_taps(jnp.arange(-RAMP_HALF, RAMP_HALF + 1, dtype=jnp.int32))

    def filter_row(single):
        return jnp.convolve(single, taps, mode="same", precision=lax.Precision.HIGHEST)

    return jax.vmap(filter_row)(clean)
```

```python
import functools
import math

import jax
import jax.numpy as jnp
import ml_dtypes
import numpy as np
from jax import lax
from jax.experimental import pallas as pl
from jax.experimental.pallas import tpu as pltpu
from jax.sharding import PartitionSpec as P

W = 16384
RAMP_HALF = 128
JITTER = 64
SHRINK_SCALE = 1.0
EPSILON = 1e-06
LANES = 128
SPAN = 2048
SHARED = 0.625

F32 = jnp.float32
BF16 = jnp.bfloat16


def split_np(table):
    high = table.astype(ml_dtypes.bfloat16)
    low = (table - high.astype(np.float64)).astype(ml_dtypes.bfloat16)
    return high, low


def freq_rows(angles):
    return -(-(angles // 2 + 1) // 8) * 8


def forward_table(angles, devices, fold):
    rows = freq_rows(angles)
    here = angles // devices
    k = np.arange(rows)[:, None]
    a = np.arange(angles)[None, :]
    phase = 2.0 * np.pi * ((k * a) % angles) / angles
    keep = (k <= angles // 2).astype(np.float64)
    table = np.concatenate([np.cos(phase) * keep, -np.sin(phase) * keep], axis=0)
    placed = np.zeros((fold, 2 * rows, devices, fold, here))
    for part in range(fold):
        placed[part, :, :, part, :] = table.reshape(2 * rows, devices, here)
    high, low = split_np(placed.reshape(fold, 2 * rows, devices * fold * here))
    return np.concatenate([high, low], axis=1)


def inverse_table(angles, devices, fold):
    rows = freq_rows(angles)
    k = np.arange(rows)[None, :]
    a = np.arange(angles)[:, None]
    phase = 2.0 * np.pi * ((k * a) % angles) / angles
    twice = np.where((k == 0) | (2 * k == angles), 1.0, 2.0) * (k <= angles // 2)
    weight = twice * np.exp(-np.minimum(k, angles - k) / (angles // 8)) / angles
    table = np.concatenate([np.cos(phase) * weight, -np.sin(phase) * weight], axis=1)
    high, low = split_np(table)
    table = np.concatenate([high, high, low], axis=1)
    if fold == 1:
        return table[None]
    here = angles // devices
    shared = np.kron(np.eye(devices), np.ones((here, here))) * (SHARED / here)
    placed = np.zeros((fold, angles, devices, fold, here))
    for part in range(fold):
        placed[part, :, :, part, :] = -shared.reshape(angles, devices, here)
    placed = placed.reshape(fold, angles, devices * fold * here).astype(ml_dtypes.bfloat16)
    return np.concatenate([np.broadcast_to(table, (fold,) + table.shape), placed], axis=2)


def ramp_table():
    i = np.arange(3 * LANES)[:, None] - LANES
    n = np.arange(LANES)[None, :] - i
    safe = np.where(n == 0, 1, n).astype(np.float64)
    taps = np.where(n % 2 != 0, -1.0 / (np.pi * np.pi * safe * safe), 0.0)
    taps = np.where(n == 0, 0.25, taps)
    taps = np.where(np.abs(n) <= RAMP_HALF, taps, 0.0)
    high, low = split_np(taps)
    return np.stack([high, low])


def dot(left, right):
    return jnp.dot(left, right, preferred_element_type=F32)


def dot_nt(left, right):
    return lax.dot_general(left, right, (((1,), (1,)), ((), ())), preferred_element_type=F32)


def halves(x):
    high = x.astype(BF16)
    return high, (x - high.astype(F32)).astype(BF16)


def thirds(x):
    high = x.astype(BF16).astype(F32)
    rest = x - high
    mid = rest.astype(BF16).astype(F32)
    low = rest - mid
    return jnp.concatenate([high, mid, low, jnp.zeros_like(x)], axis=0).astype(BF16)


def iota(shape, axis):
    return lax.broadcasted_iota(jnp.int32, shape, axis)


def loop(count, body):
    if count <= 8:
        for step in range(count):
            body(step)
    else:

        def run(step, carry):
            body(step)
            return carry

        lax.fori_loop(0, count, run, 0)


def kernel(
    cfg,
    raw_ref,
    dest_ref,
    offset_ref,
    ramp_ref,
    width_ref,
    fwd_hbm,
    inv_hbm,
    taps_hbm,
    out_ref,
    rows_send,
    rows_recv,
    grid_ref,
    sum_ref,
    weight_ref,
    proj_ref,
    cent_send,
    cent_recv,
    spec_ref,
    level_send,
    level_recv,
    stripe_send,
    stripe_recv,
    ids_send,
    ids_recv,
    fwd_ref,
    inv_ref,
    taps_ref,
    table_sem,
    send_sem,
    recv_sem,
):
    devices, angles_here, tiles, tile_width, mods, fold = cfg
    angles = devices * angles_here
    cols = W // devices
    half = cols // fold
    rows = freq_rows(angles)
    step_cols = (W - tile_width) // (tiles - 1)
    window = tile_width + 2 * LANES
    blocks = angles_here * tiles
    me = lax.axis_index("ang")

    def ring_at(hop):
        return lax.rem(me + hop, devices)

    def peer_at(hop):
        if devices & (devices - 1):
            return ring_at(hop)
        mask = devices - hop
        peer = 0
        bit = 1
        while bit < devices:
            peer = peer + bit * lax.rem(lax.div(me, bit) + mask // bit, 2)
            bit *= 2
        return peer

    barrier = pltpu.get_barrier_semaphore()

    def greet(step):
        pl.semaphore_signal(
            barrier,
            inc=1,
            device_id={"ang": peer_at(step + 1)},
            device_id_type=pl.DeviceIdType.MESH,
        )

    loop(devices - 1, greet)
    fetch_fwd = pltpu.make_async_copy(fwd_hbm, fwd_ref, table_sem.at[0])
    fetch_inv = pltpu.make_async_copy(inv_hbm, inv_ref, table_sem.at[1])
    fetch_taps = pltpu.make_async_copy(taps_hbm, taps_ref, table_sem.at[2])
    fetch_fwd.start()
    fetch_inv.start()
    fetch_taps.start()

    def remote(phase, src, dst, slot, peer):
        return pltpu.make_async_remote_copy(
            src_ref=src,
            dst_ref=dst,
            send_sem=send_sem.at[phase, peer],
            recv_sem=recv_sem.at[phase, slot],
            device_id={"ang": peer},
            device_id_type=pl.DeviceIdType.MESH,
        )

    def finish(phase, send_of, recv_of):
        def body(step):
            peer = peer_at(step + 1)
            copy = remote(phase, send_of(peer), recv_of(peer), peer, peer)
            copy.wait_recv()
            copy.wait_send()

        loop(devices - 1, body)

    cap = -(-blocks // devices)
    slab = 16
    chunks = tile_width // LANES
    extra = chunks - cap
    slots = devices * slab
    dest_row = dest_ref[...].astype(F32)
    source_row = iota((blocks, blocks), 1)
    source_col = iota((blocks, blocks), 0)

    def turned(values):
        return jnp.sum(jnp.where(source_row == source_col, values, 0.0), axis=1, keepdims=True)

    owner_row = jnp.floor((dest_row + 0.5) * (1.0 / blocks))
    owner_col = turned(owner_row)
    earlier = (owner_col == owner_row) & (source_col < source_row)
    rank_row = jnp.sum(jnp.where(earlier, 1.0, 0.0), axis=0, keepdims=True)
    rank_col = turned(rank_row)
    place_row = dest_row - owner_row * blocks + 1.0
    slot = iota((slots, 1), 0).astype(F32)

    def one_hot(left, right):
        return jnp.where(left == right, 1.0, 0.0).astype(BF16)

    direct = one_hot(slot, owner_row * slab + rank_row)
    packed = dot(direct, raw_ref[:, : cap * LANES])
    keeps = [
        jnp.where(jnp.broadcast_to(rank_col, (blocks, LANES)) == j, 1.0, 0.0).astype(BF16)
        for j in range(cap)
    ]
    for e in range(extra):
        chunk = raw_ref[:, (cap + e) * LANES : (cap + e + 1) * LANES]
        masked = jnp.concatenate([chunk * keep for keep in keeps], axis=1)
        packed = packed + dot(one_hot(slot, owner_row * slab + (cap + e)), masked)
    rows_send[...] = packed.astype(BF16).reshape(devices, slab, cap * LANES)
    group = LANES // slab
    groups = -(-devices // group)
    lane_at = iota((blocks, LANES), 1).astype(F32)
    first_lane = (lax.rem(me, group) * slab).astype(F32)
    at_rank = one_hot(lane_at, rank_col + first_lane)
    to_owner = jnp.where(iota((devices, blocks), 0).astype(F32) == owner_row, place_row, 0.0)
    ids_send[...] = dot(to_owner.astype(BF16), at_rank).reshape(devices, 1, LANES)

    pl.semaphore_wait(barrier, devices - 1)

    def send_rows(step):
        peer = peer_at(step + 1)
        remote(4, ids_send.at[peer], ids_recv.at[me], me, peer).start()
        remote(0, rows_send.at[peer], rows_recv.at[me], me, peer).start()

    loop(devices - 1, send_rows)
    rows_recv[me] = rows_send[me]
    ids_recv[me] = ids_send[me]
    finish(4, lambda p: ids_send.at[p], lambda p: ids_recv.at[p])
    finish(0, lambda p: rows_send.at[p], lambda p: rows_recv.at[p])

    ids = [
        jnp.sum(ids_recv[g * group : min((g + 1) * group, devices)], axis=0) for g in range(groups)
    ]
    ids = ids[0] if groups == 1 else jnp.concatenate(ids, axis=1)
    ids = jnp.broadcast_to(ids[:, :slots], (8, slots))
    row = iota((blocks, 1), 0).astype(F32)
    tile_of = jnp.floor((row + 0.5) * (1.0 / angles_here))
    wanted = (row - tile_of * angles_here) * tiles + tile_of + 1.0
    lead = rows_recv[...].reshape(slots, cap * LANES)
    grid_ref[:, : cap * LANES] = dot(one_hot(wanted, ids[0:1]), lead)
    if extra:
        within = iota((8, slots), 1) & (slab - 1)
        turns = [pltpu.roll(ids, n, 1) if n else ids for n in range(slab)]
        wanted_at = jnp.concatenate(
            [jnp.where(within[0:1] == cap + e, wanted, -1.0) for e in range(extra)], axis=0
        )
        rest = jnp.zeros((extra * blocks, LANES), F32)
        for j in range(cap):
            ids_j = jnp.zeros((8, slots), F32)
            for e in range(extra):
                ids_j = jnp.where(within == cap + e, turns[cap + e - j], ids_j)
            part = rows_recv[:, :, j * LANES : (j + 1) * LANES].reshape(slots, LANES)
            rest = rest + dot(one_hot(wanted_at, ids_j[0:1]), part)
        for e in range(extra):
            at = (cap + e) * LANES
            grid_ref[:, at : at + LANES] = rest[e * blocks : (e + 1) * blocks]

    fetch_fwd.wait()
    fetch_inv.wait()
    fetch_taps.wait()

    sum_ref[...] = jnp.zeros_like(sum_ref)
    weight_ref[...] = jnp.zeros_like(weight_ref)
    inverse_ramp = 1.0 / ramp_ref[...].astype(F32)
    lane = iota((angles_here, window), 1)
    for tile in range(tiles):
        base = tile * step_cols
        shift = jnp.broadcast_to(
            offset_ref[:, tile : tile + 1] - (base - LANES), (angles_here, window)
        )
        piece = jnp.concatenate(
            [
                grid_ref[tile * angles_here : (tile + 1) * angles_here, :],
                jnp.zeros((angles_here, 2 * LANES), F32),
            ],
            axis=1,
        )
        for bit in range(8):
            moved = pltpu.roll(piece, 1 << bit, 1)
            piece = jnp.where((shift & (1 << bit)) != 0, moved, piece)
        x = lane - shift
        edge = (jnp.minimum(x, tile_width - 1 - x) + 1).astype(F32)
        feather = jnp.minimum(1.0, edge * inverse_ramp[:, tile : tile + 1])
        feather = jnp.maximum(feather, 0.0)
        sum_ref[:, base : base + window] += feather * piece
        weight_ref[:, base : base + window] += feather

    wide = width_ref[...].astype(F32)
    upper = iota((mods, wide.shape[1]), 1)
    lower = iota((mods, wide.shape[1]), 0)
    bounds = jnp.sum(jnp.where(upper <= lower, wide, 0.0), axis=1, keepdims=True)
    starts = jnp.sum(jnp.where(upper < lower, wide, 0.0), axis=1, keepdims=True)
    on_diagonal = iota((mods, mods), 0) == iota((mods, mods), 1)
    safe_wide = jnp.sum(jnp.where(on_diagonal, bounds - starts, 0.0), axis=0, keepdims=True)
    safe_wide = jnp.maximum(safe_wide, 1.0)

    def member(first, count):
        c = (iota((mods, count), 1) + first).astype(F32)
        inside = (c >= starts) & (c < bounds)
        return jnp.where(inside, 1.0, 0.0).astype(BF16)

    def project(step, total):
        at = step * SPAN
        behind = at + LANES
        blended = sum_ref[:, pl.ds(behind, SPAN)] / weight_ref[:, pl.ds(behind, SPAN)]
        projection = -jnp.log(blended)
        proj_ref[:, pl.ds(at, SPAN)] = projection
        return total + dot_nt(thirds(projection), member(at, SPAN))

    total = jnp.zeros((4 * angles_here, mods), F32)
    for step in range(W // SPAN):
        total = project(step, total)

    def gather_thirds(stack):
        a = angles_here
        return stack[0:a] + stack[a : 2 * a] + stack[2 * a : 3 * a]

    mean = thirds(gather_thirds(total) / safe_wide)

    def centered_slab(owner):
        at = pl.multiple_of(owner * cols, LANES)
        flat = proj_ref[:, pl.ds(at, cols)] - gather_thirds(dot(mean, member(at, cols)))
        if fold > 1:
            flat = jnp.concatenate([flat[:, i * half : (i + 1) * half] for i in range(fold)], axis=0)
        return flat.astype(cent_send.dtype)

    def send_centered(step):
        peer = peer_at(step + 1)
        cent_send[peer] = centered_slab(peer)
        remote(1, cent_send.at[peer], cent_recv.at[me], me, peer).start()

    loop(devices - 1, send_centered)
    cent_send[me] = centered_slab(me)
    cent_recv[me] = cent_send[me]

    if fold > 1:
        shared_row = iota((fold * angles_here, fold * angles_here), 0)
        shared_col = iota((fold * angles_here, fold * angles_here), 1)
        same = (shared_row // angles_here) == (shared_col // angles_here)
        shared_table = jnp.where(same, SHARED / angles_here, 0.0).astype(BF16)

        def take_shared(owner):
            at = pl.multiple_of(owner * cols, LANES)
            shared = dot(shared_table, cent_send[owner])
            shared = jnp.concatenate(
                [shared[i * angles_here : (i + 1) * angles_here] for i in range(fold)], axis=1
            )
            proj_ref[:, pl.ds(at, cols)] = proj_ref[:, pl.ds(at, cols)] - shared

        loop(devices, take_shared)

    finish(1, lambda p: cent_send.at[p], lambda p: cent_recv.at[p])

    signal = cent_recv[...].reshape(devices * fold * angles_here, half).astype(BF16)
    k = iota((rows, 1), 0)
    count_of = jnp.where((k == 0) | (2 * k == angles), 1.0, 2.0)
    count_of = jnp.where(2 * k <= angles, count_of, 0.0)
    mine = pl.multiple_of(me * cols, LANES)
    sums = jnp.zeros((4 * 8, mods), F32)
    for part in range(fold):
        wide_spec = dot(fwd_ref[part], signal)
        spectrum = wide_spec[: 2 * rows] + wide_spec[2 * rows :]
        spec_ref[part] = spectrum
        magnitude = jnp.sqrt(
            spectrum[:rows] * spectrum[:rows] + spectrum[rows:] * spectrum[rows:]
        )
        over_k = jnp.sum(magnitude * count_of, axis=0, keepdims=True)
        first_row = jnp.where(iota((8, half), 0) == 0, over_k, 0.0)
        sums = sums + dot_nt(thirds(first_row), member(mine + part * half, half))
    level_send[...] = jnp.zeros_like(level_send)
    level_send[:, 0:mods] = sums[0:8] + sums[8:16] + sums[16:24]

    def send_level(step):
        peer = peer_at(step + 1)
        remote(2, level_send, level_recv.at[me], me, peer).start()

    loop(devices - 1, send_level)
    level_recv[me] = level_send[...]
    finish(2, lambda p: level_send, lambda p: level_recv.at[p])
    everything = jnp.sum(level_recv[...], axis=0)[:, 0:mods]
    level = SHRINK_SCALE * (everything / (angles * safe_wide) + EPSILON)
    level_parts = thirds(jnp.where(iota((8, mods), 0) == 0, level, 0.0))

    residual = []
    for part in range(fold):
        spread = dot(level_parts, member(mine + part * half, half))
        level_col = spread[0:1] + spread[8:9] + spread[16:17]
        spectrum = spec_ref[part]
        magnitude = jnp.sqrt(
            spectrum[:rows] * spectrum[:rows] + spectrum[rows:] * spectrum[rows:]
        )
        factor = jnp.maximum(magnitude - level_col, 0.0) / jnp.maximum(magnitude, level_col)
        shrunk = jnp.concatenate([spectrum[:rows] * factor, spectrum[rows:] * factor], axis=0)
        high, low = halves(shrunk)
        parts = [high, low, high] + ([signal] if fold > 1 else [])
        stripe = dot(inv_ref[part], jnp.concatenate(parts, axis=0))
        residual.append(stripe.reshape(devices, angles_here, half))
    stripe_send[...] = jnp.concatenate(residual, axis=1).astype(stripe_send.dtype)

    def send_stripe(step):
        peer = ring_at(step + 1)
        remote(3, stripe_send.at[peer], stripe_recv.at[me], me, peer).start()

    loop(devices - 1, send_stripe)
    stripe_recv[me] = stripe_send[me]

    sum_ref[:, 0:LANES] = jnp.zeros((angles_here, LANES), F32)
    sum_ref[:, W + LANES :] = jnp.zeros((angles_here, LANES), F32)
    lane_blocks = cols // LANES

    def clean(owner):
        at = pl.multiple_of(owner * cols, LANES)
        behind = pl.multiple_of(owner * cols + LANES, LANES)
        rest = stripe_recv[owner].astype(F32)
        rest = jnp.concatenate(
            [rest[i * angles_here : (i + 1) * angles_here] for i in range(fold)], axis=1
        )
        sum_ref[:, pl.ds(behind, cols)] = proj_ref[:, pl.ds(at, cols)] - rest

    def ramp(group):
        at = pl.multiple_of(group * cols, LANES)
        flat = sum_ref[:, pl.ds(at, cols + 2 * LANES)]
        stack = jnp.concatenate(
            [flat[:, b * LANES : (b + 1) * LANES] for b in range(lane_blocks + 2)], axis=0
        )
        n = lane_blocks * angles_here
        near = jnp.concatenate(
            [stack[s * angles_here : s * angles_here + n] for s in range(3)], axis=1
        )
        high, low = halves(near)
        done = dot(high, taps_ref[0]) + dot(low, taps_ref[0]) + dot(high, taps_ref[1])
        out_ref[:, pl.ds(at, cols)] = jnp.concatenate(
            [done[b * angles_here : (b + 1) * angles_here] for b in range(lane_blocks)], axis=1
        )

    clean(me)

    def below(hop):
        return lax.rem(me + devices - hop, devices)

    def take(hop):
        owner = below(hop)
        remote(3, stripe_send.at[owner], stripe_recv.at[owner], owner, owner).wait_recv()
        clean(owner)

    take(1)

    def advance(step):
        take(step + 2)
        ramp(below(step + 1))

    loop(devices - 2, advance)
    ramp(below(devices - 1))
    ramp(me)

    def sent(step):
        peer = ring_at(step + 1)
        remote(3, stripe_send.at[peer], stripe_recv.at[peer], peer, peer).wait_send()

    loop(devices - 1, sent)


def per_device(raw, block_dest, section_offset, ramp_length, module_width):
    devices = lax.axis_size("ang")
    blocks_here = raw.shape[0]
    tile_width = raw.shape[1]
    angles_here, tiles = section_offset.shape
    angles = angles_here * devices
    capacity = (blocks_here + devices - 1) // devices
    cols = W // devices
    fold = 2 if cols % (2 * LANES) == 0 else 1
    wire = BF16 if fold == 2 else F32
    mods = -(-module_width.shape[0] // 16) * 16
    half = cols // fold
    rows = freq_rows(angles)
    cfg = (devices, angles_here, tiles, tile_width, mods, fold)
    forward = forward_table(angles, devices, fold)
    inverse = inverse_table(angles, devices, fold)
    taps = ramp_table()
    vmem = pl.BlockSpec(memory_space=pltpu.VMEM)
    return pl.pallas_call(
        functools.partial(kernel, cfg),
        out_shape=pltpu.VMEM((angles_here, W), F32),
        in_specs=[vmem] * 5 + [pl.BlockSpec(memory_space=pl.ANY)] * 3,
        out_specs=vmem,
        scratch_shapes=[
            pltpu.VMEM((devices, 16, capacity * LANES), BF16),
            pltpu.VMEM((devices, 16, capacity * LANES), BF16),
            pltpu.VMEM((angles_here * tiles, tile_width), F32),
            pltpu.VMEM((angles_here, W + 2 * LANES), F32),
            pltpu.VMEM((angles_here, W + 2 * LANES), F32),
            pltpu.VMEM((angles_here, W), F32),
            pltpu.VMEM((devices, angles_here * fold, half), wire),
            pltpu.VMEM((devices, angles_here * fold, half), wire),
            pltpu.VMEM((fold, 2 * rows, half), F32),
            pltpu.VMEM((8, max(mods, LANES)), F32),
            pltpu.VMEM((devices, 8, max(mods, LANES)), F32),
            pltpu.VMEM((devices, angles_here * fold, half), wire),
            pltpu.VMEM((devices, angles_here * fold, half), wire),
            pltpu.VMEM((devices, 1, LANES), F32),
            pltpu.VMEM((devices, 1, LANES), F32),
            pltpu.VMEM(forward.shape, BF16),
            pltpu.VMEM(inverse.shape, BF16),
            pltpu.VMEM(taps.shape, BF16),
            pltpu.SemaphoreType.DMA((3,)),
            pltpu.SemaphoreType.DMA((5, devices)),
            pltpu.SemaphoreType.DMA((5, devices)),
        ],
        compiler_params=pltpu.CompilerParams(
            collective_id=0, has_side_effects=True, vmem_limit_bytes=60 << 20
        ),
    )(
        raw,
        block_dest[None, :],
        section_offset,
        ramp_length[None, :],
        module_width[None, :],
        jnp.asarray(forward),
        jnp.asarray(inverse),
        jnp.asarray(taps),
    )


def solution(mesh):
    in_specs = (P(("row", "ang"), None), P("ang"), P("ang", None), P(), P())
    out_specs = P(("row", "ang"), None)
    return jax.shard_map(
        per_device, mesh=mesh, in_specs=in_specs, out_specs=out_specs, check_vma=False
    )
```

```python
import functools
import math

import jax
import jax.numpy as jnp
import ml_dtypes
import numpy as np
from jax import lax
from jax.experimental import pallas as pl
from jax.experimental.pallas import tpu as pltpu
from jax.sharding import PartitionSpec as P

W = 16384
RAMP_HALF = 128
JITTER = 64
SHRINK_SCALE = 1.0
EPSILON = 1e-06
LANES = 128
SPAN = 2048
SHARED = 0.625

F32 = jnp.float32
BF16 = jnp.bfloat16


def split_np(table):
    high = table.astype(ml_dtypes.bfloat16)
    low = (table - high.astype(np.float64)).astype(ml_dtypes.bfloat16)
    return high, low


def freq_rows(angles):
    return -(-(angles // 2 + 1) // 8) * 8


def forward_table(angles, devices, fold):
    rows = freq_rows(angles)
    here = angles // devices
    k = np.arange(rows)[:, None]
    a = np.arange(angles)[None, :]
    phase = 2.0 * np.pi * ((k * a) % angles) / angles
    keep = (k <= angles // 2).astype(np.float64)
    table = np.concatenate([np.cos(phase) * keep, -np.sin(phase) * keep], axis=0)
    placed = np.zeros((fold, 2 * rows, devices, fold, here))
    for part in range(fold):
        placed[part, :, :, part, :] = table.reshape(2 * rows, devices, here)
    high, low = split_np(placed.reshape(fold, 2 * rows, devices * fold * here))
    return np.concatenate([high, low], axis=1)


def inverse_table(angles, devices, fold):
    rows = freq_rows(angles)
    k = np.arange(rows)[None, :]
    a = np.arange(angles)[:, None]
    phase = 2.0 * np.pi * ((k * a) % angles) / angles
    twice = np.where((k == 0) | (2 * k == angles), 1.0, 2.0) * (k <= angles // 2)
    weight = twice * np.exp(-np.minimum(k, angles - k) / (angles // 8)) / angles
    table = np.concatenate([np.cos(phase) * weight, -np.sin(phase) * weight], axis=1)
    high, low = split_np(table)
    table = np.concatenate([high, high, low], axis=1)
    if fold == 1:
        return table[None]
    here = angles // devices
    shared = np.kron(np.eye(devices), np.ones((here, here))) * (SHARED / here)
    placed = np.zeros((fold, angles, devices, fold, here))
    for part in range(fold):
        placed[part, :, :, part, :] = -shared.reshape(angles, devices, here)
    placed = placed.reshape(fold, angles, devices * fold * here).astype(ml_dtypes.bfloat16)
    return np.concatenate([np.broadcast_to(table, (fold,) + table.shape), placed], axis=2)


def ramp_table():
    i = np.arange(3 * LANES)[:, None] - LANES
    n = np.arange(LANES)[None, :] - i
    safe = np.where(n == 0, 1, n).astype(np.float64)
    taps = np.where(n % 2 != 0, -1.0 / (np.pi * np.pi * safe * safe), 0.0)
    taps = np.where(n == 0, 0.25, taps)
    taps = np.where(np.abs(n) <= RAMP_HALF, taps, 0.0)
    high, low = split_np(taps)
    return np.stack([high, low])


def dot(left, right):
    return jnp.dot(left, right, preferred_element_type=F32)


def dot_nt(left, right):
    return lax.dot_general(left, right, (((1,), (1,)), ((), ())), preferred_element_type=F32)


def halves(x):
    high = x.astype(BF16)
    return high, (x - high.astype(F32)).astype(BF16)


def thirds(x):
    high = x.astype(BF16).astype(F32)
    rest = x - high
    mid = rest.astype(BF16).astype(F32)
    low = rest - mid
    return jnp.concatenate([high, mid, low, jnp.zeros_like(x)], axis=0).astype(BF16)


def iota(shape, axis):
    return lax.broadcasted_iota(jnp.int32, shape, axis)


def loop(count, body):
    if count <= 8:
        for step in range(count):
            body(step)
    else:

        def run(step, carry):
            body(step)
            return carry

        lax.fori_loop(0, count, run, 0)


def kernel(
    cfg,
    raw_ref,
    dest_ref,
    offset_ref,
    ramp_ref,
    width_ref,
    fwd_hbm,
    inv_hbm,
    taps_hbm,
    out_ref,
    rows_send,
    rows_recv,
    grid_ref,
    sum_ref,
    weight_ref,
    proj_ref,
    cent_send,
    cent_recv,
    spec_ref,
    level_send,
    level_recv,
    stripe_send,
    stripe_recv,
    ids_send,
    ids_recv,
    fwd_ref,
    inv_ref,
    taps_ref,
    table_sem,
    send_sem,
    recv_sem,
):
    devices, angles_here, tiles, tile_width, mods, fold = cfg
    angles = devices * angles_here
    cols = W // devices
    half = cols // fold
    rows = freq_rows(angles)
    step_cols = (W - tile_width) // (tiles - 1)
    window = tile_width + 2 * LANES
    blocks = angles_here * tiles
    me = lax.axis_index("ang")

    def ring_at(hop):
        return lax.rem(me + hop, devices)

    def peer_at(hop):
        if devices & (devices - 1):
            return ring_at(hop)
        mask = devices - hop
        peer = 0
        bit = 1
        while bit < devices:
            peer = peer + bit * lax.rem(lax.div(me, bit) + mask // bit, 2)
            bit *= 2
        return peer

    barrier = pltpu.get_barrier_semaphore()

    def greet(step):
        pl.semaphore_signal(
            barrier,
            inc=1,
            device_id={"ang": peer_at(step + 1)},
            device_id_type=pl.DeviceIdType.MESH,
        )

    loop(devices - 1, greet)
    fetch_fwd = pltpu.make_async_copy(fwd_hbm, fwd_ref, table_sem.at[0])
    fetch_inv = pltpu.make_async_copy(inv_hbm, inv_ref, table_sem.at[1])
    fetch_taps = pltpu.make_async_copy(taps_hbm, taps_ref, table_sem.at[2])
    fetch_fwd.start()
    fetch_inv.start()
    fetch_taps.start()

    def remote(phase, src, dst, slot, peer):
        return pltpu.make_async_remote_copy(
            src_ref=src,
            dst_ref=dst,
            send_sem=send_sem.at[phase, peer],
            recv_sem=recv_sem.at[phase, slot],
            device_id={"ang": peer},
            device_id_type=pl.DeviceIdType.MESH,
        )

    def finish(phase, send_of, recv_of):
        def body(step):
            peer = peer_at(step + 1)
            copy = remote(phase, send_of(peer), recv_of(peer), peer, peer)
            copy.wait_recv()
            copy.wait_send()

        loop(devices - 1, body)

    cap = -(-blocks // devices)
    slab = 16
    chunks = tile_width // LANES
    extra = chunks - cap
    slots = devices * slab
    dest_row = dest_ref[...].astype(F32)
    source_row = iota((blocks, blocks), 1)
    source_col = iota((blocks, blocks), 0)

    def turned(values):
        return jnp.sum(jnp.where(source_row == source_col, values, 0.0), axis=1, keepdims=True)

    owner_row = jnp.floor((dest_row + 0.5) * (1.0 / blocks))
    owner_col = turned(owner_row)
    earlier = (owner_col == owner_row) & (source_col < source_row)
    rank_row = jnp.sum(jnp.where(earlier, 1.0, 0.0), axis=0, keepdims=True)
    rank_col = turned(rank_row)
    place_row = dest_row - owner_row * blocks + 1.0
    slot = iota((slots, 1), 0).astype(F32)

    def one_hot(left, right):
        return jnp.where(left == right, 1.0, 0.0).astype(BF16)

    direct = one_hot(slot, owner_row * slab + rank_row)
    packed = dot(direct, raw_ref[:, : cap * LANES])
    keeps = [
        jnp.where(jnp.broadcast_to(rank_col, (blocks, LANES)) == j, 1.0, 0.0).astype(BF16)
        for j in range(cap)
    ]
    for e in range(extra):
        chunk = raw_ref[:, (cap + e) * LANES : (cap + e + 1) * LANES]
        masked = jnp.concatenate([chunk * keep for keep in keeps], axis=1)
        packed = packed + dot(one_hot(slot, owner_row * slab + (cap + e)), masked)
    rows_send[...] = packed.astype(BF16).reshape(devices, slab, cap * LANES)
    group = LANES // slab
    groups = -(-devices // group)
    lane_at = iota((blocks, LANES), 1).astype(F32)
    first_lane = (lax.rem(me, group) * slab).astype(F32)
    at_rank = one_hot(lane_at, rank_col + first_lane)
    to_owner = jnp.where(iota((devices, blocks), 0).astype(F32) == owner_row, place_row, 0.0)
    ids_send[...] = dot(to_owner.astype(BF16), at_rank).reshape(devices, 1, LANES)

    pl.semaphore_wait(barrier, devices - 1)

    def send_rows(step):
        peer = peer_at(step + 1)
        remote(4, ids_send.at[peer], ids_recv.at[me], me, peer).start()
        remote(0, rows_send.at[peer], rows_recv.at[me], me, peer).start()

    loop(devices - 1, send_rows)
    rows_recv[me] = rows_send[me]
    ids_recv[me] = ids_send[me]
    finish(4, lambda p: ids_send.at[p], lambda p: ids_recv.at[p])
    finish(0, lambda p: rows_send.at[p], lambda p: rows_recv.at[p])

    ids = [
        jnp.sum(ids_recv[g * group : min((g + 1) * group, devices)], axis=0) for g in range(groups)
    ]
    ids = ids[0] if groups == 1 else jnp.concatenate(ids, axis=1)
    ids = jnp.broadcast_to(ids[:, :slots], (8, slots))
    row = iota((blocks, 1), 0).astype(F32)
    tile_of = jnp.floor((row + 0.5) * (1.0 / angles_here))
    wanted = (row - tile_of * angles_here) * tiles + tile_of + 1.0
    lead = rows_recv[...].reshape(slots, cap * LANES)
    grid_ref[:, : cap * LANES] = dot(one_hot(wanted, ids[0:1]), lead)
    if extra:
        within = iota((8, slots), 1) & (slab - 1)
        turns = [pltpu.roll(ids, n, 1) if n else ids for n in range(slab)]
        wanted_at = jnp.concatenate(
            [jnp.where(within[0:1] == cap + e, wanted, -1.0) for e in range(extra)], axis=0
        )
        rest = jnp.zeros((extra * blocks, LANES), F32)
        for j in range(cap):
            ids_j = jnp.zeros((8, slots), F32)
            for e in range(extra):
                ids_j = jnp.where(within == cap + e, turns[cap + e - j], ids_j)
            part = rows_recv[:, :, j * LANES : (j + 1) * LANES].reshape(slots, LANES)
            rest = rest + dot(one_hot(wanted_at, ids_j[0:1]), part)
        for e in range(extra):
            at = (cap + e) * LANES
            grid_ref[:, at : at + LANES] = rest[e * blocks : (e + 1) * blocks]

    fetch_fwd.wait()
    fetch_inv.wait()
    fetch_taps.wait()

    sum_ref[...] = jnp.zeros_like(sum_ref)
    weight_ref[...] = jnp.zeros_like(weight_ref)
    inverse_ramp = 1.0 / ramp_ref[...].astype(F32)
    lane = iota((angles_here, window), 1)
    for tile in range(tiles):
        base = tile * step_cols
        shift = jnp.broadcast_to(
            offset_ref[:, tile : tile + 1] - (base - LANES), (angles_here, window)
        )
        piece = jnp.concatenate(
            [
                grid_ref[tile * angles_here : (tile + 1) * angles_here, :],
                jnp.zeros((angles_here, 2 * LANES), F32),
            ],
            axis=1,
        )
        for bit in range(8):
            moved = pltpu.roll(piece, 1 << bit, 1)
            piece = jnp.where((shift & (1 << bit)) != 0, moved, piece)
        x = lane - shift
        edge = (jnp.minimum(x, tile_width - 1 - x) + 1).astype(F32)
        feather = jnp.minimum(1.0, edge * inverse_ramp[:, tile : tile + 1])
        feather = jnp.maximum(feather, 0.0)
        sum_ref[:, base : base + window] += feather * piece
        weight_ref[:, base : base + window] += feather

    wide = width_ref[...].astype(F32)
    upper = iota((mods, wide.shape[1]), 1)
    lower = iota((mods, wide.shape[1]), 0)
    bounds = jnp.sum(jnp.where(upper <= lower, wide, 0.0), axis=1, keepdims=True)
    starts = jnp.sum(jnp.where(upper < lower, wide, 0.0), axis=1, keepdims=True)
    on_diagonal = iota((mods, mods), 0) == iota((mods, mods), 1)
    safe_wide = jnp.sum(jnp.where(on_diagonal, bounds - starts, 0.0), axis=0, keepdims=True)
    safe_wide = jnp.maximum(safe_wide, 1.0)

    def member(first, count):
        c = (iota((mods, count), 1) + first).astype(F32)
        inside = (c >= starts) & (c < bounds)
        return jnp.where(inside, 1.0, 0.0).astype(BF16)

    def project(step, total):
        at = step * SPAN
        behind = at + LANES
        blended = sum_ref[:, pl.ds(behind, SPAN)] / weight_ref[:, pl.ds(behind, SPAN)]
        projection = -jnp.log(blended)
        proj_ref[:, pl.ds(at, SPAN)] = projection
        return total + dot_nt(thirds(projection), member(at, SPAN))

    total = jnp.zeros((4 * angles_here, mods), F32)
    for step in range(W // SPAN):
        total = project(step, total)

    def gather_thirds(stack):
        a = angles_here
        return stack[0:a] + stack[a : 2 * a] + stack[2 * a : 3 * a]

    mean = thirds(gather_thirds(total) / safe_wide)

    def centered_slab(owner):
        at = pl.multiple_of(owner * cols, LANES)
        flat = proj_ref[:, pl.ds(at, cols)] - gather_thirds(dot(mean, member(at, cols)))
        if fold > 1:
            flat = jnp.concatenate([flat[:, i * half : (i + 1) * half] for i in range(fold)], axis=0)
        return flat.astype(cent_send.dtype)

    def send_centered(step):
        peer = peer_at(step + 1)
        cent_send[peer] = centered_slab(peer)
        remote(1, cent_send.at[peer], cent_recv.at[me], me, peer).start()

    loop(devices - 1, send_centered)
    cent_send[me] = centered_slab(me)
    cent_recv[me] = cent_send[me]

    if fold > 1:
        shared_row = iota((fold * angles_here, fold * angles_here), 0)
        shared_col = iota((fold * angles_here, fold * angles_here), 1)
        same = (shared_row // angles_here) == (shared_col // angles_here)
        shared_table = jnp.where(same, SHARED / angles_here, 0.0).astype(BF16)

        def take_shared(owner):
            at = pl.multiple_of(owner * cols, LANES)
            shared = dot(shared_table, cent_send[owner])
            shared = jnp.concatenate(
                [shared[i * angles_here : (i + 1) * angles_here] for i in range(fold)], axis=1
            )
            proj_ref[:, pl.ds(at, cols)] = proj_ref[:, pl.ds(at, cols)] - shared

        loop(devices, take_shared)

    finish(1, lambda p: cent_send.at[p], lambda p: cent_recv.at[p])

    signal = cent_recv[...].reshape(devices * fold * angles_here, half).astype(BF16)
    k = iota((rows, 1), 0)
    count_of = jnp.where((k == 0) | (2 * k == angles), 1.0, 2.0)
    count_of = jnp.where(2 * k <= angles, count_of, 0.0)
    mine = pl.multiple_of(me * cols, LANES)
    sums = jnp.zeros((4 * 8, mods), F32)
    for part in range(fold):
        wide_spec = dot(fwd_ref[part], signal)
        spectrum = wide_spec[: 2 * rows] + wide_spec[2 * rows :]
        spec_ref[part] = spectrum
        magnitude = jnp.sqrt(
            spectrum[:rows] * spectrum[:rows] + spectrum[rows:] * spectrum[rows:]
        )
        over_k = jnp.sum(magnitude * count_of, axis=0, keepdims=True)
        first_row = jnp.where(iota((8, half), 0) == 0, over_k, 0.0)
        sums = sums + dot_nt(thirds(first_row), member(mine + part * half, half))
    level_send[...] = jnp.zeros_like(level_send)
    level_send[:, 0:mods] = sums[0:8] + sums[8:16] + sums[16:24]

    def send_level(step):
        peer = peer_at(step + 1)
        remote(2, level_send, level_recv.at[me], me, peer).start()

    loop(devices - 1, send_level)
    level_recv[me] = level_send[...]
    finish(2, lambda p: level_send, lambda p: level_recv.at[p])
    everything = jnp.sum(level_recv[...], axis=0)[:, 0:mods]
    level = SHRINK_SCALE * (everything / (angles * safe_wide) + EPSILON)
    level_parts = thirds(jnp.where(iota((8, mods), 0) == 0, level, 0.0))

    residual = []
    for part in range(fold):
        spread = dot(level_parts, member(mine + part * half, half))
        level_col = spread[0:1] + spread[8:9] + spread[16:17]
        spectrum = spec_ref[part]
        magnitude = jnp.sqrt(
            spectrum[:rows] * spectrum[:rows] + spectrum[rows:] * spectrum[rows:]
        )
        factor = jnp.maximum(magnitude - level_col, 0.0) / jnp.maximum(magnitude, level_col)
        shrunk = jnp.concatenate([spectrum[:rows] * factor, spectrum[rows:] * factor], axis=0)
        high, low = halves(shrunk)
        parts = [high, low, high] + ([signal] if fold > 1 else [])
        stripe = dot(inv_ref[part], jnp.concatenate(parts, axis=0))
        residual.append(stripe.reshape(devices, angles_here, half))
    stripe_send[...] = jnp.concatenate(residual, axis=1).astype(stripe_send.dtype)

    def send_stripe(step):
        peer = ring_at(step + 1)
        remote(3, stripe_send.at[peer], stripe_recv.at[me], me, peer).start()

    loop(devices - 1, send_stripe)
    stripe_recv[me] = stripe_send[me]

    sum_ref[:, 0:LANES] = jnp.zeros((angles_here, LANES), F32)
    sum_ref[:, W + LANES :] = jnp.zeros((angles_here, LANES), F32)
    lane_blocks = cols // LANES

    def clean(owner):
        at = pl.multiple_of(owner * cols, LANES)
        behind = pl.multiple_of(owner * cols + LANES, LANES)
        rest = stripe_recv[owner].astype(F32)
        rest = jnp.concatenate(
            [rest[i * angles_here : (i + 1) * angles_here] for i in range(fold)], axis=1
        )
        sum_ref[:, pl.ds(behind, cols)] = proj_ref[:, pl.ds(at, cols)] - rest

    def ramp(group):
        at = pl.multiple_of(group * cols, LANES)
        flat = sum_ref[:, pl.ds(at, cols + 2 * LANES)]
        stack = jnp.concatenate(
            [flat[:, b * LANES : (b + 1) * LANES] for b in range(lane_blocks + 2)], axis=0
        )
        n = lane_blocks * angles_here
        near = jnp.concatenate(
            [stack[s * angles_here : s * angles_here + n] for s in range(3)], axis=1
        )
        high, low = halves(near)
        done = dot(high, taps_ref[0]) + dot(low, taps_ref[0]) + dot(high, taps_ref[1])
        out_ref[:, pl.ds(at, cols)] = jnp.concatenate(
            [done[b * angles_here : (b + 1) * angles_here] for b in range(lane_blocks)], axis=1
        )

    clean(me)

    def below(hop):
        return lax.rem(me + devices - hop, devices)

    def take(hop):
        owner = below(hop)
        remote(3, stripe_send.at[owner], stripe_recv.at[owner], owner, owner).wait_recv()
        clean(owner)

    take(1)

    def advance(step):
        take(step + 2)
        ramp(below(step + 1))

    loop(devices - 2, advance)
    ramp(below(devices - 1))
    ramp(me)

    def sent(step):
        peer = ring_at(step + 1)
        remote(3, stripe_send.at[peer], stripe_recv.at[peer], peer, peer).wait_send()

    loop(devices - 1, sent)


def pack_plan(cap, chunks, first, need):
    split = next(
        (n for n in range(1, cap) if n + (chunks - cap) * n // cap >= need), 0
    )
    run = list(range(first, first + need))
    others = [b for b in range(chunks) if b not in run]
    direct = run[:split] + others[: cap - split]
    cells = {}
    n = 0
    early = (chunks - cap) * split
    for block in run[split:] + others[cap - split :]:
        for rank in range(cap):
            if n < early:
                cells[cap + n // split, n % split] = (rank, block)
            else:
                late = n - early
                cells[cap + late // (cap - split), split + late % (cap - split)] = (rank, block)
            n += 1
    return split, direct, cells


def fast_plan(devices, angles_here, tiles, tile_width, mods):
    cols = W // devices
    step_cols = (W - tile_width) // (tiles - 1)
    cap = -(-angles_here * tiles // devices)
    chunks = tile_width // LANES
    if cols % (4 * LANES) or step_cols % LANES or tile_width % LANES:
        return None
    mine = cols // (2 * LANES)
    per_step = step_cols // LANES
    first = -(-(tile_width - step_cols + JITTER) // LANES) + 1
    back = per_step - first - mine
    fits = (
        tiles == devices + 1
        and angles_here == 8
        and angles_here * mods == LANES
        and chunks == 16
        and devices * chunks == LANES
        and 1 < cap < chunks
        and back >= 1
        and tile_width < 2 * step_cols - 2 * JITTER
        and (first + mine) * LANES <= step_cols - JITTER
    )
    if not fits:
        return None
    split, direct, cells = pack_plan(cap, chunks, first - 1, mine + 2)
    if not split:
        return None
    early = [[t * per_step + first + i for i in range(mine)] for t in range(devices)]
    taken = {b for run in early for b in run}
    late = [b for b in range(W // LANES) if b not in taken]
    late = [late[p * mine : (p + 1) * mine] for p in range(devices)]
    return cap, split, direct, cells, first, back, mine, early, late


def fast_kernel(
    cfg,
    plan,
    raw_ref,
    dest_ref,
    offset_ref,
    ramp_ref,
    width_ref,
    fwd_hbm,
    inv_hbm,
    taps_hbm,
    out_ref,
    rows_send_a,
    rows_recv_a,
    rows_send_b,
    rows_recv_b,
    ids_send,
    ids_recv,
    grid_ref,
    clean_ref,
    proj_ref,
    member_ref,
    member_late_ref,
    cent_send_a,
    cent_recv_a,
    cent_send_b,
    cent_recv_b,
    diff_send,
    diff_recv,
    spec_ref,
    level_send,
    level_recv,
    stripe_send_a,
    stripe_recv_a,
    stripe_send_b,
    stripe_recv_b,
    fwd_ref,
    inv_ref,
    taps_ref,
    table_sem,
    send_sem,
    recv_sem,
):
    devices, angles_here, tiles, tile_width, mods, fold = cfg
    cap, split, direct_blocks, cells, first, back, mine, early, late = plan
    angles = devices * angles_here
    rows = freq_rows(angles)
    step_cols = (W - tile_width) // (tiles - 1)
    blocks = angles_here * tiles
    chunks = tile_width // LANES
    slab = chunks
    slots = devices * slab
    width = mine * LANES
    half = width // 2
    me = lax.axis_index("ang")
    ROWS_A, ROWS_B, IDS, CENT_A, CENT_B, DIFF, LEVEL, STRIPE_A, STRIPE_B = range(9)

    def peer_at(hop):
        mask = devices - hop
        peer = 0
        bit = 1
        while bit < devices:
            peer = peer + bit * lax.rem(lax.div(me, bit) + mask // bit, 2)
            bit *= 2
        return peer

    peers = [peer_at(hop) for hop in range(1, devices)]
    barrier = pltpu.get_barrier_semaphore()
    for peer in peers:
        pl.semaphore_signal(
            barrier, inc=1, device_id={"ang": peer}, device_id_type=pl.DeviceIdType.MESH
        )
    fetch_fwd = pltpu.make_async_copy(fwd_hbm, fwd_ref, table_sem.at[0])
    fetch_inv = pltpu.make_async_copy(inv_hbm, inv_ref, table_sem.at[1])
    fetch_taps = pltpu.make_async_copy(taps_hbm, taps_ref, table_sem.at[2])
    fetch_fwd.start()
    fetch_inv.start()
    fetch_taps.start()

    def remote(phase, src, dst, slot, peer):
        return pltpu.make_async_remote_copy(
            src_ref=src,
            dst_ref=dst,
            send_sem=send_sem.at[phase, peer],
            recv_sem=recv_sem.at[phase, slot],
            device_id={"ang": peer},
            device_id_type=pl.DeviceIdType.MESH,
        )

    def send_all(phase, send_ref, recv_ref):
        for peer in peers:
            remote(phase, send_ref.at[peer], recv_ref.at[me], me, peer).start()

    def wait_recv(phase, send_ref, recv_ref):
        for peer in peers:
            remote(phase, send_ref.at[peer], recv_ref.at[peer], peer, peer).wait_recv()

    def wait_send(phase, send_ref, recv_ref):
        for peer in peers:
            remote(phase, send_ref.at[peer], recv_ref.at[peer], peer, peer).wait_send()

    dest_row = dest_ref[...].astype(F32)
    source_row = iota((blocks, blocks), 1)
    source_col = iota((blocks, blocks), 0)

    def turned(values):
        return jnp.sum(jnp.where(source_row == source_col, values, 0.0), axis=1, keepdims=True)

    owner_row = jnp.floor((dest_row + 0.5) * (1.0 / blocks))
    owner_col = turned(owner_row)
    earlier = (owner_col == owner_row) & (source_col < source_row)
    rank_row = jnp.sum(jnp.where(earlier, 1.0, 0.0), axis=0, keepdims=True)
    rank_col = turned(rank_row)
    place_row = dest_row - owner_row * blocks + 1.0
    slot = iota((slots, 1), 0).astype(F32)

    def one_hot(left, right):
        return jnp.where(left == right, 1.0, 0.0).astype(BF16)

    direct = one_hot(slot, owner_row * slab + rank_row)
    keeps = [
        jnp.where(jnp.broadcast_to(rank_col, (blocks, LANES)) == j, 1.0, 0.0).astype(BF16)
        for j in range(cap)
    ]

    def lane_block(b):
        return raw_ref[:, b * LANES : (b + 1) * LANES]

    def pack(columns):
        packed = dot(direct, jnp.concatenate([lane_block(direct_blocks[k]) for k in columns], axis=1))
        for r in range(cap, slab):
            masked = jnp.concatenate(
                [lane_block(cells[r, k][1]) * keeps[cells[r, k][0]] for k in columns], axis=1
            )
            packed = packed + dot(one_hot(slot, owner_row * slab + r), masked)
        return packed.astype(BF16).reshape(devices, slab, len(columns) * LANES)

    columns_a = range(split)
    columns_b = range(split, cap)
    lane_at = iota((blocks, LANES), 1).astype(F32)
    first_lane = (me * slab).astype(F32)
    at_rank = one_hot(lane_at, rank_col + first_lane)
    to_owner = jnp.where(iota((devices, blocks), 0).astype(F32) == owner_row, place_row, 0.0)
    ids_send[...] = dot(to_owner.astype(BF16), at_rank).reshape(devices, 1, LANES)
    rows_send_a[...] = pack(columns_a)

    pl.semaphore_wait(barrier, devices - 1)

    send_all(IDS, ids_send, ids_recv)
    send_all(ROWS_A, rows_send_a, rows_recv_a)
    rows_send_b[...] = pack(columns_b)
    send_all(ROWS_B, rows_send_b, rows_recv_b)
    rows_recv_a[me] = rows_send_a[me]
    rows_recv_b[me] = rows_send_b[me]
    ids_recv[me] = ids_send[me]

    wide = width_ref[...].astype(F32)
    upper = iota((mods, wide.shape[1]), 1)
    lower = iota((mods, wide.shape[1]), 0)
    bounds = jnp.sum(jnp.where(upper <= lower, wide, 0.0), axis=1, keepdims=True)
    starts = jnp.sum(jnp.where(upper < lower, wide, 0.0), axis=1, keepdims=True)
    on_diagonal = iota((mods, mods), 0) == iota((mods, mods), 1)
    safe_wide = jnp.sum(jnp.where(on_diagonal, bounds - starts, 0.0), axis=0, keepdims=True)
    safe_wide = jnp.maximum(safe_wide, 1.0)
    bounds = jnp.broadcast_to(bounds, (mods, LANES))
    starts = jnp.broadcast_to(starts, (mods, LANES))
    lane = iota((mods, LANES), 1).astype(F32)
    for b in range(W // LANES):
        c = lane + float(b * LANES)
        inside = (c >= starts) & (c < bounds)
        member_ref[:, b * LANES : (b + 1) * LANES] = jnp.where(inside, 1.0, 0.0).astype(BF16)
    for p in range(devices):
        for i, b in enumerate(late[p]):
            member_late_ref[p, :, i * LANES : (i + 1) * LANES] = member_ref[
                :, b * LANES : (b + 1) * LANES
            ]

    row = iota((blocks, 1), 0).astype(F32)
    tile_of = jnp.floor((row + 0.5) * (1.0 / angles_here))
    wanted = (row - tile_of * angles_here) * tiles + tile_of + 1.0
    wanted = jnp.broadcast_to(wanted, (blocks, LANES))
    within = iota((8, slots), 1) & (slab - 1)

    wait_recv(IDS, ids_send, ids_recv)
    ids = jnp.broadcast_to(jnp.sum(ids_recv[...], axis=0), (8, slots))
    turns = [pltpu.roll(ids, n, 1) if n else ids for n in range(slab)]

    def match(ids_row):
        return jnp.where(wanted == jnp.broadcast_to(ids_row[0:1], (blocks, LANES)), 1.0, 0.0)

    begun = set()

    def unpack(columns, recv_ref):
        lead = recv_ref[...].reshape(slots, len(columns) * LANES)
        flat = dot(match(ids).astype(BF16), lead)
        for at, k in enumerate(columns):
            b = direct_blocks[k]
            grid_ref[:, b * LANES : (b + 1) * LANES] = flat[:, at * LANES : (at + 1) * LANES]
        sums = {}
        for at, k in enumerate(columns):
            held = sorted({cells[r, k][1] for r in range(cap, slab)})
            hot = []
            for b in held:
                ids_b = jnp.zeros((8, slots), F32)
                for r in range(cap, slab):
                    if cells[r, k][1] == b:
                        ids_b = jnp.where(within == r, turns[r - cells[r, k][0]], ids_b)
                hot.append(match(ids_b))
            part = dot(
                jnp.concatenate(hot, axis=0).astype(BF16), lead[:, at * LANES : (at + 1) * LANES]
            )
            for i, b in enumerate(held):
                piece = part[i * blocks : (i + 1) * blocks]
                sums[b] = sums[b] + piece if b in sums else piece
        for b, value in sums.items():
            at = b * LANES
            if b in begun:
                value = value + grid_ref[:, at : at + LANES]
            begun.add(b)
            grid_ref[:, at : at + LANES] = value

    def shift_of(tile):
        ahead = LANES - (offset_ref[:, tile : tile + 1] - tile * step_cols)
        return jnp.broadcast_to(ahead, (angles_here, LANES))

    def shifted(piece, ahead):
        count = piece.shape[1] // LANES - 1
        wide_ahead = jnp.concatenate([ahead] * count, axis=1)
        piece = jnp.where((wide_ahead & LANES) != 0, piece[:, LANES:], piece[:, :-LANES])
        bit = LANES // 2
        while bit:
            moved = pltpu.roll(piece, count * LANES - bit, 1)
            piece = jnp.where((wide_ahead & bit) != 0, moved, piece)
            bit //= 2
        return piece[:, :-LANES]

    def tile_rows(tile, start, stop):
        return grid_ref[
            tile * angles_here : (tile + 1) * angles_here, start * LANES : stop * LANES
        ]

    def member(blocks_at, count):
        return member_ref[:, blocks_at * LANES : (blocks_at + count) * LANES]

    def split_ones(x):
        high = x.astype(BF16).astype(F32)
        rest = x - high
        mid = rest.astype(BF16).astype(F32)
        return jnp.concatenate([high, mid, rest - mid, jnp.ones_like(x)], axis=0).astype(BF16)

    def gather_thirds(stack):
        a = angles_here
        return stack[0:a] + stack[a : 2 * a] + stack[2 * a : 3 * a]

    wait_recv(ROWS_A, rows_send_a, rows_recv_a)
    unpack(columns_a, rows_recv_a)
    shifts = [shift_of(t) for t in range(tiles)]
    total_a = jnp.zeros((4 * angles_here, mods), F32)
    bunch = 4
    for t0 in range(0, devices, bunch):
        group = range(t0, min(t0 + bunch, devices))
        value = shifted(
            jnp.concatenate([tile_rows(t, first - 1, first + mine + 1) for t in group], axis=0),
            jnp.concatenate([shifts[t] for t in group], axis=0),
        )
        value = -jnp.log(value)
        for i, t in enumerate(group):
            flat = value[i * angles_here : (i + 1) * angles_here]
            proj_ref[:, early[t][0] * LANES : (early[t][0] + mine) * LANES] = flat
            total_a = total_a + dot_nt(split_ones(flat), member(early[t][0], mine))
    mean_a = gather_thirds(total_a) / jnp.maximum(total_a[3 * angles_here :], 1.0)
    mean_a_parts = thirds(mean_a)
    for p in range(devices):
        at = early[p][0] * LANES
        flat = proj_ref[:, at : at + width] - gather_thirds(
            dot(mean_a_parts, member(early[p][0], mine))
        )
        flat = jnp.concatenate([flat[:, :half], flat[:, half:]], axis=0)
        cent_send_a[p] = flat.astype(BF16)
    send_all(CENT_A, cent_send_a, cent_recv_a)
    cent_recv_a[me] = cent_send_a[me]

    wait_recv(ROWS_B, rows_send_b, rows_recv_b)
    unpack(columns_b, rows_recv_b)
    gap = back + first
    inverse_ramp = 1.0 / ramp_ref[...].astype(F32)
    lane_gap = iota((angles_here, gap * LANES), 1)
    left_at = step_cols // LANES - back - 1
    zeros = jnp.zeros((angles_here, (back + 1) * LANES), F32)
    segments = [(0, first, -jnp.log(tile_rows(0, 0, first)))]
    for g0 in range(1, tiles, 2):
        group = range(g0, min(g0 + 2, tiles))
        pieces, aheads = [], []
        for g in group:
            pieces.append(
                jnp.concatenate([tile_rows(g - 1, left_at, chunks)] + [zeros], axis=1)
            )
            pieces.append(jnp.concatenate([zeros, tile_rows(g, 0, gap + 1 - back)], axis=1))
            aheads += [shifts[g - 1], shifts[g]]
        moved = shifted(jnp.concatenate(pieces, axis=0), jnp.concatenate(aheads, axis=0))
        for i, g in enumerate(group):
            left = moved[2 * i * angles_here : (2 * i + 1) * angles_here]
            right = moved[(2 * i + 1) * angles_here : (2 * i + 2) * angles_here]
            ahead_left = jnp.concatenate([shifts[g - 1]] * gap, axis=1)
            ahead_right = jnp.concatenate([shifts[g]] * gap, axis=1)
            x_left = lane_gap + ahead_left + left_at * LANES
            x_right = lane_gap + ahead_right - (back + 1) * LANES
            feather_left = (tile_width - x_left).astype(F32) * inverse_ramp[:, g - 1 : g]
            feather_right = (x_right + 1).astype(F32) * inverse_ramp[:, g : g + 1]
            feather_left = jnp.maximum(jnp.minimum(1.0, feather_left), 0.0)
            feather_right = jnp.maximum(jnp.minimum(1.0, feather_right), 0.0)
            blended = (feather_left * left + feather_right * right) / (
                feather_left + feather_right
            )
            segments.append((g * (step_cols // LANES) - back, gap, -jnp.log(blended)))
    last = (tiles - 1) * (step_cols // LANES) + first
    segments.append((last, chunks - first, -jnp.log(tile_rows(tiles - 1, first, chunks))))
    for at, count, flat in segments:
        proj_ref[:, at * LANES : (at + count) * LANES] = flat
    spread_out = jnp.concatenate([flat for _, _, flat in segments], axis=1)
    flats = [spread_out[:, p * width : (p + 1) * width] for p in range(devices)]
    total_b = jnp.zeros((4 * angles_here, mods), F32)
    for p in range(devices):
        total_b = total_b + dot_nt(thirds(flats[p]), member_late_ref[p])
    mean = (gather_thirds(total_a) + gather_thirds(total_b)) / safe_wide
    mean_parts = thirds(mean)
    diff = mean_a - mean
    diff = jnp.concatenate([diff] * angles_here, axis=1)
    own = (iota((angles_here, LANES), 1) // mods) == iota((angles_here, LANES), 0)
    diff_row = jnp.sum(jnp.where(own, diff, 0.0), axis=0, keepdims=True)
    diff_send[...] = diff_row
    for peer in peers:
        remote(DIFF, diff_send, diff_recv.at[me], me, peer).start()
    diff_recv[me] = diff_row
    for p in range(devices):
        flat = flats[p] - gather_thirds(dot(mean_parts, member_late_ref[p]))
        flat = jnp.concatenate([flat[:, :half], flat[:, half:]], axis=0)
        cent_send_b[p] = flat.astype(BF16)
    send_all(CENT_B, cent_send_b, cent_recv_b)
    cent_recv_b[me] = cent_send_b[me]

    shared_row = iota((fold * angles_here, fold * angles_here), 0)
    shared_col = iota((fold * angles_here, fold * angles_here), 1)
    same = (shared_row // angles_here) == (shared_col // angles_here)
    shared_table = jnp.where(same, SHARED / angles_here, 0.0).astype(BF16)
    for p in range(devices):
        for send_ref, block_list in ((cent_send_a, early[p]), (cent_send_b, late[p])):
            shared = dot(shared_table, send_ref[p])
            for i, b in enumerate(block_list):
                part, at = divmod(i, mine // 2)
                piece = shared[
                    part * angles_here : (part + 1) * angles_here, at * LANES : (at + 1) * LANES
                ]
                proj_ref[:, b * LANES : (b + 1) * LANES] = (
                    proj_ref[:, b * LANES : (b + 1) * LANES] - piece
                )
    clean_ref[:, 0:LANES] = jnp.zeros((angles_here, LANES), F32)
    clean_ref[:, W + LANES :] = jnp.zeros((angles_here, LANES), F32)
    fetch_fwd.wait()
    fetch_inv.wait()
    fetch_taps.wait()

    k = iota((rows, 1), 0)
    count_of = jnp.where((k == 0) | (2 * k == angles), 1.0, 2.0)
    count_of = jnp.where(2 * k <= angles, count_of, 0.0)

    def magnitude_of(spectrum):
        return jnp.sqrt(spectrum[:rows] * spectrum[:rows] + spectrum[rows:] * spectrum[rows:])

    def summed(spectrum, inside):
        over_k = jnp.sum(magnitude_of(spectrum) * count_of, axis=0, keepdims=True)
        first_row = jnp.where(iota((8, half), 0) == 0, over_k, 0.0)
        return dot_nt(thirds(first_row), inside)

    member_own = [
        member_ref[
            :, pl.ds(pl.multiple_of(me * step_cols + first * LANES + part * half, LANES), half)
        ]
        for part in range(fold)
    ]
    member_own += [
        member_late_ref[me][:, part * half : (part + 1) * half] for part in range(fold)
    ]

    wait_recv(CENT_A, cent_send_a, cent_recv_a)
    signal_a = cent_recv_a[...].reshape(devices * fold * angles_here, half)
    sums = jnp.zeros((4 * 8, mods), F32)
    found = []
    for part in range(fold):
        spread = dot(fwd_ref[part], signal_a)
        found.append(spread[: 2 * rows] + spread[2 * rows :])
    for peer in peers:
        remote(DIFF, diff_send, diff_recv.at[peer], peer, peer).wait_recv()
    diffs = []
    for p in range(devices):
        spread = jnp.where(own, jnp.broadcast_to(diff_recv[p], (angles_here, LANES)), 0.0)
        diffs += [spread] * fold
    high, low = halves(jnp.concatenate(diffs, axis=0))
    shift = dot(fwd_ref[0], jnp.concatenate([high, low], axis=1))
    shift = shift[: 2 * rows] + shift[2 * rows :]
    high, low = halves(shift[:, :LANES] + shift[:, LANES:])
    shift = jnp.concatenate([high, low], axis=1)
    for part in range(fold):
        inside = jnp.concatenate([member_own[part]] * (2 * LANES // mods), axis=0)
        spectrum = found[part] + dot(shift, inside)
        spec_ref[part] = spectrum
        sums = sums + summed(spectrum, member_own[part])

    wait_recv(CENT_B, cent_send_b, cent_recv_b)
    signal_b = cent_recv_b[...].reshape(devices * fold * angles_here, half)
    for part in range(fold):
        spread = dot(fwd_ref[part], signal_b)
        spectrum = spread[: 2 * rows] + spread[2 * rows :]
        spec_ref[fold + part] = spectrum
        sums = sums + summed(spectrum, member_own[fold + part])
    level_send[...] = jnp.zeros_like(level_send)
    level_send[:, 0:mods] = sums[0:1] + sums[8:9] + sums[16:17]
    for peer in peers:
        remote(LEVEL, level_send, level_recv.at[me], me, peer).start()
    level_recv[me] = level_send[...]
    wait_send(IDS, ids_send, ids_recv)
    wait_send(ROWS_A, rows_send_a, rows_recv_a)
    wait_send(ROWS_B, rows_send_b, rows_recv_b)
    for peer in peers:
        remote(LEVEL, level_send, level_recv.at[peer], peer, peer).wait_recv()
    everything = jnp.sum(level_recv[...], axis=0)[:, 0:mods]
    level = SHRINK_SCALE * (everything / (angles * safe_wide) + EPSILON)
    level_parts = thirds(jnp.where(iota((8, mods), 0) == 0, level, 0.0))

    def inverse(at, part, signal):
        spread = dot(level_parts, member_own[at])
        level_col = spread[0:1] + spread[8:9] + spread[16:17]
        spectrum = spec_ref[at]
        magnitude = magnitude_of(spectrum)
        factor = jnp.maximum(magnitude - level_col, 0.0) / jnp.maximum(magnitude, level_col)
        shrunk = jnp.concatenate([spectrum[:rows] * factor, spectrum[rows:] * factor], axis=0)
        high, low = halves(shrunk)
        stripe = dot(inv_ref[part], jnp.concatenate([high, low, high, signal], axis=0))
        return stripe.reshape(devices, angles_here, half)

    both = [inverse(part, part, signal_a) for part in range(fold)]
    stripe_send_a[...] = jnp.concatenate(both, axis=1).astype(BF16)
    send_all(STRIPE_A, stripe_send_a, stripe_recv_a)
    both = [inverse(fold + part, part, signal_b) for part in range(fold)]
    stripe_send_b[...] = jnp.concatenate(both, axis=1).astype(BF16)
    send_all(STRIPE_B, stripe_send_b, stripe_recv_b)
    stripe_recv_a[me] = stripe_send_a[me]
    stripe_recv_b[me] = stripe_send_b[me]
    wait_send(CENT_A, cent_send_a, cent_recv_a)
    wait_send(CENT_B, cent_send_b, cent_recv_b)
    for peer in peers:
        remote(DIFF, diff_send, diff_recv.at[peer], peer, peer).wait_send()
        remote(LEVEL, level_send, level_recv.at[peer], peer, peer).wait_send()

    def clean(recv_ref, block_lists):
        for p in range(devices):
            rest = recv_ref[p].astype(F32)
            for i, b in enumerate(block_lists[p]):
                part, at = divmod(i, mine // 2)
                piece = rest[
                    part * angles_here : (part + 1) * angles_here, at * LANES : (at + 1) * LANES
                ]
                clean_ref[:, (b + 1) * LANES : (b + 2) * LANES] = (
                    proj_ref[:, b * LANES : (b + 1) * LANES] - piece
                )

    def ramp(block_list):
        near = jnp.concatenate(
            [clean_ref[:, b * LANES : (b + 3) * LANES] for b in block_list], axis=0
        )
        high, low = halves(near)
        done = dot(high, taps_ref[0]) + dot(low, taps_ref[0]) + dot(high, taps_ref[1])
        for i, b in enumerate(block_list):
            out_ref[:, b * LANES : (b + 1) * LANES] = done[i * angles_here : (i + 1) * angles_here]

    wait_recv(STRIPE_A, stripe_send_a, stripe_recv_a)
    clean(stripe_recv_a, early)
    inner = [b for run in early for b in run[1:-1]]
    outer = [b for b in range(W // LANES) if b not in set(inner)]
    for at in range(0, len(inner), 16):
        ramp(inner[at : at + 16])
    wait_recv(STRIPE_B, stripe_send_b, stripe_recv_b)
    clean(stripe_recv_b, late)
    for at in range(0, len(outer), 16):
        ramp(outer[at : at + 16])
    wait_send(STRIPE_A, stripe_send_a, stripe_recv_a)
    wait_send(STRIPE_B, stripe_send_b, stripe_recv_b)


def fast_call(cfg, plan, tables, args):
    devices, angles_here, tiles, tile_width, mods, fold = cfg
    cap, split, mine = plan[0], plan[1], plan[6]
    rows = freq_rows(devices * angles_here)
    half = mine * LANES // 2
    vmem = pl.BlockSpec(memory_space=pltpu.VMEM)
    message = pltpu.VMEM((devices, fold * angles_here, half), BF16)
    line = pltpu.VMEM((1, LANES), F32)
    lines = pltpu.VMEM((devices, 1, LANES), F32)
    rows_a = pltpu.VMEM((devices, 16, split * LANES), BF16)
    rows_b = pltpu.VMEM((devices, 16, (cap - split) * LANES), BF16)
    return pl.pallas_call(
        functools.partial(fast_kernel, cfg, plan),
        out_shape=pltpu.VMEM((angles_here, W), F32),
        in_specs=[vmem] * 5 + [pl.BlockSpec(memory_space=pl.ANY)] * 3,
        out_specs=vmem,
        scratch_shapes=[
            rows_a,
            rows_a,
            rows_b,
            rows_b,
            lines,
            lines,
            pltpu.VMEM((angles_here * tiles, tile_width), F32),
            pltpu.VMEM((angles_here, W + 2 * LANES), F32),
            pltpu.VMEM((angles_here, W), F32),
            pltpu.VMEM((mods, W), BF16),
            pltpu.VMEM((devices, mods, mine * LANES), BF16),
            message,
            message,
            message,
            message,
            line,
            lines,
            pltpu.VMEM((2 * fold, 2 * rows, half), F32),
            line,
            lines,
            message,
            message,
            message,
            message,
            *[pltpu.VMEM(table.shape, BF16) for table in tables],
            pltpu.SemaphoreType.DMA((3,)),
            pltpu.SemaphoreType.DMA((9, devices)),
            pltpu.SemaphoreType.DMA((9, devices)),
        ],
        compiler_params=pltpu.CompilerParams(
            collective_id=0, has_side_effects=True, vmem_limit_bytes=60 << 20
        ),
    )(*args, *[jnp.asarray(table) for table in tables])


def per_device(raw, block_dest, section_offset, ramp_length, module_width):
    devices = lax.axis_size("ang")
    blocks_here = raw.shape[0]
    tile_width = raw.shape[1]
    angles_here, tiles = section_offset.shape
    angles = angles_here * devices
    capacity = (blocks_here + devices - 1) // devices
    cols = W // devices
    fold = 2 if cols % (2 * LANES) == 0 else 1
    wire = BF16 if fold == 2 else F32
    mods = -(-module_width.shape[0] // 16) * 16
    half = cols // fold
    rows = freq_rows(angles)
    cfg = (devices, angles_here, tiles, tile_width, mods, fold)
    forward = forward_table(angles, devices, fold)
    inverse = inverse_table(angles, devices, fold)
    taps = ramp_table()
    plan = fast_plan(devices, angles_here, tiles, tile_width, mods)
    if fold == 2 and plan:
        args = (
            raw,
            block_dest[None, :],
            section_offset,
            ramp_length[None, :],
            module_width[None, :],
        )
        return fast_call(cfg, plan, (forward, inverse, taps), args)
    vmem = pl.BlockSpec(memory_space=pltpu.VMEM)
    return pl.pallas_call(
        functools.partial(kernel, cfg),
        out_shape=pltpu.VMEM((angles_here, W), F32),
        in_specs=[vmem] * 5 + [pl.BlockSpec(memory_space=pl.ANY)] * 3,
        out_specs=vmem,
        scratch_shapes=[
            pltpu.VMEM((devices, 16, capacity * LANES), BF16),
            pltpu.VMEM((devices, 16, capacity * LANES), BF16),
            pltpu.VMEM((angles_here * tiles, tile_width), F32),
            pltpu.VMEM((angles_here, W + 2 * LANES), F32),
            pltpu.VMEM((angles_here, W + 2 * LANES), F32),
            pltpu.VMEM((angles_here, W), F32),
            pltpu.VMEM((devices, angles_here * fold, half), wire),
            pltpu.VMEM((devices, angles_here * fold, half), wire),
            pltpu.VMEM((fold, 2 * rows, half), F32),
            pltpu.VMEM((8, max(mods, LANES)), F32),
            pltpu.VMEM((devices, 8, max(mods, LANES)), F32),
            pltpu.VMEM((devices, angles_here * fold, half), wire),
            pltpu.VMEM((devices, angles_here * fold, half), wire),
            pltpu.VMEM((devices, 1, LANES), F32),
            pltpu.VMEM((devices, 1, LANES), F32),
            pltpu.VMEM(forward.shape, BF16),
            pltpu.VMEM(inverse.shape, BF16),
            pltpu.VMEM(taps.shape, BF16),
            pltpu.SemaphoreType.DMA((3,)),
            pltpu.SemaphoreType.DMA((5, devices)),
            pltpu.SemaphoreType.DMA((5, devices)),
        ],
        compiler_params=pltpu.CompilerParams(
            collective_id=0, has_side_effects=True, vmem_limit_bytes=60 << 20
        ),
    )(
        raw,
        block_dest[None, :],
        section_offset,
        ramp_length[None, :],
        module_width[None, :],
        jnp.asarray(forward),
        jnp.asarray(inverse),
        jnp.asarray(taps),
    )


def solution(mesh):
    in_specs = (P(("row", "ang"), None), P("ang"), P("ang", None), P(), P())
    out_specs = P(("row", "ang"), None)
    return jax.shard_map(
        per_device, mesh=mesh, in_specs=in_specs, out_specs=out_specs, check_vma=False
    )
```

```python
import functools
import math

import jax
import jax.numpy as jnp
import ml_dtypes
import numpy as np
from jax import lax
from jax.experimental import pallas as pl
from jax.experimental.pallas import tpu as pltpu
from jax.sharding import PartitionSpec as P

W = 16384
RAMP_HALF = 128
JITTER = 64
SHRINK_SCALE = 1.0
EPSILON = 1e-06
LANES = 128
SPAN = 2048
SHARED = 0.625

F32 = jnp.float32
BF16 = jnp.bfloat16


def split_np(table):
    high = table.astype(ml_dtypes.bfloat16)
    low = (table - high.astype(np.float64)).astype(ml_dtypes.bfloat16)
    return high, low


def freq_rows(angles):
    return -(-(angles // 2 + 1) // 8) * 8


def forward_table(angles, devices, fold):
    rows = freq_rows(angles)
    here = angles // devices
    k = np.arange(rows)[:, None]
    a = np.arange(angles)[None, :]
    phase = 2.0 * np.pi * ((k * a) % angles) / angles
    keep = (k <= angles // 2).astype(np.float64)
    table = np.concatenate([np.cos(phase) * keep, -np.sin(phase) * keep], axis=0)
    placed = np.zeros((fold, 2 * rows, devices, fold, here))
    for part in range(fold):
        placed[part, :, :, part, :] = table.reshape(2 * rows, devices, here)
    high, low = split_np(placed.reshape(fold, 2 * rows, devices * fold * here))
    return np.concatenate([high, low], axis=1)


def inverse_table(angles, devices, fold):
    rows = freq_rows(angles)
    k = np.arange(rows)[None, :]
    a = np.arange(angles)[:, None]
    phase = 2.0 * np.pi * ((k * a) % angles) / angles
    twice = np.where((k == 0) | (2 * k == angles), 1.0, 2.0) * (k <= angles // 2)
    weight = twice * np.exp(-np.minimum(k, angles - k) / (angles // 8)) / angles
    table = np.concatenate([np.cos(phase) * weight, -np.sin(phase) * weight], axis=1)
    high, low = split_np(table)
    table = np.concatenate([high, high, low], axis=1)
    if fold == 1:
        return table[None]
    here = angles // devices
    shared = np.kron(np.eye(devices), np.ones((here, here))) * (SHARED / here)
    placed = np.zeros((fold, angles, devices, fold, here))
    for part in range(fold):
        placed[part, :, :, part, :] = -shared.reshape(angles, devices, here)
    placed = placed.reshape(fold, angles, devices * fold * here).astype(ml_dtypes.bfloat16)
    return np.concatenate([np.broadcast_to(table, (fold,) + table.shape), placed], axis=2)


def ramp_table():
    i = np.arange(3 * LANES)[:, None] - LANES
    n = np.arange(LANES)[None, :] - i
    safe = np.where(n == 0, 1, n).astype(np.float64)
    taps = np.where(n % 2 != 0, -1.0 / (np.pi * np.pi * safe * safe), 0.0)
    taps = np.where(n == 0, 0.25, taps)
    taps = np.where(np.abs(n) <= RAMP_HALF, taps, 0.0)
    high, low = split_np(taps)
    return np.stack([high, low])


def dot(left, right):
    return jnp.dot(left, right, preferred_element_type=F32)


def dot_nt(left, right):
    return lax.dot_general(left, right, (((1,), (1,)), ((), ())), preferred_element_type=F32)


def halves(x):
    high = x.astype(BF16)
    return high, (x - high.astype(F32)).astype(BF16)


def thirds(x):
    high = x.astype(BF16).astype(F32)
    rest = x - high
    mid = rest.astype(BF16).astype(F32)
    low = rest - mid
    return jnp.concatenate([high, mid, low, jnp.zeros_like(x)], axis=0).astype(BF16)


def iota(shape, axis):
    return lax.broadcasted_iota(jnp.int32, shape, axis)


def loop(count, body):
    if count <= 8:
        for step in range(count):
            body(step)
    else:

        def run(step, carry):
            body(step)
            return carry

        lax.fori_loop(0, count, run, 0)


def kernel(
    cfg,
    raw_ref,
    dest_ref,
    offset_ref,
    ramp_ref,
    width_ref,
    fwd_hbm,
    inv_hbm,
    taps_hbm,
    out_ref,
    rows_send,
    rows_recv,
    grid_ref,
    sum_ref,
    weight_ref,
    proj_ref,
    cent_send,
    cent_recv,
    spec_ref,
    level_send,
    level_recv,
    stripe_send,
    stripe_recv,
    ids_send,
    ids_recv,
    fwd_ref,
    inv_ref,
    taps_ref,
    table_sem,
    send_sem,
    recv_sem,
):
    devices, angles_here, tiles, tile_width, mods, fold = cfg
    angles = devices * angles_here
    cols = W // devices
    half = cols // fold
    rows = freq_rows(angles)
    step_cols = (W - tile_width) // (tiles - 1)
    window = tile_width + 2 * LANES
    blocks = angles_here * tiles
    me = lax.axis_index("ang")

    def ring_at(hop):
        return lax.rem(me + hop, devices)

    def peer_at(hop):
        if devices & (devices - 1):
            return ring_at(hop)
        mask = devices - hop
        peer = 0
        bit = 1
        while bit < devices:
            peer = peer + bit * lax.rem(lax.div(me, bit) + mask // bit, 2)
            bit *= 2
        return peer

    barrier = pltpu.get_barrier_semaphore()

    def greet(step):
        pl.semaphore_signal(
            barrier,
            inc=1,
            device_id={"ang": peer_at(step + 1)},
            device_id_type=pl.DeviceIdType.MESH,
        )

    loop(devices - 1, greet)
    fetch_fwd = pltpu.make_async_copy(fwd_hbm, fwd_ref, table_sem.at[0])
    fetch_inv = pltpu.make_async_copy(inv_hbm, inv_ref, table_sem.at[1])
    fetch_taps = pltpu.make_async_copy(taps_hbm, taps_ref, table_sem.at[2])
    fetch_fwd.start()
    fetch_inv.start()
    fetch_taps.start()

    def remote(phase, src, dst, slot, peer):
        return pltpu.make_async_remote_copy(
            src_ref=src,
            dst_ref=dst,
            send_sem=send_sem.at[phase, peer],
            recv_sem=recv_sem.at[phase, slot],
            device_id={"ang": peer},
            device_id_type=pl.DeviceIdType.MESH,
        )

    def finish(phase, send_of, recv_of):
        def body(step):
            peer = peer_at(step + 1)
            copy = remote(phase, send_of(peer), recv_of(peer), peer, peer)
            copy.wait_recv()
            copy.wait_send()

        loop(devices - 1, body)

    cap = -(-blocks // devices)
    slab = 16
    chunks = tile_width // LANES
    extra = chunks - cap
    slots = devices * slab
    dest_row = dest_ref[...].astype(F32)
    source_row = iota((blocks, blocks), 1)
    source_col = iota((blocks, blocks), 0)

    def turned(values):
        return jnp.sum(jnp.where(source_row == source_col, values, 0.0), axis=1, keepdims=True)

    owner_row = jnp.floor((dest_row + 0.5) * (1.0 / blocks))
    owner_col = turned(owner_row)
    earlier = (owner_col == owner_row) & (source_col < source_row)
    rank_row = jnp.sum(jnp.where(earlier, 1.0, 0.0), axis=0, keepdims=True)
    rank_col = turned(rank_row)
    place_row = dest_row - owner_row * blocks + 1.0
    slot = iota((slots, 1), 0).astype(F32)

    def one_hot(left, right):
        return jnp.where(left == right, 1.0, 0.0).astype(BF16)

    direct = one_hot(slot, owner_row * slab + rank_row)
    packed = dot(direct, raw_ref[:, : cap * LANES])
    keeps = [
        jnp.where(jnp.broadcast_to(rank_col, (blocks, LANES)) == j, 1.0, 0.0).astype(BF16)
        for j in range(cap)
    ]
    for e in range(extra):
        chunk = raw_ref[:, (cap + e) * LANES : (cap + e + 1) * LANES]
        masked = jnp.concatenate([chunk * keep for keep in keeps], axis=1)
        packed = packed + dot(one_hot(slot, owner_row * slab + (cap + e)), masked)
    rows_send[...] = packed.astype(BF16).reshape(devices, slab, cap * LANES)
    group = LANES // slab
    groups = -(-devices // group)
    lane_at = iota((blocks, LANES), 1).astype(F32)
    first_lane = (lax.rem(me, group) * slab).astype(F32)
    at_rank = one_hot(lane_at, rank_col + first_lane)
    to_owner = jnp.where(iota((devices, blocks), 0).astype(F32) == owner_row, place_row, 0.0)
    ids_send[...] = dot(to_owner.astype(BF16), at_rank).reshape(devices, 1, LANES)

    pl.semaphore_wait(barrier, devices - 1)

    def send_rows(step):
        peer = peer_at(step + 1)
        remote(4, ids_send.at[peer], ids_recv.at[me], me, peer).start()
        remote(0, rows_send.at[peer], rows_recv.at[me], me, peer).start()

    loop(devices - 1, send_rows)
    rows_recv[me] = rows_send[me]
    ids_recv[me] = ids_send[me]
    finish(4, lambda p: ids_send.at[p], lambda p: ids_recv.at[p])
    finish(0, lambda p: rows_send.at[p], lambda p: rows_recv.at[p])

    ids = [
        jnp.sum(ids_recv[g * group : min((g + 1) * group, devices)], axis=0) for g in range(groups)
    ]
    ids = ids[0] if groups == 1 else jnp.concatenate(ids, axis=1)
    ids = jnp.broadcast_to(ids[:, :slots], (8, slots))
    row = iota((blocks, 1), 0).astype(F32)
    tile_of = jnp.floor((row + 0.5) * (1.0 / angles_here))
    wanted = (row - tile_of * angles_here) * tiles + tile_of + 1.0
    lead = rows_recv[...].reshape(slots, cap * LANES)
    grid_ref[:, : cap * LANES] = dot(one_hot(wanted, ids[0:1]), lead)
    if extra:
        within = iota((8, slots), 1) & (slab - 1)
        turns = [pltpu.roll(ids, n, 1) if n else ids for n in range(slab)]
        wanted_at = jnp.concatenate(
            [jnp.where(within[0:1] == cap + e, wanted, -1.0) for e in range(extra)], axis=0
        )
        rest = jnp.zeros((extra * blocks, LANES), F32)
        for j in range(cap):
            ids_j = jnp.zeros((8, slots), F32)
            for e in range(extra):
                ids_j = jnp.where(within == cap + e, turns[cap + e - j], ids_j)
            part = rows_recv[:, :, j * LANES : (j + 1) * LANES].reshape(slots, LANES)
            rest = rest + dot(one_hot(wanted_at, ids_j[0:1]), part)
        for e in range(extra):
            at = (cap + e) * LANES
            grid_ref[:, at : at + LANES] = rest[e * blocks : (e + 1) * blocks]

    fetch_fwd.wait()
    fetch_inv.wait()
    fetch_taps.wait()

    sum_ref[...] = jnp.zeros_like(sum_ref)
    weight_ref[...] = jnp.zeros_like(weight_ref)
    inverse_ramp = 1.0 / ramp_ref[...].astype(F32)
    lane = iota((angles_here, window), 1)
    for tile in range(tiles):
        base = tile * step_cols
        shift = jnp.broadcast_to(
            offset_ref[:, tile : tile + 1] - (base - LANES), (angles_here, window)
        )
        piece = jnp.concatenate(
            [
                grid_ref[tile * angles_here : (tile + 1) * angles_here, :],
                jnp.zeros((angles_here, 2 * LANES), F32),
            ],
            axis=1,
        )
        for bit in range(8):
            moved = pltpu.roll(piece, 1 << bit, 1)
            piece = jnp.where((shift & (1 << bit)) != 0, moved, piece)
        x = lane - shift
        edge = (jnp.minimum(x, tile_width - 1 - x) + 1).astype(F32)
        feather = jnp.minimum(1.0, edge * inverse_ramp[:, tile : tile + 1])
        feather = jnp.maximum(feather, 0.0)
        sum_ref[:, base : base + window] += feather * piece
        weight_ref[:, base : base + window] += feather

    wide = width_ref[...].astype(F32)
    upper = iota((mods, wide.shape[1]), 1)
    lower = iota((mods, wide.shape[1]), 0)
    bounds = jnp.sum(jnp.where(upper <= lower, wide, 0.0), axis=1, keepdims=True)
    starts = jnp.sum(jnp.where(upper < lower, wide, 0.0), axis=1, keepdims=True)
    on_diagonal = iota((mods, mods), 0) == iota((mods, mods), 1)
    safe_wide = jnp.sum(jnp.where(on_diagonal, bounds - starts, 0.0), axis=0, keepdims=True)
    safe_wide = jnp.maximum(safe_wide, 1.0)

    def member(first, count):
        c = (iota((mods, count), 1) + first).astype(F32)
        inside = (c >= starts) & (c < bounds)
        return jnp.where(inside, 1.0, 0.0).astype(BF16)

    def project(step, total):
        at = step * SPAN
        behind = at + LANES
        blended = sum_ref[:, pl.ds(behind, SPAN)] / weight_ref[:, pl.ds(behind, SPAN)]
        projection = -jnp.log(blended)
        proj_ref[:, pl.ds(at, SPAN)] = projection
        return total + dot_nt(thirds(projection), member(at, SPAN))

    total = jnp.zeros((4 * angles_here, mods), F32)
    for step in range(W // SPAN):
        total = project(step, total)

    def gather_thirds(stack):
        a = angles_here
        return stack[0:a] + stack[a : 2 * a] + stack[2 * a : 3 * a]

    mean = thirds(gather_thirds(total) / safe_wide)

    def centered_slab(owner):
        at = pl.multiple_of(owner * cols, LANES)
        flat = proj_ref[:, pl.ds(at, cols)] - gather_thirds(dot(mean, member(at, cols)))
        if fold > 1:
            flat = jnp.concatenate([flat[:, i * half : (i + 1) * half] for i in range(fold)], axis=0)
        return flat.astype(cent_send.dtype)

    def send_centered(step):
        peer = peer_at(step + 1)
        cent_send[peer] = centered_slab(peer)
        remote(1, cent_send.at[peer], cent_recv.at[me], me, peer).start()

    loop(devices - 1, send_centered)
    cent_send[me] = centered_slab(me)
    cent_recv[me] = cent_send[me]

    if fold > 1:
        shared_row = iota((fold * angles_here, fold * angles_here), 0)
        shared_col = iota((fold * angles_here, fold * angles_here), 1)
        same = (shared_row // angles_here) == (shared_col // angles_here)
        shared_table = jnp.where(same, SHARED / angles_here, 0.0).astype(BF16)

        def take_shared(owner):
            at = pl.multiple_of(owner * cols, LANES)
            shared = dot(shared_table, cent_send[owner])
            shared = jnp.concatenate(
                [shared[i * angles_here : (i + 1) * angles_here] for i in range(fold)], axis=1
            )
            proj_ref[:, pl.ds(at, cols)] = proj_ref[:, pl.ds(at, cols)] - shared

        loop(devices, take_shared)

    finish(1, lambda p: cent_send.at[p], lambda p: cent_recv.at[p])

    signal = cent_recv[...].reshape(devices * fold * angles_here, half).astype(BF16)
    k = iota((rows, 1), 0)
    count_of = jnp.where((k == 0) | (2 * k == angles), 1.0, 2.0)
    count_of = jnp.where(2 * k <= angles, count_of, 0.0)
    mine = pl.multiple_of(me * cols, LANES)
    sums = jnp.zeros((4 * 8, mods), F32)
    for part in range(fold):
        wide_spec = dot(fwd_ref[part], signal)
        spectrum = wide_spec[: 2 * rows] + wide_spec[2 * rows :]
        spec_ref[part] = spectrum
        magnitude = jnp.sqrt(
            spectrum[:rows] * spectrum[:rows] + spectrum[rows:] * spectrum[rows:]
        )
        over_k = jnp.sum(magnitude * count_of, axis=0, keepdims=True)
        first_row = jnp.where(iota((8, half), 0) == 0, over_k, 0.0)
        sums = sums + dot_nt(thirds(first_row), member(mine + part * half, half))
    level_send[...] = jnp.zeros_like(level_send)
    level_send[:, 0:mods] = sums[0:8] + sums[8:16] + sums[16:24]

    def send_level(step):
        peer = peer_at(step + 1)
        remote(2, level_send, level_recv.at[me], me, peer).start()

    loop(devices - 1, send_level)
    level_recv[me] = level_send[...]
    finish(2, lambda p: level_send, lambda p: level_recv.at[p])
    everything = jnp.sum(level_recv[...], axis=0)[:, 0:mods]
    level = SHRINK_SCALE * (everything / (angles * safe_wide) + EPSILON)
    level_parts = thirds(jnp.where(iota((8, mods), 0) == 0, level, 0.0))

    residual = []
    for part in range(fold):
        spread = dot(level_parts, member(mine + part * half, half))
        level_col = spread[0:1] + spread[8:9] + spread[16:17]
        spectrum = spec_ref[part]
        magnitude = jnp.sqrt(
            spectrum[:rows] * spectrum[:rows] + spectrum[rows:] * spectrum[rows:]
        )
        factor = jnp.maximum(magnitude - level_col, 0.0) / jnp.maximum(magnitude, level_col)
        shrunk = jnp.concatenate([spectrum[:rows] * factor, spectrum[rows:] * factor], axis=0)
        high, low = halves(shrunk)
        parts = [high, low, high] + ([signal] if fold > 1 else [])
        stripe = dot(inv_ref[part], jnp.concatenate(parts, axis=0))
        residual.append(stripe.reshape(devices, angles_here, half))
    stripe_send[...] = jnp.concatenate(residual, axis=1).astype(stripe_send.dtype)

    def send_stripe(step):
        peer = ring_at(step + 1)
        remote(3, stripe_send.at[peer], stripe_recv.at[me], me, peer).start()

    loop(devices - 1, send_stripe)
    stripe_recv[me] = stripe_send[me]

    sum_ref[:, 0:LANES] = jnp.zeros((angles_here, LANES), F32)
    sum_ref[:, W + LANES :] = jnp.zeros((angles_here, LANES), F32)
    lane_blocks = cols // LANES

    def clean(owner):
        at = pl.multiple_of(owner * cols, LANES)
        behind = pl.multiple_of(owner * cols + LANES, LANES)
        rest = stripe_recv[owner].astype(F32)
        rest = jnp.concatenate(
            [rest[i * angles_here : (i + 1) * angles_here] for i in range(fold)], axis=1
        )
        sum_ref[:, pl.ds(behind, cols)] = proj_ref[:, pl.ds(at, cols)] - rest

    def ramp(group):
        at = pl.multiple_of(group * cols, LANES)
        flat = sum_ref[:, pl.ds(at, cols + 2 * LANES)]
        stack = jnp.concatenate(
            [flat[:, b * LANES : (b + 1) * LANES] for b in range(lane_blocks + 2)], axis=0
        )
        n = lane_blocks * angles_here
        near = jnp.concatenate(
            [stack[s * angles_here : s * angles_here + n] for s in range(3)], axis=1
        )
        high, low = halves(near)
        done = dot(high, taps_ref[0]) + dot(low, taps_ref[0]) + dot(high, taps_ref[1])
        out_ref[:, pl.ds(at, cols)] = jnp.concatenate(
            [done[b * angles_here : (b + 1) * angles_here] for b in range(lane_blocks)], axis=1
        )

    clean(me)

    def below(hop):
        return lax.rem(me + devices - hop, devices)

    def take(hop):
        owner = below(hop)
        remote(3, stripe_send.at[owner], stripe_recv.at[owner], owner, owner).wait_recv()
        clean(owner)

    take(1)

    def advance(step):
        take(step + 2)
        ramp(below(step + 1))

    loop(devices - 2, advance)
    ramp(below(devices - 1))
    ramp(me)

    def sent(step):
        peer = ring_at(step + 1)
        remote(3, stripe_send.at[peer], stripe_recv.at[peer], peer, peer).wait_send()

    loop(devices - 1, sent)


def pack_plan(cap, chunks, first, need):
    split = next(
        (n for n in range(1, cap) if n + (chunks - cap) * n // cap >= need), 0
    )
    run = list(range(first, first + need))
    others = [b for b in range(chunks) if b not in run]
    direct = run[:split] + others[: cap - split]
    cells = {}
    n = 0
    early = (chunks - cap) * split
    for block in run[split:] + others[cap - split :]:
        for rank in range(cap):
            if n < early:
                cells[cap + n // split, n % split] = (rank, block)
            else:
                late = n - early
                cells[cap + late // (cap - split), split + late % (cap - split)] = (rank, block)
            n += 1
    return split, direct, cells


def fast_plan(devices, angles_here, tiles, tile_width, mods, modules):
    cols = W // devices
    step_cols = (W - tile_width) // (tiles - 1)
    cap = -(-angles_here * tiles // devices)
    chunks = tile_width // LANES
    if cols % (4 * LANES) or step_cols % LANES or tile_width % LANES:
        return None
    mine = cols // (2 * LANES)
    per_step = step_cols // LANES
    first = -(-(tile_width - step_cols + JITTER) // LANES) + 1
    back = per_step - first - mine
    fits = (
        tiles == devices + 1
        and angles_here == 8
        and angles_here * mods == LANES
        and modules <= 8
        and chunks == 16
        and devices * chunks == LANES
        and 1 < cap < chunks
        and back >= 1
        and tile_width < 2 * step_cols - 2 * JITTER
        and (first + mine) * LANES <= step_cols - JITTER
    )
    if not fits:
        return None
    split, direct, cells = pack_plan(cap, chunks, first - 1, mine + 2)
    if not split:
        return None
    early = [[t * per_step + first + i for i in range(mine)] for t in range(devices)]
    taken = {b for run in early for b in run}
    late = [b for b in range(W // LANES) if b not in taken]
    late = [late[p * mine : (p + 1) * mine] for p in range(devices)]
    return cap, split, direct, cells, first, back, mine, early, late


def fast_kernel(
    cfg,
    plan,
    raw_hbm,
    dest_hbm,
    offset_hbm,
    ramp_hbm,
    width_hbm,
    fwd_hbm,
    inv_hbm,
    taps_hbm,
    out_ref,
    raw_ref,
    dest_ref,
    offset_ref,
    ramp_ref,
    width_ref,
    rows_send_a,
    rows_recv_a,
    rows_send_b,
    rows_recv_b,
    ids_send,
    ids_recv,
    grid_ref,
    clean_ref,
    proj_ref,
    member_ref,
    member_late_ref,
    inside_ref,
    inside_late_ref,
    cent_send_a,
    cent_recv_a,
    cent_send_b,
    cent_recv_b,
    diff_send,
    diff_recv,
    spec_ref,
    level_send,
    level_recv,
    stripe_send_a,
    stripe_recv_a,
    stripe_send_b,
    stripe_recv_b,
    fwd_ref,
    inv_ref,
    taps_ref,
    table_sem,
    send_sem,
    recv_sem,
):
    devices, angles_here, tiles, tile_width, mods, fold = cfg
    cap, split, direct_blocks, cells, first, back, mine, early, late = plan
    angles = devices * angles_here
    rows = freq_rows(angles)
    step_cols = (W - tile_width) // (tiles - 1)
    blocks = angles_here * tiles
    chunks = tile_width // LANES
    slab = chunks
    slots = devices * slab
    width = mine * LANES
    half = width // 2
    me = lax.axis_index("ang")
    ROWS_A, ROWS_B, IDS, CENT_A, CENT_B, DIFF, LEVEL, STRIPE_A, STRIPE_B = range(9)

    def peer_at(hop):
        mask = devices - hop
        peer = 0
        bit = 1
        while bit < devices:
            peer = peer + bit * lax.rem(lax.div(me, bit) + mask // bit, 2)
            bit *= 2
        return peer

    peers = [peer_at(hop) for hop in range(1, devices)]
    barrier = pltpu.get_barrier_semaphore()
    for peer in peers:
        pl.semaphore_signal(
            barrier, inc=1, device_id={"ang": peer}, device_id_type=pl.DeviceIdType.MESH
        )
    fetched = [
        (dest_hbm, dest_ref),
        (raw_hbm, raw_ref),
        (width_hbm, width_ref),
        (offset_hbm, offset_ref),
        (ramp_hbm, ramp_ref),
        (fwd_hbm, fwd_ref),
        (inv_hbm, inv_ref),
        (taps_hbm, taps_ref),
    ]
    fetches = [
        pltpu.make_async_copy(src, dst, table_sem.at[i]) for i, (src, dst) in enumerate(fetched)
    ]
    for fetch in fetches:
        fetch.start()

    def remote(phase, src, dst, slot, peer):
        return pltpu.make_async_remote_copy(
            src_ref=src,
            dst_ref=dst,
            send_sem=send_sem.at[phase, peer],
            recv_sem=recv_sem.at[phase, slot],
            device_id={"ang": peer},
            device_id_type=pl.DeviceIdType.MESH,
        )

    def send_all(phase, send_ref, recv_ref):
        for peer in peers:
            remote(phase, send_ref.at[peer], recv_ref.at[me], me, peer).start()

    def wait_recv(phase, send_ref, recv_ref):
        for peer in peers:
            remote(phase, send_ref.at[peer], recv_ref.at[peer], peer, peer).wait_recv()

    def wait_send(phase, send_ref, recv_ref):
        for peer in peers:
            remote(phase, send_ref.at[peer], recv_ref.at[peer], peer, peer).wait_send()

    fetches[0].wait()
    dest_row = dest_ref[...].astype(F32)
    source_row = iota((blocks, blocks), 1)
    source_col = iota((blocks, blocks), 0)

    def turned(values):
        return jnp.sum(jnp.where(source_row == source_col, values, 0.0), axis=1, keepdims=True)

    owner_row = jnp.floor((dest_row + 0.5) * (1.0 / blocks))
    owner_col = turned(owner_row)
    earlier = (owner_col == owner_row) & (source_col < source_row)
    rank_row = jnp.sum(jnp.where(earlier, 1.0, 0.0), axis=0, keepdims=True)
    rank_col = turned(rank_row)
    place_row = dest_row - owner_row * blocks + 1.0
    slot = iota((slots, 1), 0).astype(F32)

    def one_hot(left, right):
        return jnp.where(left == right, 1.0, 0.0).astype(BF16)

    direct = one_hot(slot, owner_row * slab + rank_row)
    keeps = [
        jnp.where(jnp.broadcast_to(rank_col, (blocks, LANES)) == j, 1.0, 0.0).astype(BF16)
        for j in range(cap)
    ]

    def lane_block(b):
        return raw_ref[:, b * LANES : (b + 1) * LANES]

    def pack(columns):
        packed = dot(direct, jnp.concatenate([lane_block(direct_blocks[k]) for k in columns], axis=1))
        for r in range(cap, slab):
            masked = jnp.concatenate(
                [lane_block(cells[r, k][1]) * keeps[cells[r, k][0]] for k in columns], axis=1
            )
            packed = packed + dot(one_hot(slot, owner_row * slab + r), masked)
        return packed.astype(BF16).reshape(devices, slab, len(columns) * LANES)

    columns_a = range(split)
    columns_b = range(split, cap)
    lane_at = iota((blocks, LANES), 1).astype(F32)
    first_lane = (me * slab).astype(F32)
    at_rank = one_hot(lane_at, rank_col + first_lane)
    to_owner = jnp.where(iota((devices, blocks), 0).astype(F32) == owner_row, place_row, 0.0)
    ids_send[...] = dot(to_owner.astype(BF16), at_rank).reshape(devices, 1, LANES)
    fetches[1].wait()
    rows_send_a[...] = pack(columns_a)

    pl.semaphore_wait(barrier, devices - 1)

    send_all(IDS, ids_send, ids_recv)
    send_all(ROWS_A, rows_send_a, rows_recv_a)
    rows_send_b[...] = pack(columns_b)
    send_all(ROWS_B, rows_send_b, rows_recv_b)
    rows_recv_a[me] = rows_send_a[me]
    rows_recv_b[me] = rows_send_b[me]
    ids_recv[me] = ids_send[me]

    for fetch in fetches[2:5]:
        fetch.wait()
    wide = width_ref[...].astype(F32)
    upper = iota((mods, wide.shape[1]), 1)
    lower = iota((mods, wide.shape[1]), 0)
    bounds = jnp.sum(jnp.where(upper <= lower, wide, 0.0), axis=1, keepdims=True)
    starts = jnp.sum(jnp.where(upper < lower, wide, 0.0), axis=1, keepdims=True)
    on_diagonal = iota((mods, mods), 0) == iota((mods, mods), 1)
    safe_wide = jnp.sum(jnp.where(on_diagonal, bounds - starts, 0.0), axis=0, keepdims=True)
    safe_wide = jnp.maximum(safe_wide, 1.0)
    bounds = jnp.broadcast_to(bounds, (mods, LANES))
    starts = jnp.broadcast_to(starts, (mods, LANES))
    lane = iota((mods, LANES), 1).astype(F32)
    for b in range(W // LANES):
        c = lane + float(b * LANES)
        inside = (c >= starts) & (c < bounds)
        inside = jnp.where(inside, 1.0, 0.0)
        member_ref[:, b * LANES : (b + 1) * LANES] = inside.astype(BF16)
        inside_ref[:, b * LANES : (b + 1) * LANES] = inside[0:8]
    for p in range(devices):
        for i, b in enumerate(late[p]):
            member_late_ref[p, :, i * LANES : (i + 1) * LANES] = member_ref[
                :, b * LANES : (b + 1) * LANES
            ]
            inside_late_ref[p, :, i * LANES : (i + 1) * LANES] = inside_ref[
                :, b * LANES : (b + 1) * LANES
            ]
    held = range(width_ref.shape[1])

    def inside_early(m, t):
        at = early[t][0] * LANES
        return inside_ref[m : m + 1, at : at + width]

    def inside_late(m, p):
        return inside_late_ref[p, m : m + 1, :]

    def narrowed(x):
        pieces = [x[:, i * LANES : (i + 1) * LANES] for i in range(mine)]
        while len(pieces) > 1:
            odd = pieces[len(pieces) // 2 * 2 :]
            pieces = [x + y for x, y in zip(pieces[::2], pieces[1::2])] + odd
        return pieces[0]

    def module_sums(flats, inside_of):
        sums = []
        for m in held:
            total = narrowed(flats[0] * inside_of(m, 0))
            for p in range(1, devices):
                total = total + narrowed(flats[p] * inside_of(m, p))
            sums.append(jnp.sum(total, axis=1, keepdims=True))
        return sums

    def less_mean(flat, means, inside_of, p):
        for m in held:
            flat = flat - means[m] * inside_of(m, p)
        flat = jnp.concatenate([flat[:, :half], flat[:, half:]], axis=0)
        return flat.astype(BF16)

    blank_row = jnp.ones((1, width), F32)
    counts = module_sums([blank_row] * devices, inside_early)
    scales_a = [1.0 / jnp.maximum(count, 1.0) for count in counts]
    scales = [
        1.0 / jnp.maximum(jnp.sum(width_ref[0:1, m : m + 1], axis=1, keepdims=True).astype(F32), 1.0)
        for m in held
    ]

    row = iota((blocks, 1), 0).astype(F32)
    tile_of = jnp.floor((row + 0.5) * (1.0 / angles_here))
    wanted = (row - tile_of * angles_here) * tiles + tile_of + 1.0
    wanted = jnp.broadcast_to(wanted, (blocks, LANES))
    within = iota((8, slots), 1) & (slab - 1)

    wait_recv(IDS, ids_send, ids_recv)
    ids = jnp.broadcast_to(jnp.sum(ids_recv[...], axis=0), (8, slots))
    turns = [pltpu.roll(ids, n, 1) if n else ids for n in range(slab)]

    def match(ids_row):
        return jnp.where(wanted == jnp.broadcast_to(ids_row[0:1], (blocks, LANES)), 1.0, 0.0)

    begun = set()

    def unpack(columns, recv_ref):
        lead = recv_ref[...].reshape(slots, len(columns) * LANES)
        flat = dot(match(ids).astype(BF16), lead)
        for at, k in enumerate(columns):
            b = direct_blocks[k]
            grid_ref[:, b * LANES : (b + 1) * LANES] = flat[:, at * LANES : (at + 1) * LANES]
        sums = {}
        for at, k in enumerate(columns):
            held = sorted({cells[r, k][1] for r in range(cap, slab)})
            hot = []
            for b in held:
                ids_b = jnp.zeros((8, slots), F32)
                for r in range(cap, slab):
                    if cells[r, k][1] == b:
                        ids_b = jnp.where(within == r, turns[r - cells[r, k][0]], ids_b)
                hot.append(match(ids_b))
            part = dot(
                jnp.concatenate(hot, axis=0).astype(BF16), lead[:, at * LANES : (at + 1) * LANES]
            )
            for i, b in enumerate(held):
                piece = part[i * blocks : (i + 1) * blocks]
                sums[b] = sums[b] + piece if b in sums else piece
        for b, value in sums.items():
            at = b * LANES
            if b in begun:
                value = value + grid_ref[:, at : at + LANES]
            begun.add(b)
            grid_ref[:, at : at + LANES] = value

    def shift_of(tile):
        ahead = LANES - (offset_ref[:, tile : tile + 1] - tile * step_cols)
        return jnp.broadcast_to(ahead, (angles_here, LANES))

    lane_here = iota((angles_here, LANES), 1)

    def shifted(pieces, ahead, wanted_blocks):
        far = (ahead & LANES) != 0
        steps = [1 << n for n in range(LANES.bit_length() - 1)]
        masks = [(ahead & step) != 0 for step in steps]
        stay = lane_here < LANES - (ahead & (LANES - 1))
        blank = jnp.zeros((angles_here, LANES), F32)
        turned_at = {}
        for i in sorted({i + n for i in wanted_blocks for n in (0, 1)}):
            near_piece, far_piece = pieces.get(i), pieces.get(i + 1)
            if near_piece is None and far_piece is None:
                turned_at[i] = blank
                continue
            x = jnp.where(
                far,
                blank if far_piece is None else far_piece,
                blank if near_piece is None else near_piece,
            )
            for step, mask in zip(steps, masks):
                x = jnp.where(mask, pltpu.roll(x, LANES - step, 1), x)
            turned_at[i] = x
        return {i: jnp.where(stay, turned_at[i], turned_at[i + 1]) for i in wanted_blocks}

    def tile_block(tile, b):
        return grid_ref[tile * angles_here : (tile + 1) * angles_here, b * LANES : (b + 1) * LANES]

    def tile_blocks(tile, start, stop, at):
        return {at + b - start: tile_block(tile, b) for b in range(start, stop)}

    wait_recv(ROWS_A, rows_send_a, rows_recv_a)
    unpack(columns_a, rows_recv_a)
    shifts = [shift_of(t) for t in range(tiles)]
    flats_a = []
    for t in range(devices):
        if t == 0:
            value = [tile_block(t, b) for b in range(first, first + mine)]
        else:
            pieces = tile_blocks(t, first - 1, first + mine + 1, 0)
            value = shifted(pieces, shifts[t], range(mine))
            value = [value[i] for i in range(mine)]
        flat = -jnp.log(jnp.concatenate(value, axis=1))
        proj_ref[:, early[t][0] * LANES : (early[t][0] + mine) * LANES] = flat
        flats_a.append(flat)
    sums_a = module_sums(flats_a, inside_early)
    means_a = [sums_a[m] * scales_a[m] for m in held]
    for p in range(devices):
        cent_send_a[p] = less_mean(flats_a[p], means_a, inside_early, p)
    send_all(CENT_A, cent_send_a, cent_recv_a)
    cent_recv_a[me] = cent_send_a[me]

    wait_recv(ROWS_B, rows_send_b, rows_recv_b)
    unpack(columns_b, rows_recv_b)
    gap = back + first
    inverse_ramp = 1.0 / ramp_ref[...].astype(F32)
    left_at = step_cols // LANES - back - 1
    per_step = step_cols // LANES
    left_end = back - (-(tile_width - step_cols + JITTER) // LANES)
    right_start = back - 1 - (JITTER - 1) // LANES
    lane_float = lane_here.astype(F32)
    values = [tile_block(0, b) for b in range(first)]
    for g in range(1, tiles):
        left_pieces = tile_blocks(g - 1, left_at, chunks, 0)
        right_pieces = tile_blocks(g, 0, gap + 1 - back, back + 1)
        if g == 1:
            left = {i: left_pieces[i + 1] for i in range(left_end) if i + 1 in left_pieces}
        else:
            left = shifted(left_pieces, shifts[g - 1], range(left_end))
        if g == tiles - 1:
            right = {i: right_pieces[i + 1] for i in range(back, gap)}
        else:
            right = shifted(right_pieces, shifts[g], range(right_start, gap))
        ahead_left = lane_float + shifts[g - 1].astype(F32)
        ahead_right = lane_float + shifts[g].astype(F32)
        for i in range(gap):
            if i not in left or i not in right:
                values.append(left[i] if i in left else right[i])
                continue
            till = float(tile_width - (left_at + i) * LANES)
            since = float((i - back - 1) * LANES + 1)
            feather_left = (till - ahead_left) * inverse_ramp[:, g - 1 : g]
            feather_right = (ahead_right + since) * inverse_ramp[:, g : g + 1]
            feather_left = jnp.maximum(jnp.minimum(1.0, feather_left), 0.0)
            feather_right = jnp.maximum(jnp.minimum(1.0, feather_right), 0.0)
            blended = feather_left * left[i] + feather_right * right[i]
            values.append(blended / (feather_left + feather_right))
    values += [tile_block(tiles - 1, b) for b in range(first, chunks)]
    flats = []
    for p in range(devices):
        flat = -jnp.log(jnp.concatenate(values[p * mine : (p + 1) * mine], axis=1))
        flats.append(flat)
        for i, b in enumerate(late[p]):
            proj_ref[:, b * LANES : (b + 1) * LANES] = flat[:, i * LANES : (i + 1) * LANES]
    sums_b = module_sums(flats, inside_late)
    means = [(sums_a[m] + sums_b[m]) * scales[m] for m in held]
    lane_of = iota((angles_here, LANES), 1)
    own = (lane_of // mods) == iota((angles_here, LANES), 0)
    diff = jnp.zeros((angles_here, LANES), F32)
    for m in held:
        diff = jnp.where(lane_of % mods == m, means_a[m] - means[m], diff)
    diff_row = jnp.sum(jnp.where(own, diff, 0.0), axis=0, keepdims=True)
    diff_send[...] = diff_row
    for peer in peers:
        remote(DIFF, diff_send, diff_recv.at[me], me, peer).start()
    diff_recv[me] = diff_row
    for p in range(devices):
        cent_send_b[p] = less_mean(flats[p], means, inside_late, p)
    send_all(CENT_B, cent_send_b, cent_recv_b)
    cent_recv_b[me] = cent_send_b[me]

    shared_row = iota((fold * angles_here, fold * angles_here), 0)
    shared_col = iota((fold * angles_here, fold * angles_here), 1)
    same = (shared_row // angles_here) == (shared_col // angles_here)
    shared_table = jnp.where(same, SHARED / angles_here, 0.0).astype(BF16)
    for p in range(devices):
        for send_ref, block_list in ((cent_send_a, early[p]), (cent_send_b, late[p])):
            shared = dot(shared_table, send_ref[p])
            for i, b in enumerate(block_list):
                part, at = divmod(i, mine // 2)
                piece = shared[
                    part * angles_here : (part + 1) * angles_here, at * LANES : (at + 1) * LANES
                ]
                proj_ref[:, b * LANES : (b + 1) * LANES] = (
                    proj_ref[:, b * LANES : (b + 1) * LANES] - piece
                )
    clean_ref[:, 0:LANES] = jnp.zeros((angles_here, LANES), F32)
    clean_ref[:, W + LANES :] = jnp.zeros((angles_here, LANES), F32)
    for fetch in fetches[5:]:
        fetch.wait()

    k = iota((rows, 1), 0)
    count_of = jnp.where((k == 0) | (2 * k == angles), 1.0, 2.0)
    count_of = jnp.where(2 * k <= angles, count_of, 0.0)

    def magnitude_of(spectrum):
        return jnp.sqrt(spectrum[:rows] * spectrum[:rows] + spectrum[rows:] * spectrum[rows:])

    def summed(spectrum, inside):
        over_k = jnp.sum(magnitude_of(spectrum) * count_of, axis=0, keepdims=True)
        first_row = jnp.where(iota((8, half), 0) == 0, over_k, 0.0)
        return dot_nt(thirds(first_row), inside)

    member_own = [
        member_ref[
            :, pl.ds(pl.multiple_of(me * step_cols + first * LANES + part * half, LANES), half)
        ]
        for part in range(fold)
    ]
    member_own += [
        member_late_ref[me][:, part * half : (part + 1) * half] for part in range(fold)
    ]

    wait_recv(CENT_A, cent_send_a, cent_recv_a)
    signal_a = cent_recv_a[...].reshape(devices * fold * angles_here, half)
    sums = jnp.zeros((4 * 8, mods), F32)
    found = []
    for part in range(fold):
        spread = dot(fwd_ref[part], signal_a)
        found.append(spread[: 2 * rows] + spread[2 * rows :])
    for peer in peers:
        remote(DIFF, diff_send, diff_recv.at[peer], peer, peer).wait_recv()
    diffs = []
    for p in range(devices):
        spread = jnp.where(own, jnp.broadcast_to(diff_recv[p], (angles_here, LANES)), 0.0)
        diffs += [spread] * fold
    high, low = halves(jnp.concatenate(diffs, axis=0))
    shift = dot(fwd_ref[0], jnp.concatenate([high, low], axis=1))
    shift = shift[: 2 * rows] + shift[2 * rows :]
    high, low = halves(shift[:, :LANES] + shift[:, LANES:])
    shift = jnp.concatenate([high, low], axis=1)
    for part in range(fold):
        inside = jnp.concatenate([member_own[part]] * (2 * LANES // mods), axis=0)
        spectrum = found[part] + dot(shift, inside)
        spec_ref[part] = spectrum
        sums = sums + summed(spectrum, member_own[part])

    wait_recv(CENT_B, cent_send_b, cent_recv_b)
    signal_b = cent_recv_b[...].reshape(devices * fold * angles_here, half)
    for part in range(fold):
        spread = dot(fwd_ref[part], signal_b)
        spectrum = spread[: 2 * rows] + spread[2 * rows :]
        spec_ref[fold + part] = spectrum
        sums = sums + summed(spectrum, member_own[fold + part])
    level_send[...] = jnp.zeros_like(level_send)
    level_send[:, 0:mods] = sums[0:1] + sums[8:9] + sums[16:17]
    for peer in peers:
        remote(LEVEL, level_send, level_recv.at[me], me, peer).start()
    level_recv[me] = level_send[...]
    wait_send(IDS, ids_send, ids_recv)
    wait_send(ROWS_A, rows_send_a, rows_recv_a)
    wait_send(ROWS_B, rows_send_b, rows_recv_b)
    for peer in peers:
        remote(LEVEL, level_send, level_recv.at[peer], peer, peer).wait_recv()
    everything = jnp.sum(level_recv[...], axis=0)[:, 0:mods]
    level = SHRINK_SCALE * (everything / (angles * safe_wide) + EPSILON)
    level_parts = thirds(jnp.where(iota((8, mods), 0) == 0, level, 0.0))

    def inverse(at, part, signal):
        spread = dot(level_parts, member_own[at])
        level_col = spread[0:1] + spread[8:9] + spread[16:17]
        spectrum = spec_ref[at]
        magnitude = magnitude_of(spectrum)
        factor = jnp.maximum(magnitude - level_col, 0.0) / jnp.maximum(magnitude, level_col)
        shrunk = jnp.concatenate([spectrum[:rows] * factor, spectrum[rows:] * factor], axis=0)
        high, low = halves(shrunk)
        stripe = dot(inv_ref[part], jnp.concatenate([high, low, high, signal], axis=0))
        return stripe.reshape(devices, angles_here, half)

    both = [inverse(part, part, signal_a) for part in range(fold)]
    stripe_send_a[...] = jnp.concatenate(both, axis=1).astype(BF16)
    send_all(STRIPE_A, stripe_send_a, stripe_recv_a)
    both = [inverse(fold + part, part, signal_b) for part in range(fold)]
    stripe_send_b[...] = jnp.concatenate(both, axis=1).astype(BF16)
    send_all(STRIPE_B, stripe_send_b, stripe_recv_b)
    stripe_recv_a[me] = stripe_send_a[me]
    stripe_recv_b[me] = stripe_send_b[me]
    wait_send(CENT_A, cent_send_a, cent_recv_a)
    wait_send(CENT_B, cent_send_b, cent_recv_b)
    for peer in peers:
        remote(DIFF, diff_send, diff_recv.at[peer], peer, peer).wait_send()
        remote(LEVEL, level_send, level_recv.at[peer], peer, peer).wait_send()

    def clean(recv_ref, block_lists):
        for p in range(devices):
            rest = recv_ref[p].astype(F32)
            for i, b in enumerate(block_lists[p]):
                part, at = divmod(i, mine // 2)
                piece = rest[
                    part * angles_here : (part + 1) * angles_here, at * LANES : (at + 1) * LANES
                ]
                clean_ref[:, (b + 1) * LANES : (b + 2) * LANES] = (
                    proj_ref[:, b * LANES : (b + 1) * LANES] - piece
                )

    def ramp(block_list):
        near = jnp.concatenate(
            [clean_ref[:, b * LANES : (b + 3) * LANES] for b in block_list], axis=0
        )
        high, low = halves(near)
        done = dot(high, taps_ref[0]) + dot(low, taps_ref[0]) + dot(high, taps_ref[1])
        for i, b in enumerate(block_list):
            out_ref[:, b * LANES : (b + 1) * LANES] = done[i * angles_here : (i + 1) * angles_here]

    wait_recv(STRIPE_A, stripe_send_a, stripe_recv_a)
    clean(stripe_recv_a, early)
    inner = [b for run in early for b in run[1:-1]]
    outer = [b for b in range(W // LANES) if b not in set(inner)]
    for at in range(0, len(inner), 16):
        ramp(inner[at : at + 16])
    wait_recv(STRIPE_B, stripe_send_b, stripe_recv_b)
    clean(stripe_recv_b, late)
    for at in range(0, len(outer), 16):
        ramp(outer[at : at + 16])
    wait_send(STRIPE_A, stripe_send_a, stripe_recv_a)
    wait_send(STRIPE_B, stripe_send_b, stripe_recv_b)


def fast_call(cfg, plan, tables, args):
    devices, angles_here, tiles, tile_width, mods, fold = cfg
    cap, split, mine = plan[0], plan[1], plan[6]
    rows = freq_rows(devices * angles_here)
    half = mine * LANES // 2
    vmem = pl.BlockSpec(memory_space=pltpu.VMEM)
    message = pltpu.VMEM((devices, fold * angles_here, half), BF16)
    line = pltpu.VMEM((1, LANES), F32)
    lines = pltpu.VMEM((devices, 1, LANES), F32)
    rows_a = pltpu.VMEM((devices, 16, split * LANES), BF16)
    rows_b = pltpu.VMEM((devices, 16, (cap - split) * LANES), BF16)
    return pl.pallas_call(
        functools.partial(fast_kernel, cfg, plan),
        out_shape=pltpu.VMEM((angles_here, W), F32),
        in_specs=[pl.BlockSpec(memory_space=pl.ANY)] * 8,
        out_specs=vmem,
        scratch_shapes=[
            *[pltpu.VMEM(arg.shape, arg.dtype) for arg in args],
            rows_a,
            rows_a,
            rows_b,
            rows_b,
            lines,
            lines,
            pltpu.VMEM((angles_here * tiles, tile_width), F32),
            pltpu.VMEM((angles_here, W + 2 * LANES), F32),
            pltpu.VMEM((angles_here, W), F32),
            pltpu.VMEM((mods, W), BF16),
            pltpu.VMEM((devices, mods, mine * LANES), BF16),
            pltpu.VMEM((8, W), F32),
            pltpu.VMEM((devices, 8, mine * LANES), F32),
            message,
            message,
            message,
            message,
            line,
            lines,
            pltpu.VMEM((2 * fold, 2 * rows, half), F32),
            line,
            lines,
            message,
            message,
            message,
            message,
            *[pltpu.VMEM(table.shape, BF16) for table in tables],
            pltpu.SemaphoreType.DMA((8,)),
            pltpu.SemaphoreType.DMA((9, devices)),
            pltpu.SemaphoreType.DMA((9, devices)),
        ],
        compiler_params=pltpu.CompilerParams(
            collective_id=0, has_side_effects=True, vmem_limit_bytes=60 << 20
        ),
    )(*args, *[jnp.asarray(table) for table in tables])


def per_device(raw, block_dest, section_offset, ramp_length, module_width):
    devices = lax.axis_size("ang")
    blocks_here = raw.shape[0]
    tile_width = raw.shape[1]
    angles_here, tiles = section_offset.shape
    angles = angles_here * devices
    capacity = (blocks_here + devices - 1) // devices
    cols = W // devices
    fold = 2 if cols % (2 * LANES) == 0 else 1
    wire = BF16 if fold == 2 else F32
    mods = -(-module_width.shape[0] // 16) * 16
    half = cols // fold
    rows = freq_rows(angles)
    cfg = (devices, angles_here, tiles, tile_width, mods, fold)
    forward = forward_table(angles, devices, fold)
    inverse = inverse_table(angles, devices, fold)
    taps = ramp_table()
    plan = fast_plan(devices, angles_here, tiles, tile_width, mods, module_width.shape[0])
    if fold == 2 and plan:
        args = (
            raw,
            block_dest[None, :],
            section_offset,
            ramp_length[None, :],
            module_width[None, :],
        )
        return fast_call(cfg, plan, (forward, inverse, taps), args)
    vmem = pl.BlockSpec(memory_space=pltpu.VMEM)
    return pl.pallas_call(
        functools.partial(kernel, cfg),
        out_shape=pltpu.VMEM((angles_here, W), F32),
        in_specs=[vmem] * 5 + [pl.BlockSpec(memory_space=pl.ANY)] * 3,
        out_specs=vmem,
        scratch_shapes=[
            pltpu.VMEM((devices, 16, capacity * LANES), BF16),
            pltpu.VMEM((devices, 16, capacity * LANES), BF16),
            pltpu.VMEM((angles_here * tiles, tile_width), F32),
            pltpu.VMEM((angles_here, W + 2 * LANES), F32),
            pltpu.VMEM((angles_here, W + 2 * LANES), F32),
            pltpu.VMEM((angles_here, W), F32),
            pltpu.VMEM((devices, angles_here * fold, half), wire),
            pltpu.VMEM((devices, angles_here * fold, half), wire),
            pltpu.VMEM((fold, 2 * rows, half), F32),
            pltpu.VMEM((8, max(mods, LANES)), F32),
            pltpu.VMEM((devices, 8, max(mods, LANES)), F32),
            pltpu.VMEM((devices, angles_here * fold, half), wire),
            pltpu.VMEM((devices, angles_here * fold, half), wire),
            pltpu.VMEM((devices, 1, LANES), F32),
            pltpu.VMEM((devices, 1, LANES), F32),
            pltpu.VMEM(forward.shape, BF16),
            pltpu.VMEM(inverse.shape, BF16),
            pltpu.VMEM(taps.shape, BF16),
            pltpu.SemaphoreType.DMA((3,)),
            pltpu.SemaphoreType.DMA((5, devices)),
            pltpu.SemaphoreType.DMA((5, devices)),
        ],
        compiler_params=pltpu.CompilerParams(
            collective_id=0, has_side_effects=True, vmem_limit_bytes=60 << 20
        ),
    )(
        raw,
        block_dest[None, :],
        section_offset,
        ramp_length[None, :],
        module_width[None, :],
        jnp.asarray(forward),
        jnp.asarray(inverse),
        jnp.asarray(taps),
    )


def solution(mesh):
    in_specs = (P(("row", "ang"), None), P("ang"), P("ang", None), P(), P())
    out_specs = P(("row", "ang"), None)
    return jax.shard_map(
        per_device, mesh=mesh, in_specs=in_specs, out_specs=out_specs, check_vma=False
    )
```

```python
import functools
import math

import jax
import jax.numpy as jnp
import ml_dtypes
import numpy as np
from jax import lax
from jax.experimental import pallas as pl
from jax.experimental.pallas import tpu as pltpu
from jax.sharding import PartitionSpec as P

W = 16384
RAMP_HALF = 128
JITTER = 64
SHRINK_SCALE = 1.0
EPSILON = 1e-06
LANES = 128
SPAN = 2048
SHARED = 0.625

F32 = jnp.float32
BF16 = jnp.bfloat16


def split_np(table):
    high = table.astype(ml_dtypes.bfloat16)
    low = (table - high.astype(np.float64)).astype(ml_dtypes.bfloat16)
    return high, low


def freq_rows(angles):
    return -(-(angles // 2 + 1) // 8) * 8


def forward_table(angles, devices, fold):
    rows = freq_rows(angles)
    here = angles // devices
    k = np.arange(rows)[:, None]
    a = np.arange(angles)[None, :]
    phase = 2.0 * np.pi * ((k * a) % angles) / angles
    keep = (k <= angles // 2).astype(np.float64)
    table = np.concatenate([np.cos(phase) * keep, -np.sin(phase) * keep], axis=0)
    placed = np.zeros((fold, 2 * rows, devices, fold, here))
    for part in range(fold):
        placed[part, :, :, part, :] = table.reshape(2 * rows, devices, here)
    high, low = split_np(placed.reshape(fold, 2 * rows, devices * fold * here))
    return np.concatenate([high, low], axis=1)


def inverse_table(angles, devices, fold):
    rows = freq_rows(angles)
    k = np.arange(rows)[None, :]
    a = np.arange(angles)[:, None]
    phase = 2.0 * np.pi * ((k * a) % angles) / angles
    twice = np.where((k == 0) | (2 * k == angles), 1.0, 2.0) * (k <= angles // 2)
    weight = twice * np.exp(-np.minimum(k, angles - k) / (angles // 8)) / angles
    table = np.concatenate([np.cos(phase) * weight, -np.sin(phase) * weight], axis=1)
    high, low = split_np(table)
    table = np.concatenate([high, high, low], axis=1)
    if fold == 1:
        return table[None]
    here = angles // devices
    shared = np.kron(np.eye(devices), np.ones((here, here))) * (SHARED / here)
    placed = np.zeros((fold, angles, devices, fold, here))
    for part in range(fold):
        placed[part, :, :, part, :] = -shared.reshape(angles, devices, here)
    placed = placed.reshape(fold, angles, devices * fold * here).astype(ml_dtypes.bfloat16)
    return np.concatenate([np.broadcast_to(table, (fold,) + table.shape), placed], axis=2)


def ramp_table():
    i = np.arange(3 * LANES)[:, None] - LANES
    n = np.arange(LANES)[None, :] - i
    safe = np.where(n == 0, 1, n).astype(np.float64)
    taps = np.where(n % 2 != 0, -1.0 / (np.pi * np.pi * safe * safe), 0.0)
    taps = np.where(n == 0, 0.25, taps)
    taps = np.where(np.abs(n) <= RAMP_HALF, taps, 0.0)
    high, low = split_np(taps)
    return np.stack([high, low])


def dot(left, right):
    return jnp.dot(left, right, preferred_element_type=F32)


def dot_nt(left, right):
    return lax.dot_general(left, right, (((1,), (1,)), ((), ())), preferred_element_type=F32)


def halves(x):
    high = x.astype(BF16)
    return high, (x - high.astype(F32)).astype(BF16)


def thirds(x):
    high = x.astype(BF16).astype(F32)
    rest = x - high
    mid = rest.astype(BF16).astype(F32)
    low = rest - mid
    return jnp.concatenate([high, mid, low, jnp.zeros_like(x)], axis=0).astype(BF16)


def iota(shape, axis):
    return lax.broadcasted_iota(jnp.int32, shape, axis)


def loop(count, body):
    if count <= 8:
        for step in range(count):
            body(step)
    else:

        def run(step, carry):
            body(step)
            return carry

        lax.fori_loop(0, count, run, 0)


def kernel(
    cfg,
    raw_ref,
    dest_ref,
    offset_ref,
    ramp_ref,
    width_ref,
    fwd_hbm,
    inv_hbm,
    taps_hbm,
    out_ref,
    rows_send,
    rows_recv,
    grid_ref,
    sum_ref,
    weight_ref,
    proj_ref,
    cent_send,
    cent_recv,
    spec_ref,
    level_send,
    level_recv,
    stripe_send,
    stripe_recv,
    ids_send,
    ids_recv,
    fwd_ref,
    inv_ref,
    taps_ref,
    table_sem,
    send_sem,
    recv_sem,
):
    devices, angles_here, tiles, tile_width, mods, fold = cfg
    angles = devices * angles_here
    cols = W // devices
    half = cols // fold
    rows = freq_rows(angles)
    step_cols = (W - tile_width) // (tiles - 1)
    window = tile_width + 2 * LANES
    blocks = angles_here * tiles
    me = lax.axis_index("ang")

    def ring_at(hop):
        return lax.rem(me + hop, devices)

    def peer_at(hop):
        if devices & (devices - 1):
            return ring_at(hop)
        mask = devices - hop
        peer = 0
        bit = 1
        while bit < devices:
            peer = peer + bit * lax.rem(lax.div(me, bit) + mask // bit, 2)
            bit *= 2
        return peer

    barrier = pltpu.get_barrier_semaphore()

    def greet(step):
        pl.semaphore_signal(
            barrier,
            inc=1,
            device_id={"ang": peer_at(step + 1)},
            device_id_type=pl.DeviceIdType.MESH,
        )

    loop(devices - 1, greet)
    fetch_fwd = pltpu.make_async_copy(fwd_hbm, fwd_ref, table_sem.at[0])
    fetch_inv = pltpu.make_async_copy(inv_hbm, inv_ref, table_sem.at[1])
    fetch_taps = pltpu.make_async_copy(taps_hbm, taps_ref, table_sem.at[2])
    fetch_fwd.start()
    fetch_inv.start()
    fetch_taps.start()

    def remote(phase, src, dst, slot, peer):
        return pltpu.make_async_remote_copy(
            src_ref=src,
            dst_ref=dst,
            send_sem=send_sem.at[phase, peer],
            recv_sem=recv_sem.at[phase, slot],
            device_id={"ang": peer},
            device_id_type=pl.DeviceIdType.MESH,
        )

    def finish(phase, send_of, recv_of):
        def body(step):
            peer = peer_at(step + 1)
            copy = remote(phase, send_of(peer), recv_of(peer), peer, peer)
            copy.wait_recv()
            copy.wait_send()

        loop(devices - 1, body)

    cap = -(-blocks // devices)
    slab = 16
    chunks = tile_width // LANES
    extra = chunks - cap
    slots = devices * slab
    dest_row = dest_ref[...].astype(F32)
    source_row = iota((blocks, blocks), 1)
    source_col = iota((blocks, blocks), 0)

    def turned(values):
        return jnp.sum(jnp.where(source_row == source_col, values, 0.0), axis=1, keepdims=True)

    owner_row = jnp.floor((dest_row + 0.5) * (1.0 / blocks))
    owner_col = turned(owner_row)
    earlier = (owner_col == owner_row) & (source_col < source_row)
    rank_row = jnp.sum(jnp.where(earlier, 1.0, 0.0), axis=0, keepdims=True)
    rank_col = turned(rank_row)
    place_row = dest_row - owner_row * blocks + 1.0
    slot = iota((slots, 1), 0).astype(F32)

    def one_hot(left, right):
        return jnp.where(left == right, 1.0, 0.0).astype(BF16)

    direct = one_hot(slot, owner_row * slab + rank_row)
    packed = dot(direct, raw_ref[:, : cap * LANES])
    keeps = [
        jnp.where(jnp.broadcast_to(rank_col, (blocks, LANES)) == j, 1.0, 0.0).astype(BF16)
        for j in range(cap)
    ]
    for e in range(extra):
        chunk = raw_ref[:, (cap + e) * LANES : (cap + e + 1) * LANES]
        masked = jnp.concatenate([chunk * keep for keep in keeps], axis=1)
        packed = packed + dot(one_hot(slot, owner_row * slab + (cap + e)), masked)
    rows_send[...] = packed.astype(BF16).reshape(devices, slab, cap * LANES)
    group = LANES // slab
    groups = -(-devices // group)
    lane_at = iota((blocks, LANES), 1).astype(F32)
    first_lane = (lax.rem(me, group) * slab).astype(F32)
    at_rank = one_hot(lane_at, rank_col + first_lane)
    to_owner = jnp.where(iota((devices, blocks), 0).astype(F32) == owner_row, place_row, 0.0)
    ids_send[...] = dot(to_owner.astype(BF16), at_rank).reshape(devices, 1, LANES)

    pl.semaphore_wait(barrier, devices - 1)

    def send_rows(step):
        peer = peer_at(step + 1)
        remote(4, ids_send.at[peer], ids_recv.at[me], me, peer).start()
        remote(0, rows_send.at[peer], rows_recv.at[me], me, peer).start()

    loop(devices - 1, send_rows)
    rows_recv[me] = rows_send[me]
    ids_recv[me] = ids_send[me]
    finish(4, lambda p: ids_send.at[p], lambda p: ids_recv.at[p])
    finish(0, lambda p: rows_send.at[p], lambda p: rows_recv.at[p])

    ids = [
        jnp.sum(ids_recv[g * group : min((g + 1) * group, devices)], axis=0) for g in range(groups)
    ]
    ids = ids[0] if groups == 1 else jnp.concatenate(ids, axis=1)
    ids = jnp.broadcast_to(ids[:, :slots], (8, slots))
    row = iota((blocks, 1), 0).astype(F32)
    tile_of = jnp.floor((row + 0.5) * (1.0 / angles_here))
    wanted = (row - tile_of * angles_here) * tiles + tile_of + 1.0
    lead = rows_recv[...].reshape(slots, cap * LANES)
    grid_ref[:, : cap * LANES] = dot(one_hot(wanted, ids[0:1]), lead)
    if extra:
        within = iota((8, slots), 1) & (slab - 1)
        turns = [pltpu.roll(ids, n, 1) if n else ids for n in range(slab)]
        wanted_at = jnp.concatenate(
            [jnp.where(within[0:1] == cap + e, wanted, -1.0) for e in range(extra)], axis=0
        )
        rest = jnp.zeros((extra * blocks, LANES), F32)
        for j in range(cap):
            ids_j = jnp.zeros((8, slots), F32)
            for e in range(extra):
                ids_j = jnp.where(within == cap + e, turns[cap + e - j], ids_j)
            part = rows_recv[:, :, j * LANES : (j + 1) * LANES].reshape(slots, LANES)
            rest = rest + dot(one_hot(wanted_at, ids_j[0:1]), part)
        for e in range(extra):
            at = (cap + e) * LANES
            grid_ref[:, at : at + LANES] = rest[e * blocks : (e + 1) * blocks]

    fetch_fwd.wait()
    fetch_inv.wait()
    fetch_taps.wait()

    sum_ref[...] = jnp.zeros_like(sum_ref)
    weight_ref[...] = jnp.zeros_like(weight_ref)
    inverse_ramp = 1.0 / ramp_ref[...].astype(F32)
    lane = iota((angles_here, window), 1)
    for tile in range(tiles):
        base = tile * step_cols
        shift = jnp.broadcast_to(
            offset_ref[:, tile : tile + 1] - (base - LANES), (angles_here, window)
        )
        piece = jnp.concatenate(
            [
                grid_ref[tile * angles_here : (tile + 1) * angles_here, :],
                jnp.zeros((angles_here, 2 * LANES), F32),
            ],
            axis=1,
        )
        for bit in range(8):
            moved = pltpu.roll(piece, 1 << bit, 1)
            piece = jnp.where((shift & (1 << bit)) != 0, moved, piece)
        x = lane - shift
        edge = (jnp.minimum(x, tile_width - 1 - x) + 1).astype(F32)
        feather = jnp.minimum(1.0, edge * inverse_ramp[:, tile : tile + 1])
        feather = jnp.maximum(feather, 0.0)
        sum_ref[:, base : base + window] += feather * piece
        weight_ref[:, base : base + window] += feather

    wide = width_ref[...].astype(F32)
    upper = iota((mods, wide.shape[1]), 1)
    lower = iota((mods, wide.shape[1]), 0)
    bounds = jnp.sum(jnp.where(upper <= lower, wide, 0.0), axis=1, keepdims=True)
    starts = jnp.sum(jnp.where(upper < lower, wide, 0.0), axis=1, keepdims=True)
    on_diagonal = iota((mods, mods), 0) == iota((mods, mods), 1)
    safe_wide = jnp.sum(jnp.where(on_diagonal, bounds - starts, 0.0), axis=0, keepdims=True)
    safe_wide = jnp.maximum(safe_wide, 1.0)

    def member(first, count):
        c = (iota((mods, count), 1) + first).astype(F32)
        inside = (c >= starts) & (c < bounds)
        return jnp.where(inside, 1.0, 0.0).astype(BF16)

    def project(step, total):
        at = step * SPAN
        behind = at + LANES
        blended = sum_ref[:, pl.ds(behind, SPAN)] / weight_ref[:, pl.ds(behind, SPAN)]
        projection = -jnp.log(blended)
        proj_ref[:, pl.ds(at, SPAN)] = projection
        return total + dot_nt(thirds(projection), member(at, SPAN))

    total = jnp.zeros((4 * angles_here, mods), F32)
    for step in range(W // SPAN):
        total = project(step, total)

    def gather_thirds(stack):
        a = angles_here
        return stack[0:a] + stack[a : 2 * a] + stack[2 * a : 3 * a]

    mean = thirds(gather_thirds(total) / safe_wide)

    def centered_slab(owner):
        at = pl.multiple_of(owner * cols, LANES)
        flat = proj_ref[:, pl.ds(at, cols)] - gather_thirds(dot(mean, member(at, cols)))
        if fold > 1:
            flat = jnp.concatenate([flat[:, i * half : (i + 1) * half] for i in range(fold)], axis=0)
        return flat.astype(cent_send.dtype)

    def send_centered(step):
        peer = peer_at(step + 1)
        cent_send[peer] = centered_slab(peer)
        remote(1, cent_send.at[peer], cent_recv.at[me], me, peer).start()

    loop(devices - 1, send_centered)
    cent_send[me] = centered_slab(me)
    cent_recv[me] = cent_send[me]

    if fold > 1:
        shared_row = iota((fold * angles_here, fold * angles_here), 0)
        shared_col = iota((fold * angles_here, fold * angles_here), 1)
        same = (shared_row // angles_here) == (shared_col // angles_here)
        shared_table = jnp.where(same, SHARED / angles_here, 0.0).astype(BF16)

        def take_shared(owner):
            at = pl.multiple_of(owner * cols, LANES)
            shared = dot(shared_table, cent_send[owner])
            shared = jnp.concatenate(
                [shared[i * angles_here : (i + 1) * angles_here] for i in range(fold)], axis=1
            )
            proj_ref[:, pl.ds(at, cols)] = proj_ref[:, pl.ds(at, cols)] - shared

        loop(devices, take_shared)

    finish(1, lambda p: cent_send.at[p], lambda p: cent_recv.at[p])

    signal = cent_recv[...].reshape(devices * fold * angles_here, half).astype(BF16)
    k = iota((rows, 1), 0)
    count_of = jnp.where((k == 0) | (2 * k == angles), 1.0, 2.0)
    count_of = jnp.where(2 * k <= angles, count_of, 0.0)
    mine = pl.multiple_of(me * cols, LANES)
    sums = jnp.zeros((4 * 8, mods), F32)
    for part in range(fold):
        wide_spec = dot(fwd_ref[part], signal)
        spectrum = wide_spec[: 2 * rows] + wide_spec[2 * rows :]
        spec_ref[part] = spectrum
        magnitude = jnp.sqrt(
            spectrum[:rows] * spectrum[:rows] + spectrum[rows:] * spectrum[rows:]
        )
        over_k = jnp.sum(magnitude * count_of, axis=0, keepdims=True)
        first_row = jnp.where(iota((8, half), 0) == 0, over_k, 0.0)
        sums = sums + dot_nt(thirds(first_row), member(mine + part * half, half))
    level_send[...] = jnp.zeros_like(level_send)
    level_send[:, 0:mods] = sums[0:8] + sums[8:16] + sums[16:24]

    def send_level(step):
        peer = peer_at(step + 1)
        remote(2, level_send, level_recv.at[me], me, peer).start()

    loop(devices - 1, send_level)
    level_recv[me] = level_send[...]
    finish(2, lambda p: level_send, lambda p: level_recv.at[p])
    everything = jnp.sum(level_recv[...], axis=0)[:, 0:mods]
    level = SHRINK_SCALE * (everything / (angles * safe_wide) + EPSILON)
    level_parts = thirds(jnp.where(iota((8, mods), 0) == 0, level, 0.0))

    residual = []
    for part in range(fold):
        spread = dot(level_parts, member(mine + part * half, half))
        level_col = spread[0:1] + spread[8:9] + spread[16:17]
        spectrum = spec_ref[part]
        magnitude = jnp.sqrt(
            spectrum[:rows] * spectrum[:rows] + spectrum[rows:] * spectrum[rows:]
        )
        factor = jnp.maximum(magnitude - level_col, 0.0) / jnp.maximum(magnitude, level_col)
        shrunk = jnp.concatenate([spectrum[:rows] * factor, spectrum[rows:] * factor], axis=0)
        high, low = halves(shrunk)
        parts = [high, low, high] + ([signal] if fold > 1 else [])
        stripe = dot(inv_ref[part], jnp.concatenate(parts, axis=0))
        residual.append(stripe.reshape(devices, angles_here, half))
    stripe_send[...] = jnp.concatenate(residual, axis=1).astype(stripe_send.dtype)

    def send_stripe(step):
        peer = ring_at(step + 1)
        remote(3, stripe_send.at[peer], stripe_recv.at[me], me, peer).start()

    loop(devices - 1, send_stripe)
    stripe_recv[me] = stripe_send[me]

    sum_ref[:, 0:LANES] = jnp.zeros((angles_here, LANES), F32)
    sum_ref[:, W + LANES :] = jnp.zeros((angles_here, LANES), F32)
    lane_blocks = cols // LANES

    def clean(owner):
        at = pl.multiple_of(owner * cols, LANES)
        behind = pl.multiple_of(owner * cols + LANES, LANES)
        rest = stripe_recv[owner].astype(F32)
        rest = jnp.concatenate(
            [rest[i * angles_here : (i + 1) * angles_here] for i in range(fold)], axis=1
        )
        sum_ref[:, pl.ds(behind, cols)] = proj_ref[:, pl.ds(at, cols)] - rest

    def ramp(group):
        at = pl.multiple_of(group * cols, LANES)
        flat = sum_ref[:, pl.ds(at, cols + 2 * LANES)]
        stack = jnp.concatenate(
            [flat[:, b * LANES : (b + 1) * LANES] for b in range(lane_blocks + 2)], axis=0
        )
        n = lane_blocks * angles_here
        near = jnp.concatenate(
            [stack[s * angles_here : s * angles_here + n] for s in range(3)], axis=1
        )
        high, low = halves(near)
        done = dot(high, taps_ref[0]) + dot(low, taps_ref[0]) + dot(high, taps_ref[1])
        out_ref[:, pl.ds(at, cols)] = jnp.concatenate(
            [done[b * angles_here : (b + 1) * angles_here] for b in range(lane_blocks)], axis=1
        )

    clean(me)

    def below(hop):
        return lax.rem(me + devices - hop, devices)

    def take(hop):
        owner = below(hop)
        remote(3, stripe_send.at[owner], stripe_recv.at[owner], owner, owner).wait_recv()
        clean(owner)

    take(1)

    def advance(step):
        take(step + 2)
        ramp(below(step + 1))

    loop(devices - 2, advance)
    ramp(below(devices - 1))
    ramp(me)

    def sent(step):
        peer = ring_at(step + 1)
        remote(3, stripe_send.at[peer], stripe_recv.at[peer], peer, peer).wait_send()

    loop(devices - 1, sent)


def pack_plan(cap, chunks, first, need):
    split = next(
        (n for n in range(1, cap) if n + (chunks - cap) * n // cap >= need), 0
    )
    run = list(range(first, first + need))
    others = [b for b in range(chunks) if b not in run]
    direct = run[:split] + others[: cap - split]
    cells = {}
    n = 0
    early = (chunks - cap) * split
    for block in run[split:] + others[cap - split :]:
        for rank in range(cap):
            if n < early:
                cells[cap + n // split, n % split] = (rank, block)
            else:
                late = n - early
                cells[cap + late // (cap - split), split + late % (cap - split)] = (rank, block)
            n += 1
    return split, direct, cells


def fast_plan(devices, angles_here, tiles, tile_width, mods, modules):
    cols = W // devices
    step_cols = (W - tile_width) // (tiles - 1)
    cap = -(-angles_here * tiles // devices)
    chunks = tile_width // LANES
    if cols % (4 * LANES) or step_cols % LANES or tile_width % LANES:
        return None
    mine = cols // (2 * LANES)
    per_step = step_cols // LANES
    first = -(-(tile_width - step_cols + JITTER) // LANES) + 1
    back = per_step - first - mine
    fits = (
        tiles == devices + 1
        and angles_here == 8
        and angles_here * mods == LANES
        and modules <= 8
        and chunks == 16
        and devices * chunks == LANES
        and 1 < cap < chunks
        and back >= 1
        and tile_width < 2 * step_cols - 2 * JITTER
        and (first + mine) * LANES <= step_cols - JITTER
    )
    if not fits:
        return None
    split, direct, cells = pack_plan(cap, chunks, first - 1, mine + 2)
    if not split:
        return None
    alone = {t * per_step + first + i for t in range(tiles) for i in range(mine)}
    early, late = [], []
    for p in range(devices):
        window = range(2 * p * mine, 2 * (p + 1) * mine)
        early.append([b for b in window if b in alone][:mine])
        late.append([b for b in window if b not in early[p]])
    if any(len(run) != mine for run in early):
        return None
    reach = -(-2 * W // modules // cols)
    return cap, split, direct, cells, first, back, mine, early, late, reach


def fast_kernel(
    cfg,
    plan,
    raw_hbm,
    dest_hbm,
    offset_hbm,
    ramp_hbm,
    width_hbm,
    fwd_hbm,
    inv_hbm,
    taps_hbm,
    out_ref,
    raw_ref,
    dest_ref,
    offset_ref,
    ramp_ref,
    width_ref,
    rows_send_a,
    rows_recv_a,
    rows_send_b,
    rows_recv_b,
    ids_send,
    ids_recv,
    grid_ref,
    clean_ref,
    proj_ref,
    member_ref,
    member_own_ref,
    inside_ref,
    inside_own_ref,
    cent_send_a,
    cent_recv_a,
    cent_send_b,
    cent_recv_b,
    diff_send,
    diff_recv,
    spec_ref,
    level_send,
    level_recv,
    stripe_send_a,
    stripe_recv_a,
    stripe_send_b,
    stripe_recv_b,
    fwd_ref,
    inv_ref,
    taps_ref,
    table_sem,
    send_sem,
    recv_sem,
):
    devices, angles_here, tiles, tile_width, mods, fold = cfg
    cap, split, direct_blocks, cells, first, back, mine, early, late, reach = plan
    angles = devices * angles_here
    rows = freq_rows(angles)
    step_cols = (W - tile_width) // (tiles - 1)
    blocks = angles_here * tiles
    chunks = tile_width // LANES
    slab = chunks
    slots = devices * slab
    width = mine * LANES
    half = width // 2
    me = lax.axis_index("ang")
    ROWS_A, ROWS_B, IDS, CENT_A, CENT_B, DIFF, LEVEL, STRIPE_A, STRIPE_B = range(9)

    def peer_at(hop):
        mask = devices - hop
        peer = 0
        bit = 1
        while bit < devices:
            peer = peer + bit * lax.rem(lax.div(me, bit) + mask // bit, 2)
            bit *= 2
        return peer

    peers = [peer_at(hop) for hop in range(1, devices)]
    barrier = pltpu.get_barrier_semaphore()
    for peer in peers:
        pl.semaphore_signal(
            barrier, inc=1, device_id={"ang": peer}, device_id_type=pl.DeviceIdType.MESH
        )
    fetched = [
        (dest_hbm, dest_ref),
        (raw_hbm, raw_ref),
        (width_hbm, width_ref),
        (offset_hbm, offset_ref),
        (ramp_hbm, ramp_ref),
        (fwd_hbm, fwd_ref),
        (inv_hbm, inv_ref),
        (taps_hbm, taps_ref),
    ]
    fetches = [
        pltpu.make_async_copy(src, dst, table_sem.at[i]) for i, (src, dst) in enumerate(fetched)
    ]
    for fetch in fetches:
        fetch.start()

    def remote(phase, src, dst, slot, peer):
        return pltpu.make_async_remote_copy(
            src_ref=src,
            dst_ref=dst,
            send_sem=send_sem.at[phase, peer],
            recv_sem=recv_sem.at[phase, slot],
            device_id={"ang": peer},
            device_id_type=pl.DeviceIdType.MESH,
        )

    def send_all(phase, send_ref, recv_ref):
        for peer in peers:
            remote(phase, send_ref.at[peer], recv_ref.at[me], me, peer).start()

    def wait_recv(phase, send_ref, recv_ref):
        for peer in peers:
            remote(phase, send_ref.at[peer], recv_ref.at[peer], peer, peer).wait_recv()

    def wait_send(phase, send_ref, recv_ref):
        for peer in peers:
            remote(phase, send_ref.at[peer], recv_ref.at[peer], peer, peer).wait_send()

    fetches[0].wait()
    dest_row = dest_ref[...].astype(F32)
    source_row = iota((blocks, blocks), 1)
    source_col = iota((blocks, blocks), 0)

    def turned(values):
        return jnp.sum(jnp.where(source_row == source_col, values, 0.0), axis=1, keepdims=True)

    owner_row = jnp.floor((dest_row + 0.5) * (1.0 / blocks))
    owner_col = turned(owner_row)
    earlier = (owner_col == owner_row) & (source_col < source_row)
    rank_row = jnp.sum(jnp.where(earlier, 1.0, 0.0), axis=0, keepdims=True)
    rank_col = turned(rank_row)
    place_row = dest_row - owner_row * blocks + 1.0
    slot = iota((slots, 1), 0).astype(F32)

    def one_hot(left, right):
        return jnp.where(left == right, 1.0, 0.0).astype(BF16)

    direct = one_hot(slot, owner_row * slab + rank_row)
    keeps = [
        jnp.where(jnp.broadcast_to(rank_col, (blocks, LANES)) == j, 1.0, 0.0).astype(BF16)
        for j in range(cap)
    ]

    def lane_block(b):
        return raw_ref[:, b * LANES : (b + 1) * LANES]

    def pack(columns):
        packed = dot(direct, jnp.concatenate([lane_block(direct_blocks[k]) for k in columns], axis=1))
        for r in range(cap, slab):
            masked = jnp.concatenate(
                [lane_block(cells[r, k][1]) * keeps[cells[r, k][0]] for k in columns], axis=1
            )
            packed = packed + dot(one_hot(slot, owner_row * slab + r), masked)
        return packed.astype(BF16).reshape(devices, slab, len(columns) * LANES)

    columns_a = range(split)
    columns_b = range(split, cap)
    lane_at = iota((blocks, LANES), 1).astype(F32)
    first_lane = (me * slab).astype(F32)
    at_rank = one_hot(lane_at, rank_col + first_lane)
    to_owner = jnp.where(iota((devices, blocks), 0).astype(F32) == owner_row, place_row, 0.0)
    ids_send[...] = dot(to_owner.astype(BF16), at_rank).reshape(devices, 1, LANES)
    fetches[1].wait()
    rows_send_a[...] = pack(columns_a)

    pl.semaphore_wait(barrier, devices - 1)

    send_all(IDS, ids_send, ids_recv)
    send_all(ROWS_A, rows_send_a, rows_recv_a)
    rows_send_b[...] = pack(columns_b)
    send_all(ROWS_B, rows_send_b, rows_recv_b)
    rows_recv_a[me] = rows_send_a[me]
    rows_recv_b[me] = rows_send_b[me]
    ids_recv[me] = ids_send[me]

    for fetch in fetches[2:5]:
        fetch.wait()
    wide = width_ref[...].astype(F32)
    upper = iota((mods, wide.shape[1]), 1)
    lower = iota((mods, wide.shape[1]), 0)
    bounds = jnp.sum(jnp.where(upper <= lower, wide, 0.0), axis=1, keepdims=True)
    starts = jnp.sum(jnp.where(upper < lower, wide, 0.0), axis=1, keepdims=True)
    on_diagonal = iota((mods, mods), 0) == iota((mods, mods), 1)
    safe_wide = jnp.sum(jnp.where(on_diagonal, bounds - starts, 0.0), axis=0, keepdims=True)
    safe_wide = jnp.maximum(safe_wide, 1.0)
    bounds = jnp.broadcast_to(bounds, (mods, LANES))
    starts = jnp.broadcast_to(starts, (mods, LANES))
    lane = iota((mods, LANES), 1).astype(F32)
    for b in range(W // LANES):
        c = lane + float(b * LANES)
        inside = (c >= starts) & (c < bounds)
        inside = jnp.where(inside, 1.0, 0.0)
        member_ref[:, b * LANES : (b + 1) * LANES] = inside.astype(BF16)
        inside_ref[:, b * LANES : (b + 1) * LANES] = inside[0:8]
    for p in range(devices):
        for i, b in enumerate(early[p] + late[p]):
            at = i * LANES
            member_own_ref[p, :, at : at + LANES] = member_ref[:, b * LANES : (b + 1) * LANES]
            inside_own_ref[p, :, at : at + LANES] = inside_ref[:, b * LANES : (b + 1) * LANES]
    held = range(width_ref.shape[1])

    def inside_early(m, p):
        return inside_own_ref[p, m : m + 1, :width]

    def inside_late(m, p):
        return inside_own_ref[p, m : m + 1, width:]

    def narrowed(x):
        pieces = [x[:, i * LANES : (i + 1) * LANES] for i in range(mine)]
        while len(pieces) > 1:
            odd = pieces[len(pieces) // 2 * 2 :]
            pieces = [x + y for x, y in zip(pieces[::2], pieces[1::2])] + odd
        return pieces[0]

    def module_sums(flats, inside_of):
        sums = []
        for m in held:
            total = narrowed(flats[0] * inside_of(m, 0))
            for p in range(1, devices):
                total = total + narrowed(flats[p] * inside_of(m, p))
            sums.append(jnp.sum(total, axis=1, keepdims=True))
        return sums

    def less_mean(flat, means, inside_of, p):
        for m in held:
            flat = flat - means[m] * inside_of(m, p)
        flat = jnp.concatenate([flat[:, :half], flat[:, half:]], axis=0)
        return flat.astype(BF16)

    blank_row = jnp.ones((1, width), F32)
    counts = module_sums([blank_row] * devices, inside_early)
    scales_a = [1.0 / jnp.maximum(count, 1.0) for count in counts]
    scales = [
        1.0 / jnp.maximum(jnp.sum(width_ref[0:1, m : m + 1], axis=1, keepdims=True).astype(F32), 1.0)
        for m in held
    ]

    row = iota((blocks, 1), 0).astype(F32)
    tile_of = jnp.floor((row + 0.5) * (1.0 / angles_here))
    wanted = (row - tile_of * angles_here) * tiles + tile_of + 1.0
    wanted = jnp.broadcast_to(wanted, (blocks, LANES))
    within = iota((8, slots), 1) & (slab - 1)

    wait_recv(IDS, ids_send, ids_recv)
    ids = jnp.broadcast_to(jnp.sum(ids_recv[...], axis=0), (8, slots))
    turns = [pltpu.roll(ids, n, 1) if n else ids for n in range(slab)]

    def match(ids_row):
        return jnp.where(wanted == jnp.broadcast_to(ids_row[0:1], (blocks, LANES)), 1.0, 0.0)

    begun = set()

    def unpack(columns, recv_ref):
        lead = recv_ref[...].reshape(slots, len(columns) * LANES)
        flat = dot(match(ids).astype(BF16), lead)
        for at, k in enumerate(columns):
            b = direct_blocks[k]
            grid_ref[:, b * LANES : (b + 1) * LANES] = flat[:, at * LANES : (at + 1) * LANES]
        sums = {}
        for at, k in enumerate(columns):
            held = sorted({cells[r, k][1] for r in range(cap, slab)})
            hot = []
            for b in held:
                ids_b = jnp.zeros((8, slots), F32)
                for r in range(cap, slab):
                    if cells[r, k][1] == b:
                        ids_b = jnp.where(within == r, turns[r - cells[r, k][0]], ids_b)
                hot.append(match(ids_b))
            part = dot(
                jnp.concatenate(hot, axis=0).astype(BF16), lead[:, at * LANES : (at + 1) * LANES]
            )
            for i, b in enumerate(held):
                piece = part[i * blocks : (i + 1) * blocks]
                sums[b] = sums[b] + piece if b in sums else piece
        for b, value in sums.items():
            at = b * LANES
            if b in begun:
                value = value + grid_ref[:, at : at + LANES]
            begun.add(b)
            grid_ref[:, at : at + LANES] = value

    def shift_of(tile):
        ahead = LANES - (offset_ref[:, tile : tile + 1] - tile * step_cols)
        return jnp.broadcast_to(ahead, (angles_here, LANES))

    lane_here = iota((angles_here, LANES), 1)

    def shifted(pieces, ahead, wanted_blocks):
        far = (ahead & LANES) != 0
        steps = [1 << n for n in range(LANES.bit_length() - 1)]
        masks = [(ahead & step) != 0 for step in steps]
        stay = lane_here < LANES - (ahead & (LANES - 1))
        blank = jnp.zeros((angles_here, LANES), F32)
        turned_at = {}
        for i in sorted({i + n for i in wanted_blocks for n in (0, 1)}):
            near_piece, far_piece = pieces.get(i), pieces.get(i + 1)
            if near_piece is None and far_piece is None:
                turned_at[i] = blank
                continue
            x = jnp.where(
                far,
                blank if far_piece is None else far_piece,
                blank if near_piece is None else near_piece,
            )
            for step, mask in zip(steps, masks):
                x = jnp.where(mask, pltpu.roll(x, LANES - step, 1), x)
            turned_at[i] = x
        return {i: jnp.where(stay, turned_at[i], turned_at[i + 1]) for i in wanted_blocks}

    def tile_block(tile, b):
        return grid_ref[tile * angles_here : (tile + 1) * angles_here, b * LANES : (b + 1) * LANES]

    def tile_blocks(tile, start, stop, at):
        return {at + b - start: tile_block(tile, b) for b in range(start, stop)}

    wait_recv(ROWS_A, rows_send_a, rows_recv_a)
    unpack(columns_a, rows_recv_a)
    shifts = [shift_of(t) for t in range(tiles)]
    values = {}
    for t in range(tiles):
        if t in (0, tiles - 1):
            value = {i: tile_block(t, first + i) for i in range(mine)}
        else:
            pieces = tile_blocks(t, first - 1, first + mine + 1, 0)
            value = shifted(pieces, shifts[t], range(mine))
        for i in range(mine):
            values[t * (step_cols // LANES) + first + i] = value[i]

    def project(block_lists):
        flats = []
        for block_list in block_lists:
            flat = -jnp.log(jnp.concatenate([values[b] for b in block_list], axis=1))
            flats.append(flat)
            for i, b in enumerate(block_list):
                proj_ref[:, b * LANES : (b + 1) * LANES] = flat[:, i * LANES : (i + 1) * LANES]
        return flats

    flats_a = project(early)
    sums_a = module_sums(flats_a, inside_early)
    means_a = [sums_a[m] * scales_a[m] for m in held]
    for p in range(devices):
        cent_send_a[p] = less_mean(flats_a[p], means_a, inside_early, p)
    level_recv[...] = jnp.zeros_like(level_recv)
    send_all(CENT_A, cent_send_a, cent_recv_a)
    cent_recv_a[me] = cent_send_a[me]

    wait_recv(ROWS_B, rows_send_b, rows_recv_b)
    unpack(columns_b, rows_recv_b)
    gap = back + first
    inverse_ramp = 1.0 / ramp_ref[...].astype(F32)
    left_at = step_cols // LANES - back - 1
    per_step = step_cols // LANES
    left_end = back - (-(tile_width - step_cols + JITTER) // LANES)
    right_start = back - 1 - (JITTER - 1) // LANES
    lane_float = lane_here.astype(F32)
    for b in range(first):
        values[b] = tile_block(0, b)
    for g in range(1, tiles):
        left_pieces = tile_blocks(g - 1, left_at, chunks, 0)
        right_pieces = tile_blocks(g, 0, gap + 1 - back, back + 1)
        if g == 1:
            left = {i: left_pieces[i + 1] for i in range(left_end) if i + 1 in left_pieces}
        else:
            left = shifted(left_pieces, shifts[g - 1], range(left_end))
        if g == tiles - 1:
            right = {i: right_pieces[i + 1] for i in range(back, gap)}
        else:
            right = shifted(right_pieces, shifts[g], range(right_start, gap))
        ahead_left = lane_float + shifts[g - 1].astype(F32)
        ahead_right = lane_float + shifts[g].astype(F32)
        for i in range(gap):
            if i not in left or i not in right:
                values[g * per_step - back + i] = left[i] if i in left else right[i]
                continue
            till = float(tile_width - (left_at + i) * LANES)
            since = float((i - back - 1) * LANES + 1)
            feather_left = (till - ahead_left) * inverse_ramp[:, g - 1 : g]
            feather_right = (ahead_right + since) * inverse_ramp[:, g : g + 1]
            feather_left = jnp.maximum(jnp.minimum(1.0, feather_left), 0.0)
            feather_right = jnp.maximum(jnp.minimum(1.0, feather_right), 0.0)
            blended = feather_left * left[i] + feather_right * right[i]
            values[g * per_step - back + i] = blended / (feather_left + feather_right)
    for b in range(first + mine, chunks):
        values[(tiles - 1) * per_step + b] = tile_block(tiles - 1, b)
    flats = project(late)
    sums_b = module_sums(flats, inside_late)
    means = [(sums_a[m] + sums_b[m]) * scales[m] for m in held]
    lane_of = iota((angles_here, LANES), 1)
    own = (lane_of // mods) == iota((angles_here, LANES), 0)
    diff = jnp.zeros((angles_here, LANES), F32)
    for m in held:
        diff = jnp.where(lane_of % mods == m, means_a[m] - means[m], diff)
    diff_row = jnp.sum(jnp.where(own, diff, 0.0), axis=0, keepdims=True)
    diff_send[...] = diff_row
    for peer in peers:
        remote(DIFF, diff_send, diff_recv.at[me], me, peer).start()
    diff_recv[me] = diff_row
    for p in range(devices):
        cent_send_b[p] = less_mean(flats[p], means, inside_late, p)
    send_all(CENT_B, cent_send_b, cent_recv_b)
    cent_recv_b[me] = cent_send_b[me]

    shared_row = iota((fold * angles_here, fold * angles_here), 0)
    shared_col = iota((fold * angles_here, fold * angles_here), 1)
    same = (shared_row // angles_here) == (shared_col // angles_here)
    shared_table = jnp.where(same, SHARED / angles_here, 0.0).astype(BF16)
    for p in range(devices):
        for send_ref, block_list in ((cent_send_a, early[p]), (cent_send_b, late[p])):
            shared = dot(shared_table, send_ref[p])
            for i, b in enumerate(block_list):
                part, at = divmod(i, mine // 2)
                piece = shared[
                    part * angles_here : (part + 1) * angles_here, at * LANES : (at + 1) * LANES
                ]
                proj_ref[:, b * LANES : (b + 1) * LANES] = (
                    proj_ref[:, b * LANES : (b + 1) * LANES] - piece
                )
    clean_ref[:, 0:LANES] = jnp.zeros((angles_here, LANES), F32)
    clean_ref[:, W + LANES :] = jnp.zeros((angles_here, LANES), F32)
    for fetch in fetches[5:]:
        fetch.wait()

    k = iota((rows, 1), 0)
    count_of = jnp.where((k == 0) | (2 * k == angles), 1.0, 2.0)
    count_of = jnp.where(2 * k <= angles, count_of, 0.0)

    def magnitude_of(spectrum):
        return jnp.sqrt(spectrum[:rows] * spectrum[:rows] + spectrum[rows:] * spectrum[rows:])

    def summed(spectrum, inside):
        over_k = jnp.sum(magnitude_of(spectrum) * count_of, axis=0, keepdims=True)
        first_row = jnp.where(iota((8, half), 0) == 0, over_k, 0.0)
        return dot_nt(thirds(first_row), inside)

    member_own = [
        member_own_ref[me][:, i * half : (i + 1) * half] for i in range(2 * fold)
    ]

    wait_recv(CENT_A, cent_send_a, cent_recv_a)
    signal_a = cent_recv_a[...].reshape(devices * fold * angles_here, half)
    sums = jnp.zeros((4 * 8, mods), F32)
    found = []
    for part in range(fold):
        spread = dot(fwd_ref[part], signal_a)
        found.append(spread[: 2 * rows] + spread[2 * rows :])
    for peer in peers:
        remote(DIFF, diff_send, diff_recv.at[peer], peer, peer).wait_recv()
    diffs = []
    for p in range(devices):
        spread = jnp.where(own, jnp.broadcast_to(diff_recv[p], (angles_here, LANES)), 0.0)
        diffs += [spread] * fold
    high, low = halves(jnp.concatenate(diffs, axis=0))
    shift = dot(fwd_ref[0], jnp.concatenate([high, low], axis=1))
    shift = shift[: 2 * rows] + shift[2 * rows :]
    high, low = halves(shift[:, :LANES] + shift[:, LANES:])
    shift = jnp.concatenate([high, low], axis=1)
    for part in range(fold):
        inside = jnp.concatenate([member_own[part]] * (2 * LANES // mods), axis=0)
        spectrum = found[part] + dot(shift, inside)
        spec_ref[part] = spectrum
        sums = sums + summed(spectrum, member_own[part])

    wait_recv(CENT_B, cent_send_b, cent_recv_b)
    signal_b = cent_recv_b[...].reshape(devices * fold * angles_here, half)
    for part in range(fold):
        spread = dot(fwd_ref[part], signal_b)
        spectrum = spread[: 2 * rows] + spread[2 * rows :]
        spec_ref[fold + part] = spectrum
        sums = sums + summed(spectrum, member_own[fold + part])
    level_send[...] = jnp.zeros_like(level_send)
    level_send[:, 0:mods] = sums[0:1] + sums[8:9] + sums[16:17]
    hops = [hop for n in range(reach, 0, -1) for hop in (n, -n)]

    def near(hop, body):
        inside = me + hop < devices if hop > 0 else me + hop >= 0

        @pl.when(inside)
        def _():
            body(me + hop)

    for hop in hops:
        near(hop, lambda peer: remote(LEVEL, level_send, level_recv.at[me], me, peer).start())
    level_recv[me] = level_send[...]
    wait_send(IDS, ids_send, ids_recv)
    wait_send(ROWS_A, rows_send_a, rows_recv_a)
    wait_send(ROWS_B, rows_send_b, rows_recv_b)
    for hop in hops:
        near(
            hop,
            lambda peer: remote(LEVEL, level_send, level_recv.at[peer], peer, peer).wait_recv(),
        )
    everything = jnp.sum(level_recv[...], axis=0)[:, 0:mods]
    level = SHRINK_SCALE * (everything / (angles * safe_wide) + EPSILON)
    level_parts = thirds(jnp.where(iota((8, mods), 0) == 0, level, 0.0))

    def inverse(at, part, signal):
        spread = dot(level_parts, member_own[at])
        level_col = spread[0:1] + spread[8:9] + spread[16:17]
        spectrum = spec_ref[at]
        magnitude = magnitude_of(spectrum)
        factor = jnp.maximum(magnitude - level_col, 0.0) / jnp.maximum(magnitude, level_col)
        shrunk = jnp.concatenate([spectrum[:rows] * factor, spectrum[rows:] * factor], axis=0)
        high, low = halves(shrunk)
        stripe = dot(inv_ref[part], jnp.concatenate([high, low, high, signal], axis=0))
        return stripe.reshape(devices, angles_here, half)

    both = [inverse(part, part, signal_a) for part in range(fold)]
    stripe_send_a[...] = jnp.concatenate(both, axis=1).astype(BF16)
    send_all(STRIPE_A, stripe_send_a, stripe_recv_a)
    both = [inverse(fold + part, part, signal_b) for part in range(fold)]
    stripe_send_b[...] = jnp.concatenate(both, axis=1).astype(BF16)
    send_all(STRIPE_B, stripe_send_b, stripe_recv_b)
    stripe_recv_a[me] = stripe_send_a[me]
    stripe_recv_b[me] = stripe_send_b[me]
    wait_send(CENT_A, cent_send_a, cent_recv_a)
    wait_send(CENT_B, cent_send_b, cent_recv_b)
    for peer in peers:
        remote(DIFF, diff_send, diff_recv.at[peer], peer, peer).wait_send()
    for hop in hops:
        near(
            hop,
            lambda peer: remote(LEVEL, level_send, level_recv.at[peer], peer, peer).wait_send(),
        )

    def clean(recv_ref, block_lists):
        for p in range(devices):
            rest = recv_ref[p].astype(F32)
            for i, b in enumerate(block_lists[p]):
                part, at = divmod(i, mine // 2)
                piece = rest[
                    part * angles_here : (part + 1) * angles_here, at * LANES : (at + 1) * LANES
                ]
                clean_ref[:, (b + 1) * LANES : (b + 2) * LANES] = (
                    proj_ref[:, b * LANES : (b + 1) * LANES] - piece
                )

    def ramp(block_list):
        near = jnp.concatenate(
            [clean_ref[:, b * LANES : (b + 3) * LANES] for b in block_list], axis=0
        )
        high, low = halves(near)
        done = dot(high, taps_ref[0]) + dot(low, taps_ref[0]) + dot(high, taps_ref[1])
        for i, b in enumerate(block_list):
            out_ref[:, b * LANES : (b + 1) * LANES] = done[i * angles_here : (i + 1) * angles_here]

    wait_recv(STRIPE_A, stripe_send_a, stripe_recv_a)
    clean(stripe_recv_a, early)
    found_early = {b for run in early for b in run}
    inner = [b for b in sorted(found_early) if b - 1 in found_early and b + 1 in found_early]
    outer = [b for b in range(W // LANES) if b not in set(inner)]
    for at in range(0, len(inner), 16):
        ramp(inner[at : at + 16])
    wait_recv(STRIPE_B, stripe_send_b, stripe_recv_b)
    clean(stripe_recv_b, late)
    for at in range(0, len(outer), 16):
        ramp(outer[at : at + 16])
    wait_send(STRIPE_A, stripe_send_a, stripe_recv_a)
    wait_send(STRIPE_B, stripe_send_b, stripe_recv_b)


def fast_call(cfg, plan, tables, args):
    devices, angles_here, tiles, tile_width, mods, fold = cfg
    cap, split, mine = plan[0], plan[1], plan[6]
    rows = freq_rows(devices * angles_here)
    half = mine * LANES // 2
    vmem = pl.BlockSpec(memory_space=pltpu.VMEM)
    message = pltpu.VMEM((devices, fold * angles_here, half), BF16)
    line = pltpu.VMEM((1, LANES), F32)
    lines = pltpu.VMEM((devices, 1, LANES), F32)
    rows_a = pltpu.VMEM((devices, 16, split * LANES), BF16)
    rows_b = pltpu.VMEM((devices, 16, (cap - split) * LANES), BF16)
    return pl.pallas_call(
        functools.partial(fast_kernel, cfg, plan),
        out_shape=pltpu.VMEM((angles_here, W), F32),
        in_specs=[pl.BlockSpec(memory_space=pl.ANY)] * 8,
        out_specs=vmem,
        scratch_shapes=[
            *[pltpu.VMEM(arg.shape, arg.dtype) for arg in args],
            rows_a,
            rows_a,
            rows_b,
            rows_b,
            lines,
            lines,
            pltpu.VMEM((angles_here * tiles, tile_width), F32),
            pltpu.VMEM((angles_here, W + 2 * LANES), F32),
            pltpu.VMEM((angles_here, W), F32),
            pltpu.VMEM((mods, W), BF16),
            pltpu.VMEM((devices, mods, 2 * mine * LANES), BF16),
            pltpu.VMEM((8, W), F32),
            pltpu.VMEM((devices, 8, 2 * mine * LANES), F32),
            message,
            message,
            message,
            message,
            line,
            lines,
            pltpu.VMEM((2 * fold, 2 * rows, half), F32),
            line,
            lines,
            message,
            message,
            message,
            message,
            *[pltpu.VMEM(table.shape, BF16) for table in tables],
            pltpu.SemaphoreType.DMA((8,)),
            pltpu.SemaphoreType.DMA((9, devices)),
            pltpu.SemaphoreType.DMA((9, devices)),
        ],
        compiler_params=pltpu.CompilerParams(
            collective_id=0, has_side_effects=True, vmem_limit_bytes=60 << 20
        ),
    )(*args, *[jnp.asarray(table) for table in tables])


def per_device(raw, block_dest, section_offset, ramp_length, module_width):
    devices = lax.axis_size("ang")
    blocks_here = raw.shape[0]
    tile_width = raw.shape[1]
    angles_here, tiles = section_offset.shape
    angles = angles_here * devices
    capacity = (blocks_here + devices - 1) // devices
    cols = W // devices
    fold = 2 if cols % (2 * LANES) == 0 else 1
    wire = BF16 if fold == 2 else F32
    mods = -(-module_width.shape[0] // 16) * 16
    half = cols // fold
    rows = freq_rows(angles)
    cfg = (devices, angles_here, tiles, tile_width, mods, fold)
    forward = forward_table(angles, devices, fold)
    inverse = inverse_table(angles, devices, fold)
    taps = ramp_table()
    plan = fast_plan(devices, angles_here, tiles, tile_width, mods, module_width.shape[0])
    if fold == 2 and plan:
        args = (
            raw,
            block_dest[None, :],
            section_offset,
            ramp_length[None, :],
            module_width[None, :],
        )
        return fast_call(cfg, plan, (forward, inverse, taps), args)
    vmem = pl.BlockSpec(memory_space=pltpu.VMEM)
    return pl.pallas_call(
        functools.partial(kernel, cfg),
        out_shape=pltpu.VMEM((angles_here, W), F32),
        in_specs=[vmem] * 5 + [pl.BlockSpec(memory_space=pl.ANY)] * 3,
        out_specs=vmem,
        scratch_shapes=[
            pltpu.VMEM((devices, 16, capacity * LANES), BF16),
            pltpu.VMEM((devices, 16, capacity * LANES), BF16),
            pltpu.VMEM((angles_here * tiles, tile_width), F32),
            pltpu.VMEM((angles_here, W + 2 * LANES), F32),
            pltpu.VMEM((angles_here, W + 2 * LANES), F32),
            pltpu.VMEM((angles_here, W), F32),
            pltpu.VMEM((devices, angles_here * fold, half), wire),
            pltpu.VMEM((devices, angles_here * fold, half), wire),
            pltpu.VMEM((fold, 2 * rows, half), F32),
            pltpu.VMEM((8, max(mods, LANES)), F32),
            pltpu.VMEM((devices, 8, max(mods, LANES)), F32),
            pltpu.VMEM((devices, angles_here * fold, half), wire),
            pltpu.VMEM((devices, angles_here * fold, half), wire),
            pltpu.VMEM((devices, 1, LANES), F32),
            pltpu.VMEM((devices, 1, LANES), F32),
            pltpu.VMEM(forward.shape, BF16),
            pltpu.VMEM(inverse.shape, BF16),
            pltpu.VMEM(taps.shape, BF16),
            pltpu.SemaphoreType.DMA((3,)),
            pltpu.SemaphoreType.DMA((5, devices)),
            pltpu.SemaphoreType.DMA((5, devices)),
        ],
        compiler_params=pltpu.CompilerParams(
            collective_id=0, has_side_effects=True, vmem_limit_bytes=60 << 20
        ),
    )(
        raw,
        block_dest[None, :],
        section_offset,
        ramp_length[None, :],
        module_width[None, :],
        jnp.asarray(forward),
        jnp.asarray(inverse),
        jnp.asarray(taps),
    )


def solution(mesh):
    in_specs = (P(("row", "ang"), None), P("ang"), P("ang", None), P(), P())
    out_specs = P(("row", "ang"), None)
    return jax.shard_map(
        per_device, mesh=mesh, in_specs=in_specs, out_specs=out_specs, check_vma=False
    )
```

```python
import functools
import math

import jax
import jax.numpy as jnp
import ml_dtypes
import numpy as np
from jax import lax
from jax.experimental import pallas as pl
from jax.experimental.pallas import tpu as pltpu
from jax.sharding import PartitionSpec as P

W = 16384
RAMP_HALF = 128
JITTER = 64
SHRINK_SCALE = 1.0
EPSILON = 1e-06
LANES = 128
SPAN = 2048
SHARED = 0.625

F32 = jnp.float32
BF16 = jnp.bfloat16


def split_np(table):
    high = table.astype(ml_dtypes.bfloat16)
    low = (table - high.astype(np.float64)).astype(ml_dtypes.bfloat16)
    return high, low


def freq_rows(angles):
    return -(-(angles // 2 + 1) // 8) * 8


def forward_table(angles, devices, fold):
    rows = freq_rows(angles)
    here = angles // devices
    k = np.arange(rows)[:, None]
    a = np.arange(angles)[None, :]
    phase = 2.0 * np.pi * ((k * a) % angles) / angles
    keep = (k <= angles // 2).astype(np.float64)
    table = np.concatenate([np.cos(phase) * keep, -np.sin(phase) * keep], axis=0)
    placed = np.zeros((fold, 2 * rows, devices, fold, here))
    for part in range(fold):
        placed[part, :, :, part, :] = table.reshape(2 * rows, devices, here)
    high, low = split_np(placed.reshape(fold, 2 * rows, devices * fold * here))
    return np.concatenate([high, low], axis=1)


def inverse_table(angles, devices, fold):
    rows = freq_rows(angles)
    k = np.arange(rows)[None, :]
    a = np.arange(angles)[:, None]
    phase = 2.0 * np.pi * ((k * a) % angles) / angles
    twice = np.where((k == 0) | (2 * k == angles), 1.0, 2.0) * (k <= angles // 2)
    weight = twice * np.exp(-np.minimum(k, angles - k) / (angles // 8)) / angles
    table = np.concatenate([np.cos(phase) * weight, -np.sin(phase) * weight], axis=1)
    high, low = split_np(table)
    table = np.concatenate([high, high, low], axis=1)
    if fold == 1:
        return table[None]
    here = angles // devices
    shared = np.kron(np.eye(devices), np.ones((here, here))) * (SHARED / here)
    placed = np.zeros((fold, angles, devices, fold, here))
    for part in range(fold):
        placed[part, :, :, part, :] = -shared.reshape(angles, devices, here)
    placed = placed.reshape(fold, angles, devices * fold * here).astype(ml_dtypes.bfloat16)
    return np.concatenate([np.broadcast_to(table, (fold,) + table.shape), placed], axis=2)


def ramp_table():
    i = np.arange(3 * LANES)[:, None] - LANES
    n = np.arange(LANES)[None, :] - i
    safe = np.where(n == 0, 1, n).astype(np.float64)
    taps = np.where(n % 2 != 0, -1.0 / (np.pi * np.pi * safe * safe), 0.0)
    taps = np.where(n == 0, 0.25, taps)
    taps = np.where(np.abs(n) <= RAMP_HALF, taps, 0.0)
    high, low = split_np(taps)
    return np.stack([high, low])


def dot(left, right):
    return jnp.dot(left, right, preferred_element_type=F32)


def dot_nt(left, right):
    return lax.dot_general(left, right, (((1,), (1,)), ((), ())), preferred_element_type=F32)


def halves(x):
    high = x.astype(BF16)
    return high, (x - high.astype(F32)).astype(BF16)


def thirds(x):
    high = x.astype(BF16).astype(F32)
    rest = x - high
    mid = rest.astype(BF16).astype(F32)
    low = rest - mid
    return jnp.concatenate([high, mid, low, jnp.zeros_like(x)], axis=0).astype(BF16)


def iota(shape, axis):
    return lax.broadcasted_iota(jnp.int32, shape, axis)


def loop(count, body):
    if count <= 8:
        for step in range(count):
            body(step)
    else:

        def run(step, carry):
            body(step)
            return carry

        lax.fori_loop(0, count, run, 0)


def kernel(
    cfg,
    raw_ref,
    dest_ref,
    offset_ref,
    ramp_ref,
    width_ref,
    fwd_hbm,
    inv_hbm,
    taps_hbm,
    out_ref,
    rows_send,
    rows_recv,
    grid_ref,
    sum_ref,
    weight_ref,
    proj_ref,
    cent_send,
    cent_recv,
    spec_ref,
    level_send,
    level_recv,
    stripe_send,
    stripe_recv,
    ids_send,
    ids_recv,
    fwd_ref,
    inv_ref,
    taps_ref,
    table_sem,
    send_sem,
    recv_sem,
):
    devices, angles_here, tiles, tile_width, mods, fold = cfg
    angles = devices * angles_here
    cols = W // devices
    half = cols // fold
    rows = freq_rows(angles)
    step_cols = (W - tile_width) // (tiles - 1)
    window = tile_width + 2 * LANES
    blocks = angles_here * tiles
    me = lax.axis_index("ang")

    def ring_at(hop):
        return lax.rem(me + hop, devices)

    def peer_at(hop):
        if devices & (devices - 1):
            return ring_at(hop)
        mask = devices - hop
        peer = 0
        bit = 1
        while bit < devices:
            peer = peer + bit * lax.rem(lax.div(me, bit) + mask // bit, 2)
            bit *= 2
        return peer

    barrier = pltpu.get_barrier_semaphore()

    def greet(step):
        pl.semaphore_signal(
            barrier,
            inc=1,
            device_id={"ang": peer_at(step + 1)},
            device_id_type=pl.DeviceIdType.MESH,
        )

    loop(devices - 1, greet)
    fetch_fwd = pltpu.make_async_copy(fwd_hbm, fwd_ref, table_sem.at[0])
    fetch_inv = pltpu.make_async_copy(inv_hbm, inv_ref, table_sem.at[1])
    fetch_taps = pltpu.make_async_copy(taps_hbm, taps_ref, table_sem.at[2])
    fetch_fwd.start()
    fetch_inv.start()
    fetch_taps.start()

    def remote(phase, src, dst, slot, peer):
        return pltpu.make_async_remote_copy(
            src_ref=src,
            dst_ref=dst,
            send_sem=send_sem.at[phase, peer],
            recv_sem=recv_sem.at[phase, slot],
            device_id={"ang": peer},
            device_id_type=pl.DeviceIdType.MESH,
        )

    def finish(phase, send_of, recv_of):
        def body(step):
            peer = peer_at(step + 1)
            copy = remote(phase, send_of(peer), recv_of(peer), peer, peer)
            copy.wait_recv()
            copy.wait_send()

        loop(devices - 1, body)

    cap = -(-blocks // devices)
    slab = 16
    chunks = tile_width // LANES
    extra = chunks - cap
    slots = devices * slab
    dest_row = dest_ref[...].astype(F32)
    source_row = iota((blocks, blocks), 1)
    source_col = iota((blocks, blocks), 0)

    def turned(values):
        return jnp.sum(jnp.where(source_row == source_col, values, 0.0), axis=1, keepdims=True)

    owner_row = jnp.floor((dest_row + 0.5) * (1.0 / blocks))
    owner_col = turned(owner_row)
    earlier = (owner_col == owner_row) & (source_col < source_row)
    rank_row = jnp.sum(jnp.where(earlier, 1.0, 0.0), axis=0, keepdims=True)
    rank_col = turned(rank_row)
    place_row = dest_row - owner_row * blocks + 1.0
    slot = iota((slots, 1), 0).astype(F32)

    def one_hot(left, right):
        return jnp.where(left == right, 1.0, 0.0).astype(BF16)

    direct = one_hot(slot, owner_row * slab + rank_row)
    packed = dot(direct, raw_ref[:, : cap * LANES])
    keeps = [
        jnp.where(jnp.broadcast_to(rank_col, (blocks, LANES)) == j, 1.0, 0.0).astype(BF16)
        for j in range(cap)
    ]
    for e in range(extra):
        chunk = raw_ref[:, (cap + e) * LANES : (cap + e + 1) * LANES]
        masked = jnp.concatenate([chunk * keep for keep in keeps], axis=1)
        packed = packed + dot(one_hot(slot, owner_row * slab + (cap + e)), masked)
    rows_send[...] = packed.astype(BF16).reshape(devices, slab, cap * LANES)
    group = LANES // slab
    groups = -(-devices // group)
    lane_at = iota((blocks, LANES), 1).astype(F32)
    first_lane = (lax.rem(me, group) * slab).astype(F32)
    at_rank = one_hot(lane_at, rank_col + first_lane)
    to_owner = jnp.where(iota((devices, blocks), 0).astype(F32) == owner_row, place_row, 0.0)
    ids_send[...] = dot(to_owner.astype(BF16), at_rank).reshape(devices, 1, LANES)

    pl.semaphore_wait(barrier, devices - 1)

    def send_rows(step):
        peer = peer_at(step + 1)
        remote(4, ids_send.at[peer], ids_recv.at[me], me, peer).start()
        remote(0, rows_send.at[peer], rows_recv.at[me], me, peer).start()

    loop(devices - 1, send_rows)
    rows_recv[me] = rows_send[me]
    ids_recv[me] = ids_send[me]
    finish(4, lambda p: ids_send.at[p], lambda p: ids_recv.at[p])
    finish(0, lambda p: rows_send.at[p], lambda p: rows_recv.at[p])

    ids = [
        jnp.sum(ids_recv[g * group : min((g + 1) * group, devices)], axis=0) for g in range(groups)
    ]
    ids = ids[0] if groups == 1 else jnp.concatenate(ids, axis=1)
    ids = jnp.broadcast_to(ids[:, :slots], (8, slots))
    row = iota((blocks, 1), 0).astype(F32)
    tile_of = jnp.floor((row + 0.5) * (1.0 / angles_here))
    wanted = (row - tile_of * angles_here) * tiles + tile_of + 1.0
    lead = rows_recv[...].reshape(slots, cap * LANES)
    grid_ref[:, : cap * LANES] = dot(one_hot(wanted, ids[0:1]), lead)
    if extra:
        within = iota((8, slots), 1) & (slab - 1)
        turns = [pltpu.roll(ids, n, 1) if n else ids for n in range(slab)]
        wanted_at = jnp.concatenate(
            [jnp.where(within[0:1] == cap + e, wanted, -1.0) for e in range(extra)], axis=0
        )
        rest = jnp.zeros((extra * blocks, LANES), F32)
        for j in range(cap):
            ids_j = jnp.zeros((8, slots), F32)
            for e in range(extra):
                ids_j = jnp.where(within == cap + e, turns[cap + e - j], ids_j)
            part = rows_recv[:, :, j * LANES : (j + 1) * LANES].reshape(slots, LANES)
            rest = rest + dot(one_hot(wanted_at, ids_j[0:1]), part)
        for e in range(extra):
            at = (cap + e) * LANES
            grid_ref[:, at : at + LANES] = rest[e * blocks : (e + 1) * blocks]

    fetch_fwd.wait()
    fetch_inv.wait()
    fetch_taps.wait()

    sum_ref[...] = jnp.zeros_like(sum_ref)
    weight_ref[...] = jnp.zeros_like(weight_ref)
    inverse_ramp = 1.0 / ramp_ref[...].astype(F32)
    lane = iota((angles_here, window), 1)
    for tile in range(tiles):
        base = tile * step_cols
        shift = jnp.broadcast_to(
            offset_ref[:, tile : tile + 1] - (base - LANES), (angles_here, window)
        )
        piece = jnp.concatenate(
            [
                grid_ref[tile * angles_here : (tile + 1) * angles_here, :],
                jnp.zeros((angles_here, 2 * LANES), F32),
            ],
            axis=1,
        )
        for bit in range(8):
            moved = pltpu.roll(piece, 1 << bit, 1)
            piece = jnp.where((shift & (1 << bit)) != 0, moved, piece)
        x = lane - shift
        edge = (jnp.minimum(x, tile_width - 1 - x) + 1).astype(F32)
        feather = jnp.minimum(1.0, edge * inverse_ramp[:, tile : tile + 1])
        feather = jnp.maximum(feather, 0.0)
        sum_ref[:, base : base + window] += feather * piece
        weight_ref[:, base : base + window] += feather

    wide = width_ref[...].astype(F32)
    upper = iota((mods, wide.shape[1]), 1)
    lower = iota((mods, wide.shape[1]), 0)
    bounds = jnp.sum(jnp.where(upper <= lower, wide, 0.0), axis=1, keepdims=True)
    starts = jnp.sum(jnp.where(upper < lower, wide, 0.0), axis=1, keepdims=True)
    on_diagonal = iota((mods, mods), 0) == iota((mods, mods), 1)
    safe_wide = jnp.sum(jnp.where(on_diagonal, bounds - starts, 0.0), axis=0, keepdims=True)
    safe_wide = jnp.maximum(safe_wide, 1.0)

    def member(first, count):
        c = (iota((mods, count), 1) + first).astype(F32)
        inside = (c >= starts) & (c < bounds)
        return jnp.where(inside, 1.0, 0.0).astype(BF16)

    def project(step, total):
        at = step * SPAN
        behind = at + LANES
        blended = sum_ref[:, pl.ds(behind, SPAN)] / weight_ref[:, pl.ds(behind, SPAN)]
        projection = -jnp.log(blended)
        proj_ref[:, pl.ds(at, SPAN)] = projection
        return total + dot_nt(thirds(projection), member(at, SPAN))

    total = jnp.zeros((4 * angles_here, mods), F32)
    for step in range(W // SPAN):
        total = project(step, total)

    def gather_thirds(stack):
        a = angles_here
        return stack[0:a] + stack[a : 2 * a] + stack[2 * a : 3 * a]

    mean = thirds(gather_thirds(total) / safe_wide)

    def centered_slab(owner):
        at = pl.multiple_of(owner * cols, LANES)
        flat = proj_ref[:, pl.ds(at, cols)] - gather_thirds(dot(mean, member(at, cols)))
        if fold > 1:
            flat = jnp.concatenate([flat[:, i * half : (i + 1) * half] for i in range(fold)], axis=0)
        return flat.astype(cent_send.dtype)

    def send_centered(step):
        peer = peer_at(step + 1)
        cent_send[peer] = centered_slab(peer)
        remote(1, cent_send.at[peer], cent_recv.at[me], me, peer).start()

    loop(devices - 1, send_centered)
    cent_send[me] = centered_slab(me)
    cent_recv[me] = cent_send[me]

    if fold > 1:
        shared_row = iota((fold * angles_here, fold * angles_here), 0)
        shared_col = iota((fold * angles_here, fold * angles_here), 1)
        same = (shared_row // angles_here) == (shared_col // angles_here)
        shared_table = jnp.where(same, SHARED / angles_here, 0.0).astype(BF16)

        def take_shared(owner):
            at = pl.multiple_of(owner * cols, LANES)
            shared = dot(shared_table, cent_send[owner])
            shared = jnp.concatenate(
                [shared[i * angles_here : (i + 1) * angles_here] for i in range(fold)], axis=1
            )
            proj_ref[:, pl.ds(at, cols)] = proj_ref[:, pl.ds(at, cols)] - shared

        loop(devices, take_shared)

    finish(1, lambda p: cent_send.at[p], lambda p: cent_recv.at[p])

    signal = cent_recv[...].reshape(devices * fold * angles_here, half).astype(BF16)
    k = iota((rows, 1), 0)
    count_of = jnp.where((k == 0) | (2 * k == angles), 1.0, 2.0)
    count_of = jnp.where(2 * k <= angles, count_of, 0.0)
    mine = pl.multiple_of(me * cols, LANES)
    sums = jnp.zeros((4 * 8, mods), F32)
    for part in range(fold):
        wide_spec = dot(fwd_ref[part], signal)
        spectrum = wide_spec[: 2 * rows] + wide_spec[2 * rows :]
        spec_ref[part] = spectrum
        magnitude = jnp.sqrt(
            spectrum[:rows] * spectrum[:rows] + spectrum[rows:] * spectrum[rows:]
        )
        over_k = jnp.sum(magnitude * count_of, axis=0, keepdims=True)
        first_row = jnp.where(iota((8, half), 0) == 0, over_k, 0.0)
        sums = sums + dot_nt(thirds(first_row), member(mine + part * half, half))
    level_send[...] = jnp.zeros_like(level_send)
    level_send[:, 0:mods] = sums[0:8] + sums[8:16] + sums[16:24]

    def send_level(step):
        peer = peer_at(step + 1)
        remote(2, level_send, level_recv.at[me], me, peer).start()

    loop(devices - 1, send_level)
    level_recv[me] = level_send[...]
    finish(2, lambda p: level_send, lambda p: level_recv.at[p])
    everything = jnp.sum(level_recv[...], axis=0)[:, 0:mods]
    level = SHRINK_SCALE * (everything / (angles * safe_wide) + EPSILON)
    level_parts = thirds(jnp.where(iota((8, mods), 0) == 0, level, 0.0))

    residual = []
    for part in range(fold):
        spread = dot(level_parts, member(mine + part * half, half))
        level_col = spread[0:1] + spread[8:9] + spread[16:17]
        spectrum = spec_ref[part]
        magnitude = jnp.sqrt(
            spectrum[:rows] * spectrum[:rows] + spectrum[rows:] * spectrum[rows:]
        )
        factor = jnp.maximum(magnitude - level_col, 0.0) / jnp.maximum(magnitude, level_col)
        shrunk = jnp.concatenate([spectrum[:rows] * factor, spectrum[rows:] * factor], axis=0)
        high, low = halves(shrunk)
        parts = [high, low, high] + ([signal] if fold > 1 else [])
        stripe = dot(inv_ref[part], jnp.concatenate(parts, axis=0))
        residual.append(stripe.reshape(devices, angles_here, half))
    stripe_send[...] = jnp.concatenate(residual, axis=1).astype(stripe_send.dtype)

    def send_stripe(step):
        peer = ring_at(step + 1)
        remote(3, stripe_send.at[peer], stripe_recv.at[me], me, peer).start()

    loop(devices - 1, send_stripe)
    stripe_recv[me] = stripe_send[me]

    sum_ref[:, 0:LANES] = jnp.zeros((angles_here, LANES), F32)
    sum_ref[:, W + LANES :] = jnp.zeros((angles_here, LANES), F32)
    lane_blocks = cols // LANES

    def clean(owner):
        at = pl.multiple_of(owner * cols, LANES)
        behind = pl.multiple_of(owner * cols + LANES, LANES)
        rest = stripe_recv[owner].astype(F32)
        rest = jnp.concatenate(
            [rest[i * angles_here : (i + 1) * angles_here] for i in range(fold)], axis=1
        )
        sum_ref[:, pl.ds(behind, cols)] = proj_ref[:, pl.ds(at, cols)] - rest

    def ramp(group):
        at = pl.multiple_of(group * cols, LANES)
        flat = sum_ref[:, pl.ds(at, cols + 2 * LANES)]
        stack = jnp.concatenate(
            [flat[:, b * LANES : (b + 1) * LANES] for b in range(lane_blocks + 2)], axis=0
        )
        n = lane_blocks * angles_here
        near = jnp.concatenate(
            [stack[s * angles_here : s * angles_here + n] for s in range(3)], axis=1
        )
        high, low = halves(near)
        done = dot(high, taps_ref[0]) + dot(low, taps_ref[0]) + dot(high, taps_ref[1])
        out_ref[:, pl.ds(at, cols)] = jnp.concatenate(
            [done[b * angles_here : (b + 1) * angles_here] for b in range(lane_blocks)], axis=1
        )

    clean(me)

    def below(hop):
        return lax.rem(me + devices - hop, devices)

    def take(hop):
        owner = below(hop)
        remote(3, stripe_send.at[owner], stripe_recv.at[owner], owner, owner).wait_recv()
        clean(owner)

    take(1)

    def advance(step):
        take(step + 2)
        ramp(below(step + 1))

    loop(devices - 2, advance)
    ramp(below(devices - 1))
    ramp(me)

    def sent(step):
        peer = ring_at(step + 1)
        remote(3, stripe_send.at[peer], stripe_recv.at[peer], peer, peer).wait_send()

    loop(devices - 1, sent)


def pack_plan(cap, chunks, first, need):
    split = next(
        (n for n in range(1, cap) if n + (chunks - cap) * n // cap >= need), 0
    )
    run = list(range(first, first + need))
    others = [b for b in range(chunks) if b not in run]
    direct = run[:split] + others[: cap - split]
    cells = {}
    n = 0
    early = (chunks - cap) * split
    for block in run[split:] + others[cap - split :]:
        for rank in range(cap):
            if n < early:
                cells[cap + n // split, n % split] = (rank, block)
            else:
                late = n - early
                cells[cap + late // (cap - split), split + late % (cap - split)] = (rank, block)
            n += 1
    return split, direct, cells


def fast_plan(devices, angles_here, tiles, tile_width, mods, modules):
    cols = W // devices
    step_cols = (W - tile_width) // (tiles - 1)
    cap = -(-angles_here * tiles // devices)
    chunks = tile_width // LANES
    if cols % (4 * LANES) or step_cols % LANES or tile_width % LANES:
        return None
    mine = cols // (2 * LANES)
    per_step = step_cols // LANES
    first = -(-(tile_width - step_cols + JITTER) // LANES) + 1
    back = per_step - first - mine
    fits = (
        tiles == devices + 1
        and angles_here == 8
        and angles_here * mods == LANES
        and modules <= 8
        and chunks == 16
        and devices * chunks == LANES
        and 1 < cap < chunks
        and back >= 1
        and tile_width < 2 * step_cols - 2 * JITTER
        and (first + mine) * LANES <= step_cols - JITTER
    )
    if not fits:
        return None
    split, direct, cells = pack_plan(cap, chunks, first - 1, mine + 2)
    if not split:
        return None
    alone = {t * per_step + first + i for t in range(tiles) for i in range(mine)}
    early, late = [], []
    for p in range(devices):
        window = range(2 * p * mine, 2 * (p + 1) * mine)
        early.append([b for b in window if b in alone][:mine])
        late.append([b for b in window if b not in early[p]])
    if any(len(run) != mine for run in early):
        return None
    reach = -(-2 * W // modules // cols)
    return cap, split, direct, cells, first, back, mine, early, late, reach


def fast_kernel(
    cfg,
    plan,
    raw_hbm,
    dest_hbm,
    offset_hbm,
    ramp_hbm,
    width_hbm,
    fwd_hbm,
    inv_hbm,
    taps_hbm,
    shared_hbm,
    out_ref,
    raw_ref,
    dest_ref,
    offset_ref,
    ramp_ref,
    width_ref,
    rows_send_a,
    rows_recv_a,
    rows_send_b,
    rows_recv_b,
    ids_send,
    ids_recv,
    grid_ref,
    clean_ref,
    proj_ref,
    hot_ref,
    weight_ref,
    member_ref,
    member_own_ref,
    inside_ref,
    inside_own_ref,
    cent_send_a,
    cent_recv_a,
    cent_send_b,
    cent_recv_b,
    diff_send,
    diff_recv,
    spec_ref,
    size_ref,
    level_send,
    level_recv,
    stripe_send_a,
    stripe_recv_a,
    stripe_send_b,
    stripe_recv_b,
    known_ref,
    fwd_ref,
    inv_ref,
    taps_ref,
    shared_ref,
    table_sem,
    send_sem,
    recv_sem,
):
    devices, angles_here, tiles, tile_width, mods, fold = cfg
    cap, split, direct_blocks, cells, first, back, mine, early, late, reach = plan
    angles = devices * angles_here
    rows = freq_rows(angles)
    step_cols = (W - tile_width) // (tiles - 1)
    blocks = angles_here * tiles
    chunks = tile_width // LANES
    slab = chunks
    slots = devices * slab
    width = mine * LANES
    half = width // 2
    me = lax.axis_index("ang")
    ROWS_A, ROWS_B, IDS, CENT_A, CENT_B, DIFF, LEVEL, STRIPE_A, STRIPE_B = range(9)

    def peer_at(hop):
        mask = devices - hop
        peer = 0
        bit = 1
        while bit < devices:
            peer = peer + bit * lax.rem(lax.div(me, bit) + mask // bit, 2)
            bit *= 2
        return peer

    peers = [peer_at(hop) for hop in range(1, devices)]
    barrier = pltpu.get_barrier_semaphore()
    for peer in peers:
        pl.semaphore_signal(
            barrier, inc=1, device_id={"ang": peer}, device_id_type=pl.DeviceIdType.MESH
        )
    fetched = [
        (dest_hbm, dest_ref),
        (raw_hbm, raw_ref),
        (width_hbm, width_ref),
        (offset_hbm, offset_ref),
        (ramp_hbm, ramp_ref),
        (fwd_hbm, fwd_ref),
        (inv_hbm, inv_ref),
        (taps_hbm, taps_ref),
        (shared_hbm, shared_ref),
    ]
    fetches = [
        pltpu.make_async_copy(src, dst, table_sem.at[i]) for i, (src, dst) in enumerate(fetched)
    ]
    for fetch in fetches:
        fetch.start()

    def remote(phase, src, dst, slot, peer):
        return pltpu.make_async_remote_copy(
            src_ref=src,
            dst_ref=dst,
            send_sem=send_sem.at[phase, peer],
            recv_sem=recv_sem.at[phase, slot],
            device_id={"ang": peer},
            device_id_type=pl.DeviceIdType.MESH,
        )

    def send_all(phase, send_ref, recv_ref):
        for peer in peers:
            remote(phase, send_ref.at[peer], recv_ref.at[me], me, peer).start()

    def wait_recv(phase, send_ref, recv_ref):
        for peer in peers:
            remote(phase, send_ref.at[peer], recv_ref.at[peer], peer, peer).wait_recv()

    def wait_send(phase, send_ref, recv_ref):
        for peer in peers:
            remote(phase, send_ref.at[peer], recv_ref.at[peer], peer, peer).wait_send()

    fetches[0].wait()
    dest_row = dest_ref[...].astype(F32)
    source_row = iota((blocks, blocks), 1)
    source_col = iota((blocks, blocks), 0)

    def turned(values):
        return jnp.sum(jnp.where(source_row == source_col, values, 0.0), axis=1, keepdims=True)

    owner_row = jnp.floor((dest_row + 0.5) * (1.0 / blocks))
    owner_col = turned(owner_row)
    earlier = (owner_col == owner_row) & (source_col < source_row)
    rank_row = jnp.sum(jnp.where(earlier, 1.0, 0.0), axis=0, keepdims=True)
    rank_col = turned(rank_row)
    place_row = dest_row - owner_row * blocks + 1.0
    slot = iota((slots, 1), 0).astype(F32)

    def one_hot(left, right):
        return jnp.where(left == right, 1.0, 0.0).astype(BF16)

    direct = one_hot(slot, owner_row * slab + rank_row)
    keeps = [
        jnp.where(jnp.broadcast_to(rank_col, (blocks, LANES)) == j, 1.0, 0.0).astype(BF16)
        for j in range(cap)
    ]

    def lane_block(b):
        return raw_ref[:, b * LANES : (b + 1) * LANES]

    def pack(columns):
        packed = dot(direct, jnp.concatenate([lane_block(direct_blocks[k]) for k in columns], axis=1))
        for r in range(cap, slab):
            masked = jnp.concatenate(
                [lane_block(cells[r, k][1]) * keeps[cells[r, k][0]] for k in columns], axis=1
            )
            packed = packed + dot(one_hot(slot, owner_row * slab + r), masked)
        return packed.astype(BF16).reshape(devices, slab, len(columns) * LANES)

    columns_a = range(split)
    columns_b = range(split, cap)
    lane_at = iota((blocks, LANES), 1).astype(F32)
    first_lane = (me * slab).astype(F32)
    at_rank = one_hot(lane_at, rank_col + first_lane)
    to_owner = jnp.where(iota((devices, blocks), 0).astype(F32) == owner_row, place_row, 0.0)
    ids_send[...] = dot(to_owner.astype(BF16), at_rank).reshape(devices, 1, LANES)
    fetches[1].wait()
    rows_send_a[...] = pack(columns_a)

    pl.semaphore_wait(barrier, devices - 1)

    send_all(IDS, ids_send, ids_recv)
    send_all(ROWS_A, rows_send_a, rows_recv_a)
    rows_send_b[...] = pack(columns_b)
    send_all(ROWS_B, rows_send_b, rows_recv_b)
    rows_recv_a[me] = rows_send_a[me]
    rows_recv_b[me] = rows_send_b[me]
    ids_recv[me] = ids_send[me]

    for fetch in fetches[2:5]:
        fetch.wait()
    wide = width_ref[...].astype(F32)
    upper = iota((mods, wide.shape[1]), 1)
    lower = iota((mods, wide.shape[1]), 0)
    bounds = jnp.sum(jnp.where(upper <= lower, wide, 0.0), axis=1, keepdims=True)
    starts = jnp.sum(jnp.where(upper < lower, wide, 0.0), axis=1, keepdims=True)
    on_diagonal = iota((mods, mods), 0) == iota((mods, mods), 1)
    safe_wide = jnp.sum(jnp.where(on_diagonal, bounds - starts, 0.0), axis=0, keepdims=True)
    safe_wide = jnp.maximum(safe_wide, 1.0)
    bounds = jnp.broadcast_to(bounds, (mods, LANES))
    starts = jnp.broadcast_to(starts, (mods, LANES))
    lane = iota((mods, LANES), 1).astype(F32)
    for b in range(W // LANES):
        c = lane + float(b * LANES)
        inside = (c >= starts) & (c < bounds)
        inside = jnp.where(inside, 1.0, 0.0)
        member_ref[:, b * LANES : (b + 1) * LANES] = inside.astype(BF16)
        inside_ref[:, b * LANES : (b + 1) * LANES] = inside[0:8]
    for p in range(devices):
        for i, b in enumerate(early[p] + late[p]):
            at = i * LANES
            member_own_ref[p, :, at : at + LANES] = member_ref[:, b * LANES : (b + 1) * LANES]
            inside_own_ref[p, :, at : at + LANES] = inside_ref[:, b * LANES : (b + 1) * LANES]
    held = range(width_ref.shape[1])

    def inside_early(m, p):
        return inside_own_ref[p, m : m + 1, :width]

    def inside_late(m, p):
        return inside_own_ref[p, m : m + 1, width:]

    def narrowed(x):
        pieces = [x[:, i * LANES : (i + 1) * LANES] for i in range(mine)]
        while len(pieces) > 1:
            odd = pieces[len(pieces) // 2 * 2 :]
            pieces = [x + y for x, y in zip(pieces[::2], pieces[1::2])] + odd
        return pieces[0]

    def module_sums(flats, inside_of):
        sums = []
        for m in held:
            total = narrowed(flats[0] * inside_of(m, 0))
            for p in range(1, devices):
                total = total + narrowed(flats[p] * inside_of(m, p))
            sums.append(jnp.sum(total, axis=1, keepdims=True))
        return sums

    def less_mean(flat, means, inside_of, p):
        for m in held:
            flat = flat - means[m] * inside_of(m, p)
        flat = jnp.concatenate([flat[:, :half], flat[:, half:]], axis=0)
        return flat.astype(BF16)

    blank_row = jnp.ones((1, width), F32)
    counts = module_sums([blank_row] * devices, inside_early)
    scales_a = [1.0 / jnp.maximum(count, 1.0) for count in counts]
    scales = [
        1.0 / jnp.maximum(jnp.sum(width_ref[0:1, m : m + 1], axis=1, keepdims=True).astype(F32), 1.0)
        for m in held
    ]

    row = iota((blocks, 1), 0).astype(F32)
    tile_of = jnp.floor((row + 0.5) * (1.0 / angles_here))
    wanted = (row - tile_of * angles_here) * tiles + tile_of + 1.0
    wanted = jnp.broadcast_to(wanted, (blocks, LANES))
    within = iota((8, slots), 1) & (slab - 1)

    wait_recv(IDS, ids_send, ids_recv)
    ids = jnp.broadcast_to(jnp.sum(ids_recv[...], axis=0), (8, slots))
    turns = [pltpu.roll(ids, n, 1) if n else ids for n in range(slab)]

    def match(ids_row):
        return jnp.where(wanted == jnp.broadcast_to(ids_row[0:1], (blocks, LANES)), 1.0, 0.0)

    held_in = {k: sorted({cells[r, k][1] for r in range(cap, slab)}) for k in range(cap)}
    padded = -(-blocks // 16) * 16
    direct_ref = hot_ref.at[:blocks]
    direct_ref[...] = match(ids).astype(BF16)
    hot_at = {}
    top = padded
    for k in range(cap):
        hot = []
        for b in held_in[k]:
            ids_b = jnp.zeros((8, slots), F32)
            for r in range(cap, slab):
                if cells[r, k][1] == b:
                    ids_b = jnp.where(within == r, turns[r - cells[r, k][0]], ids_b)
            hot.append(match(ids_b))
        count = len(hot) * blocks
        hot_at[k] = (top, count)
        hot_ref[top : top + count] = jnp.concatenate(hot, axis=0).astype(BF16)
        top += -(-count // 16) * 16

    begun = set()

    def unpack(columns, recv_ref):
        lead = recv_ref[...].reshape(slots, len(columns) * LANES)
        flat = dot(direct_ref[...], lead)
        for at, k in enumerate(columns):
            b = direct_blocks[k]
            grid_ref[:, b * LANES : (b + 1) * LANES] = flat[:, at * LANES : (at + 1) * LANES]
        sums = {}
        for at, k in enumerate(columns):
            start, count = hot_at[k]
            part = dot(hot_ref[start : start + count], lead[:, at * LANES : (at + 1) * LANES])
            for i, b in enumerate(held_in[k]):
                piece = part[i * blocks : (i + 1) * blocks]
                sums[b] = sums[b] + piece if b in sums else piece
        for b, value in sums.items():
            at = b * LANES
            if b in begun:
                value = value + grid_ref[:, at : at + LANES]
            begun.add(b)
            grid_ref[:, at : at + LANES] = value

    def shift_of(tile):
        ahead = LANES - (offset_ref[:, tile : tile + 1] - tile * step_cols)
        return jnp.broadcast_to(ahead, (angles_here, LANES))

    lane_here = iota((angles_here, LANES), 1)

    def shifted(pieces, ahead, wanted_blocks):
        far = (ahead & LANES) != 0
        steps = [1 << n for n in range(LANES.bit_length() - 1)]
        masks = [(ahead & step) != 0 for step in steps]
        stay = lane_here < LANES - (ahead & (LANES - 1))
        blank = jnp.zeros((angles_here, LANES), F32)
        turned_at = {}
        for i in sorted({i + n for i in wanted_blocks for n in (0, 1)}):
            near_piece, far_piece = pieces.get(i), pieces.get(i + 1)
            if near_piece is None and far_piece is None:
                turned_at[i] = blank
                continue
            x = jnp.where(
                far,
                blank if far_piece is None else far_piece,
                blank if near_piece is None else near_piece,
            )
            for step, mask in zip(steps, masks):
                x = jnp.where(mask, pltpu.roll(x, LANES - step, 1), x)
            turned_at[i] = x
        return {i: jnp.where(stay, turned_at[i], turned_at[i + 1]) for i in wanted_blocks}

    def tile_block(tile, b):
        return grid_ref[tile * angles_here : (tile + 1) * angles_here, b * LANES : (b + 1) * LANES]

    def tile_blocks(tile, start, stop, at):
        return {at + b - start: tile_block(tile, b) for b in range(start, stop)}

    shifts = [shift_of(t) for t in range(tiles)]
    gap = back + first
    inverse_ramp = 1.0 / ramp_ref[...].astype(F32)
    left_at = step_cols // LANES - back - 1
    per_step = step_cols // LANES
    left_end = back - (-(tile_width - step_cols + JITTER) // LANES)
    right_start = back - 1 - (JITTER - 1) // LANES
    lane_float = lane_here.astype(F32)
    shared_blocks = range(right_start, left_end)
    for g in range(1, tiles):
        ahead_left = lane_float + shifts[g - 1].astype(F32)
        ahead_right = lane_float + shifts[g].astype(F32)
        for n, i in enumerate(shared_blocks):
            till = float(tile_width - (left_at + i) * LANES)
            since = float((i - back - 1) * LANES + 1)
            feather_left = (till - ahead_left) * inverse_ramp[:, g - 1 : g]
            feather_right = (ahead_right + since) * inverse_ramp[:, g : g + 1]
            feather_left = jnp.maximum(jnp.minimum(1.0, feather_left), 0.0)
            feather_right = jnp.maximum(jnp.minimum(1.0, feather_right), 0.0)
            both = 1.0 / (feather_left + feather_right)
            weight_ref[0, g - 1, :, n * LANES : (n + 1) * LANES] = feather_left * both
            weight_ref[1, g - 1, :, n * LANES : (n + 1) * LANES] = feather_right * both

    wait_recv(ROWS_A, rows_send_a, rows_recv_a)
    unpack(columns_a, rows_recv_a)
    values = {}
    for t in range(tiles):
        if t in (0, tiles - 1):
            value = {i: tile_block(t, first + i) for i in range(mine)}
        else:
            pieces = tile_blocks(t, first - 1, first + mine + 1, 0)
            value = shifted(pieces, shifts[t], range(mine))
        for i in range(mine):
            values[t * (step_cols // LANES) + first + i] = value[i]

    def project(block_lists):
        flats = []
        for block_list in block_lists:
            flat = -jnp.log(jnp.concatenate([values[b] for b in block_list], axis=1))
            flats.append(flat)
            for i, b in enumerate(block_list):
                proj_ref[:, b * LANES : (b + 1) * LANES] = flat[:, i * LANES : (i + 1) * LANES]
        return flats

    flats_a = project(early)
    sums_a = module_sums(flats_a, inside_early)
    means_a = [sums_a[m] * scales_a[m] for m in held]
    for p in range(devices):
        cent_send_a[p] = less_mean(flats_a[p], means_a, inside_early, p)
    level_recv[...] = jnp.zeros_like(level_recv)
    send_all(CENT_A, cent_send_a, cent_recv_a)
    cent_recv_a[me] = cent_send_a[me]

    wait_recv(ROWS_B, rows_send_b, rows_recv_b)
    unpack(columns_b, rows_recv_b)
    for b in range(first):
        values[b] = tile_block(0, b)
    for g in range(1, tiles):
        left_pieces = tile_blocks(g - 1, left_at, chunks, 0)
        right_pieces = tile_blocks(g, 0, gap + 1 - back, back + 1)
        if g == 1:
            left = {i: left_pieces[i + 1] for i in range(left_end) if i + 1 in left_pieces}
        else:
            left = shifted(left_pieces, shifts[g - 1], range(left_end))
        if g == tiles - 1:
            right = {i: right_pieces[i + 1] for i in range(back, gap)}
        else:
            right = shifted(right_pieces, shifts[g], range(right_start, gap))
        for i in range(gap):
            if i not in left or i not in right:
                values[g * per_step - back + i] = left[i] if i in left else right[i]
                continue
            at = (i - right_start) * LANES
            values[g * per_step - back + i] = (
                weight_ref[0, g - 1, :, at : at + LANES] * left[i]
                + weight_ref[1, g - 1, :, at : at + LANES] * right[i]
            )
    for b in range(first + mine, chunks):
        values[(tiles - 1) * per_step + b] = tile_block(tiles - 1, b)
    flats = project(late)
    sums_b = module_sums(flats, inside_late)
    means = [(sums_a[m] + sums_b[m]) * scales[m] for m in held]
    lane_of = iota((angles_here, LANES), 1)
    own = (lane_of // mods) == iota((angles_here, LANES), 0)
    diff = jnp.zeros((angles_here, LANES), F32)
    for m in held:
        diff = jnp.where(lane_of % mods == m, means_a[m] - means[m], diff)
    diff_row = jnp.sum(jnp.where(own, diff, 0.0), axis=0, keepdims=True)
    diff_send[...] = diff_row
    for peer in peers:
        remote(DIFF, diff_send, diff_recv.at[me], me, peer).start()
    diff_recv[me] = diff_row
    for p in range(devices):
        cent_send_b[p] = less_mean(flats[p], means, inside_late, p)
    send_all(CENT_B, cent_send_b, cent_recv_b)
    cent_recv_b[me] = cent_send_b[me]

    shared_row = iota((fold * angles_here, fold * angles_here), 0)
    shared_col = iota((fold * angles_here, fold * angles_here), 1)
    same = (shared_row // angles_here) == (shared_col // angles_here)
    shared_table = jnp.where(same, SHARED / angles_here, 0.0).astype(BF16)
    for p in range(devices):
        for send_ref, block_list in ((cent_send_a, early[p]), (cent_send_b, late[p])):
            shared = dot(shared_table, send_ref[p])
            for i, b in enumerate(block_list):
                part, at = divmod(i, mine // 2)
                piece = shared[
                    part * angles_here : (part + 1) * angles_here, at * LANES : (at + 1) * LANES
                ]
                clean_ref[:, (b + 1) * LANES : (b + 2) * LANES] = (
                    proj_ref[:, b * LANES : (b + 1) * LANES] - piece
                )
    clean_ref[:, 0:LANES] = jnp.zeros((angles_here, LANES), F32)
    clean_ref[:, W + LANES :] = jnp.zeros((angles_here, LANES), F32)
    for fetch in fetches[5:]:
        fetch.wait()

    def near_of(block_list):
        return jnp.concatenate(
            [clean_ref[:, b * LANES : (b + 3) * LANES] for b in block_list], axis=0
        )

    def ramp_known(block_list):
        high, low = halves(near_of(block_list))
        done = dot(high, taps_ref[...])
        done = done[:, :LANES] + done[:, LANES:] + dot(low, taps_ref[:, :LANES])
        for i, b in enumerate(block_list):
            out_ref[:, b * LANES : (b + 1) * LANES] = done[i * angles_here : (i + 1) * angles_here]

    def ramp_less(block_list):
        done = dot(near_of(block_list).astype(BF16), taps_ref[...])
        done = done[:, :LANES] + done[:, LANES:]
        for i, b in enumerate(block_list):
            at = b * LANES
            out_ref[:, at : at + LANES] = (
                out_ref[:, at : at + LANES] - done[i * angles_here : (i + 1) * angles_here]
            )

    for at in range(0, W // LANES, 16):
        ramp_known(range(at, at + 16))

    k = iota((rows, 1), 0)
    count_of = jnp.where((k == 0) | (2 * k == angles), 1.0, 2.0)
    count_of = jnp.where(2 * k <= angles, count_of, 0.0)

    def magnitude_of(spectrum):
        return jnp.sqrt(spectrum[:rows] * spectrum[:rows] + spectrum[rows:] * spectrum[rows:])

    def summed(at, spectrum, inside):
        magnitude = magnitude_of(spectrum)
        spec_ref[at] = spectrum
        size_ref[at] = magnitude
        over_k = jnp.sum(magnitude * count_of, axis=0, keepdims=True)
        first_row = jnp.where(iota((8, half), 0) == 0, over_k, 0.0)
        return dot_nt(thirds(first_row), inside)

    member_own = [
        member_own_ref[me][:, i * half : (i + 1) * half] for i in range(2 * fold)
    ]

    wait_recv(CENT_A, cent_send_a, cent_recv_a)
    signal_a = cent_recv_a[...].reshape(devices * fold * angles_here, half)
    sums = jnp.zeros((4 * 8, mods), F32)
    found = []
    for part in range(fold):
        spread = dot(fwd_ref[part], signal_a)
        found.append(spread[: 2 * rows] + spread[2 * rows :])
    for peer in peers:
        remote(DIFF, diff_send, diff_recv.at[peer], peer, peer).wait_recv()
    diffs = []
    for p in range(devices):
        spread = jnp.where(own, jnp.broadcast_to(diff_recv[p], (angles_here, LANES)), 0.0)
        diffs += [spread] * fold
    high, low = halves(jnp.concatenate(diffs, axis=0))
    shift = dot(fwd_ref[0], jnp.concatenate([high, low], axis=1))
    shift = shift[: 2 * rows] + shift[2 * rows :]
    high, low = halves(shift[:, :LANES] + shift[:, LANES:])
    shift = jnp.concatenate([high, low], axis=1)
    for part in range(fold):
        inside = jnp.concatenate([member_own[part]] * (2 * LANES // mods), axis=0)
        spectrum = found[part] + dot(shift, inside)
        sums = sums + summed(part, spectrum, member_own[part])

    wait_recv(CENT_B, cent_send_b, cent_recv_b)
    signal_b = cent_recv_b[...].reshape(devices * fold * angles_here, half)
    for part in range(fold):
        spread = dot(fwd_ref[part], signal_b)
        spectrum = spread[: 2 * rows] + spread[2 * rows :]
        sums = sums + summed(fold + part, spectrum, member_own[fold + part])
    level_send[...] = jnp.zeros_like(level_send)
    level_send[:, 0:mods] = sums[0:1] + sums[8:9] + sums[16:17]
    hops = [hop for n in range(reach, 0, -1) for hop in (n, -n)]

    def near(hop, body):
        inside = me + hop < devices if hop > 0 else me + hop >= 0

        @pl.when(inside)
        def _():
            body(me + hop)

    for hop in hops:
        near(hop, lambda peer: remote(LEVEL, level_send, level_recv.at[me], me, peer).start())
    level_recv[me] = level_send[...]
    for at in range(2 * fold):
        size_ref[at] = 1.0 / size_ref[at]
        known_ref[at] = dot(shared_ref[at % fold], signal_a if at < fold else signal_b)
    wait_send(IDS, ids_send, ids_recv)
    wait_send(ROWS_A, rows_send_a, rows_recv_a)
    wait_send(ROWS_B, rows_send_b, rows_recv_b)
    for hop in hops:
        near(
            hop,
            lambda peer: remote(LEVEL, level_send, level_recv.at[peer], peer, peer).wait_recv(),
        )
    everything = jnp.sum(level_recv[...], axis=0)[:, 0:mods]
    level = SHRINK_SCALE * (everything / (angles * safe_wide) + EPSILON)
    level_parts = thirds(jnp.where(iota((8, mods), 0) == 0, level, 0.0))

    def inverse(at):
        spread = dot(level_parts, member_own[at])
        level_col = spread[0:1] + spread[8:9] + spread[16:17]
        spectrum = spec_ref[at]
        factor = jnp.maximum(1.0 - level_col * size_ref[at], 0.0)
        shrunk = jnp.concatenate([spectrum[:rows] * factor, spectrum[rows:] * factor], axis=0)
        high, low = halves(shrunk)
        stripe = dot(inv_ref[...], jnp.concatenate([high, low, high], axis=0)) + known_ref[at]
        return stripe.reshape(devices, angles_here, half)

    both = [inverse(part) for part in range(fold)]
    stripe_send_a[...] = jnp.concatenate(both, axis=1).astype(BF16)
    send_all(STRIPE_A, stripe_send_a, stripe_recv_a)
    both = [inverse(fold + part) for part in range(fold)]
    stripe_send_b[...] = jnp.concatenate(both, axis=1).astype(BF16)
    send_all(STRIPE_B, stripe_send_b, stripe_recv_b)
    stripe_recv_a[me] = stripe_send_a[me]
    stripe_recv_b[me] = stripe_send_b[me]
    wait_send(CENT_A, cent_send_a, cent_recv_a)
    wait_send(CENT_B, cent_send_b, cent_recv_b)
    for peer in peers:
        remote(DIFF, diff_send, diff_recv.at[peer], peer, peer).wait_send()
    for hop in hops:
        near(
            hop,
            lambda peer: remote(LEVEL, level_send, level_recv.at[peer], peer, peer).wait_send(),
        )

    def spread_stripe(recv_ref, block_lists):
        for p in range(devices):
            rest = recv_ref[p].astype(F32)
            for i, b in enumerate(block_lists[p]):
                part, at = divmod(i, mine // 2)
                piece = rest[
                    part * angles_here : (part + 1) * angles_here, at * LANES : (at + 1) * LANES
                ]
                clean_ref[:, (b + 1) * LANES : (b + 2) * LANES] = piece

    wait_recv(STRIPE_A, stripe_send_a, stripe_recv_a)
    spread_stripe(stripe_recv_a, early)
    found_early = {b for run in early for b in run}
    inner = [b for b in sorted(found_early) if b - 1 in found_early and b + 1 in found_early]
    outer = [b for b in range(W // LANES) if b not in set(inner)]
    for at in range(0, len(inner), 16):
        ramp_less(inner[at : at + 16])
    wait_recv(STRIPE_B, stripe_send_b, stripe_recv_b)
    spread_stripe(stripe_recv_b, late)
    for at in range(0, len(outer), 16):
        ramp_less(outer[at : at + 16])
    wait_send(STRIPE_A, stripe_send_a, stripe_recv_a)
    wait_send(STRIPE_B, stripe_send_b, stripe_recv_b)


def fast_call(cfg, plan, tables, args):
    devices, angles_here, tiles, tile_width, mods, fold = cfg
    cap, split, mine = plan[0], plan[1], plan[6]
    rows = freq_rows(devices * angles_here)
    half = mine * LANES // 2
    cells = plan[3]
    blocks = angles_here * tiles
    hot_rows = blocks + 16
    for k in range(cap):
        hot_rows += len({block for (_, at), (_, block) in cells.items() if at == k}) * blocks + 16
    hot_rows = -(-hot_rows // 16) * 16
    vmem = pl.BlockSpec(memory_space=pltpu.VMEM)
    message = pltpu.VMEM((devices, fold * angles_here, half), BF16)
    line = pltpu.VMEM((1, LANES), F32)
    lines = pltpu.VMEM((devices, 1, LANES), F32)
    rows_a = pltpu.VMEM((devices, 16, split * LANES), BF16)
    rows_b = pltpu.VMEM((devices, 16, (cap - split) * LANES), BF16)
    return pl.pallas_call(
        functools.partial(fast_kernel, cfg, plan),
        out_shape=pltpu.VMEM((angles_here, W), F32),
        in_specs=[pl.BlockSpec(memory_space=pl.ANY)] * 9,
        out_specs=vmem,
        scratch_shapes=[
            *[pltpu.VMEM(arg.shape, arg.dtype) for arg in args],
            rows_a,
            rows_a,
            rows_b,
            rows_b,
            lines,
            lines,
            pltpu.VMEM((angles_here * tiles, tile_width), F32),
            pltpu.VMEM((angles_here, W + 2 * LANES), F32),
            pltpu.VMEM((angles_here, W), F32),
            pltpu.VMEM((hot_rows, LANES), BF16),
            pltpu.VMEM((2, tiles - 1, angles_here, (plan[5] + plan[4]) * LANES), F32),
            pltpu.VMEM((mods, W), BF16),
            pltpu.VMEM((devices, mods, 2 * mine * LANES), BF16),
            pltpu.VMEM((8, W), F32),
            pltpu.VMEM((devices, 8, 2 * mine * LANES), F32),
            message,
            message,
            message,
            message,
            line,
            lines,
            pltpu.VMEM((2 * fold, 2 * rows, half), F32),
            pltpu.VMEM((2 * fold, rows, half), F32),
            line,
            lines,
            message,
            message,
            message,
            message,
            pltpu.VMEM((2 * fold, devices * angles_here, half), F32),
            *[pltpu.VMEM(table.shape, BF16) for table in tables],
            pltpu.SemaphoreType.DMA((9,)),
            pltpu.SemaphoreType.DMA((9, devices)),
            pltpu.SemaphoreType.DMA((9, devices)),
        ],
        compiler_params=pltpu.CompilerParams(
            collective_id=0, has_side_effects=True, vmem_limit_bytes=60 << 20
        ),
    )(*args, *[jnp.asarray(table) for table in tables])


def per_device(raw, block_dest, section_offset, ramp_length, module_width):
    devices = lax.axis_size("ang")
    blocks_here = raw.shape[0]
    tile_width = raw.shape[1]
    angles_here, tiles = section_offset.shape
    angles = angles_here * devices
    capacity = (blocks_here + devices - 1) // devices
    cols = W // devices
    fold = 2 if cols % (2 * LANES) == 0 else 1
    wire = BF16 if fold == 2 else F32
    mods = -(-module_width.shape[0] // 16) * 16
    half = cols // fold
    rows = freq_rows(angles)
    cfg = (devices, angles_here, tiles, tile_width, mods, fold)
    forward = forward_table(angles, devices, fold)
    inverse = inverse_table(angles, devices, fold)
    taps = ramp_table()
    plan = fast_plan(devices, angles_here, tiles, tile_width, mods, module_width.shape[0])
    if fold == 2 and plan:
        args = (
            raw,
            block_dest[None, :],
            section_offset,
            ramp_length[None, :],
            module_width[None, :],
        )
        depth = 3 * 2 * rows
        tables = (
            forward,
            inverse[0][:, :depth],
            np.concatenate(list(taps), axis=1),
            inverse[:, :, depth:],
        )
        return fast_call(cfg, plan, tables, args)
    vmem = pl.BlockSpec(memory_space=pltpu.VMEM)
    return pl.pallas_call(
        functools.partial(kernel, cfg),
        out_shape=pltpu.VMEM((angles_here, W), F32),
        in_specs=[vmem] * 5 + [pl.BlockSpec(memory_space=pl.ANY)] * 3,
        out_specs=vmem,
        scratch_shapes=[
            pltpu.VMEM((devices, 16, capacity * LANES), BF16),
            pltpu.VMEM((devices, 16, capacity * LANES), BF16),
            pltpu.VMEM((angles_here * tiles, tile_width), F32),
            pltpu.VMEM((angles_here, W + 2 * LANES), F32),
            pltpu.VMEM((angles_here, W + 2 * LANES), F32),
            pltpu.VMEM((angles_here, W), F32),
            pltpu.VMEM((devices, angles_here * fold, half), wire),
            pltpu.VMEM((devices, angles_here * fold, half), wire),
            pltpu.VMEM((fold, 2 * rows, half), F32),
            pltpu.VMEM((8, max(mods, LANES)), F32),
            pltpu.VMEM((devices, 8, max(mods, LANES)), F32),
            pltpu.VMEM((devices, angles_here * fold, half), wire),
            pltpu.VMEM((devices, angles_here * fold, half), wire),
            pltpu.VMEM((devices, 1, LANES), F32),
            pltpu.VMEM((devices, 1, LANES), F32),
            pltpu.VMEM(forward.shape, BF16),
            pltpu.VMEM(inverse.shape, BF16),
            pltpu.VMEM(taps.shape, BF16),
            pltpu.SemaphoreType.DMA((3,)),
            pltpu.SemaphoreType.DMA((5, devices)),
            pltpu.SemaphoreType.DMA((5, devices)),
        ],
        compiler_params=pltpu.CompilerParams(
            collective_id=0, has_side_effects=True, vmem_limit_bytes=60 << 20
        ),
    )(
        raw,
        block_dest[None, :],
        section_offset,
        ramp_length[None, :],
        module_width[None, :],
        jnp.asarray(forward),
        jnp.asarray(inverse),
        jnp.asarray(taps),
    )


def solution(mesh):
    in_specs = (P(("row", "ang"), None), P("ang"), P("ang", None), P(), P())
    out_specs = P(("row", "ang"), None)
    return jax.shard_map(
        per_device, mesh=mesh, in_specs=in_specs, out_specs=out_specs, check_vma=False
    )
```

```python
import functools
import math

import jax
import jax.numpy as jnp
import ml_dtypes
import numpy as np
from jax import lax
from jax.experimental import pallas as pl
from jax.experimental.pallas import tpu as pltpu
from jax.sharding import PartitionSpec as P

W = 16384
RAMP_HALF = 128
JITTER = 64
SHRINK_SCALE = 1.0
EPSILON = 1e-06
LANES = 128
SPAN = 2048
SHARED = 0.625

F32 = jnp.float32
BF16 = jnp.bfloat16


def split_np(table):
    high = table.astype(ml_dtypes.bfloat16)
    low = (table - high.astype(np.float64)).astype(ml_dtypes.bfloat16)
    return high, low


def freq_rows(angles):
    return -(-(angles // 2 + 1) // 8) * 8


def forward_table(angles, devices, fold):
    rows = freq_rows(angles)
    here = angles // devices
    k = np.arange(rows)[:, None]
    a = np.arange(angles)[None, :]
    phase = 2.0 * np.pi * ((k * a) % angles) / angles
    keep = (k <= angles // 2).astype(np.float64)
    table = np.concatenate([np.cos(phase) * keep, -np.sin(phase) * keep], axis=0)
    placed = np.zeros((fold, 2 * rows, devices, fold, here))
    for part in range(fold):
        placed[part, :, :, part, :] = table.reshape(2 * rows, devices, here)
    high, low = split_np(placed.reshape(fold, 2 * rows, devices * fold * here))
    return np.concatenate([high, low], axis=1)


def inverse_table(angles, devices, fold):
    rows = freq_rows(angles)
    k = np.arange(rows)[None, :]
    a = np.arange(angles)[:, None]
    phase = 2.0 * np.pi * ((k * a) % angles) / angles
    twice = np.where((k == 0) | (2 * k == angles), 1.0, 2.0) * (k <= angles // 2)
    weight = twice * np.exp(-np.minimum(k, angles - k) / (angles // 8)) / angles
    table = np.concatenate([np.cos(phase) * weight, -np.sin(phase) * weight], axis=1)
    high, low = split_np(table)
    table = np.concatenate([high, high, low], axis=1)
    if fold == 1:
        return table[None]
    here = angles // devices
    shared = np.kron(np.eye(devices), np.ones((here, here))) * (SHARED / here)
    placed = np.zeros((fold, angles, devices, fold, here))
    for part in range(fold):
        placed[part, :, :, part, :] = -shared.reshape(angles, devices, here)
    placed = placed.reshape(fold, angles, devices * fold * here).astype(ml_dtypes.bfloat16)
    return np.concatenate([np.broadcast_to(table, (fold,) + table.shape), placed], axis=2)


def ramp_table():
    i = np.arange(3 * LANES)[:, None] - LANES
    n = np.arange(LANES)[None, :] - i
    safe = np.where(n == 0, 1, n).astype(np.float64)
    taps = np.where(n % 2 != 0, -1.0 / (np.pi * np.pi * safe * safe), 0.0)
    taps = np.where(n == 0, 0.25, taps)
    taps = np.where(np.abs(n) <= RAMP_HALF, taps, 0.0)
    high, low = split_np(taps)
    return np.stack([high, low])


def dot(left, right):
    return jnp.dot(left, right, preferred_element_type=F32)


def dot_nt(left, right):
    return lax.dot_general(left, right, (((1,), (1,)), ((), ())), preferred_element_type=F32)


def halves(x):
    high = x.astype(BF16)
    return high, (x - high.astype(F32)).astype(BF16)


def thirds(x):
    high = x.astype(BF16).astype(F32)
    rest = x - high
    mid = rest.astype(BF16).astype(F32)
    low = rest - mid
    return jnp.concatenate([high, mid, low, jnp.zeros_like(x)], axis=0).astype(BF16)


def iota(shape, axis):
    return lax.broadcasted_iota(jnp.int32, shape, axis)


def loop(count, body):
    if count <= 8:
        for step in range(count):
            body(step)
    else:

        def run(step, carry):
            body(step)
            return carry

        lax.fori_loop(0, count, run, 0)


def kernel(
    cfg,
    raw_ref,
    dest_ref,
    offset_ref,
    ramp_ref,
    width_ref,
    fwd_hbm,
    inv_hbm,
    taps_hbm,
    out_ref,
    rows_send,
    rows_recv,
    grid_ref,
    sum_ref,
    weight_ref,
    proj_ref,
    cent_send,
    cent_recv,
    spec_ref,
    level_send,
    level_recv,
    stripe_send,
    stripe_recv,
    ids_send,
    ids_recv,
    fwd_ref,
    inv_ref,
    taps_ref,
    table_sem,
    send_sem,
    recv_sem,
):
    devices, angles_here, tiles, tile_width, mods, fold = cfg
    angles = devices * angles_here
    cols = W // devices
    half = cols // fold
    rows = freq_rows(angles)
    step_cols = (W - tile_width) // (tiles - 1)
    window = tile_width + 2 * LANES
    blocks = angles_here * tiles
    me = lax.axis_index("ang")

    def ring_at(hop):
        return lax.rem(me + hop, devices)

    def peer_at(hop):
        if devices & (devices - 1):
            return ring_at(hop)
        mask = devices - hop
        peer = 0
        bit = 1
        while bit < devices:
            peer = peer + bit * lax.rem(lax.div(me, bit) + mask // bit, 2)
            bit *= 2
        return peer

    barrier = pltpu.get_barrier_semaphore()

    def greet(step):
        pl.semaphore_signal(
            barrier,
            inc=1,
            device_id={"ang": peer_at(step + 1)},
            device_id_type=pl.DeviceIdType.MESH,
        )

    loop(devices - 1, greet)
    fetch_fwd = pltpu.make_async_copy(fwd_hbm, fwd_ref, table_sem.at[0])
    fetch_inv = pltpu.make_async_copy(inv_hbm, inv_ref, table_sem.at[1])
    fetch_taps = pltpu.make_async_copy(taps_hbm, taps_ref, table_sem.at[2])
    fetch_fwd.start()
    fetch_inv.start()
    fetch_taps.start()

    def remote(phase, src, dst, slot, peer):
        return pltpu.make_async_remote_copy(
            src_ref=src,
            dst_ref=dst,
            send_sem=send_sem.at[phase, peer],
            recv_sem=recv_sem.at[phase, slot],
            device_id={"ang": peer},
            device_id_type=pl.DeviceIdType.MESH,
        )

    def finish(phase, send_of, recv_of):
        def body(step):
            peer = peer_at(step + 1)
            copy = remote(phase, send_of(peer), recv_of(peer), peer, peer)
            copy.wait_recv()
            copy.wait_send()

        loop(devices - 1, body)

    cap = -(-blocks // devices)
    slab = 16
    chunks = tile_width // LANES
    extra = chunks - cap
    slots = devices * slab
    dest_row = dest_ref[...].astype(F32)
    source_row = iota((blocks, blocks), 1)
    source_col = iota((blocks, blocks), 0)

    def turned(values):
        return jnp.sum(jnp.where(source_row == source_col, values, 0.0), axis=1, keepdims=True)

    owner_row = jnp.floor((dest_row + 0.5) * (1.0 / blocks))
    owner_col = turned(owner_row)
    earlier = (owner_col == owner_row) & (source_col < source_row)
    rank_row = jnp.sum(jnp.where(earlier, 1.0, 0.0), axis=0, keepdims=True)
    rank_col = turned(rank_row)
    place_row = dest_row - owner_row * blocks + 1.0
    slot = iota((slots, 1), 0).astype(F32)

    def one_hot(left, right):
        return jnp.where(left == right, 1.0, 0.0).astype(BF16)

    direct = one_hot(slot, owner_row * slab + rank_row)
    packed = dot(direct, raw_ref[:, : cap * LANES])
    keeps = [
        jnp.where(jnp.broadcast_to(rank_col, (blocks, LANES)) == j, 1.0, 0.0).astype(BF16)
        for j in range(cap)
    ]
    for e in range(extra):
        chunk = raw_ref[:, (cap + e) * LANES : (cap + e + 1) * LANES]
        masked = jnp.concatenate([chunk * keep for keep in keeps], axis=1)
        packed = packed + dot(one_hot(slot, owner_row * slab + (cap + e)), masked)
    rows_send[...] = packed.astype(BF16).reshape(devices, slab, cap * LANES)
    group = LANES // slab
    groups = -(-devices // group)
    lane_at = iota((blocks, LANES), 1).astype(F32)
    first_lane = (lax.rem(me, group) * slab).astype(F32)
    at_rank = one_hot(lane_at, rank_col + first_lane)
    to_owner = jnp.where(iota((devices, blocks), 0).astype(F32) == owner_row, place_row, 0.0)
    ids_send[...] = dot(to_owner.astype(BF16), at_rank).reshape(devices, 1, LANES)

    pl.semaphore_wait(barrier, devices - 1)

    def send_rows(step):
        peer = peer_at(step + 1)
        remote(4, ids_send.at[peer], ids_recv.at[me], me, peer).start()
        remote(0, rows_send.at[peer], rows_recv.at[me], me, peer).start()

    loop(devices - 1, send_rows)
    rows_recv[me] = rows_send[me]
    ids_recv[me] = ids_send[me]
    finish(4, lambda p: ids_send.at[p], lambda p: ids_recv.at[p])
    finish(0, lambda p: rows_send.at[p], lambda p: rows_recv.at[p])

    ids = [
        jnp.sum(ids_recv[g * group : min((g + 1) * group, devices)], axis=0) for g in range(groups)
    ]
    ids = ids[0] if groups == 1 else jnp.concatenate(ids, axis=1)
    ids = jnp.broadcast_to(ids[:, :slots], (8, slots))
    row = iota((blocks, 1), 0).astype(F32)
    tile_of = jnp.floor((row + 0.5) * (1.0 / angles_here))
    wanted = (row - tile_of * angles_here) * tiles + tile_of + 1.0
    lead = rows_recv[...].reshape(slots, cap * LANES)
    grid_ref[:, : cap * LANES] = dot(one_hot(wanted, ids[0:1]), lead)
    if extra:
        within = iota((8, slots), 1) & (slab - 1)
        turns = [pltpu.roll(ids, n, 1) if n else ids for n in range(slab)]
        wanted_at = jnp.concatenate(
            [jnp.where(within[0:1] == cap + e, wanted, -1.0) for e in range(extra)], axis=0
        )
        rest = jnp.zeros((extra * blocks, LANES), F32)
        for j in range(cap):
            ids_j = jnp.zeros((8, slots), F32)
            for e in range(extra):
                ids_j = jnp.where(within == cap + e, turns[cap + e - j], ids_j)
            part = rows_recv[:, :, j * LANES : (j + 1) * LANES].reshape(slots, LANES)
            rest = rest + dot(one_hot(wanted_at, ids_j[0:1]), part)
        for e in range(extra):
            at = (cap + e) * LANES
            grid_ref[:, at : at + LANES] = rest[e * blocks : (e + 1) * blocks]

    fetch_fwd.wait()
    fetch_inv.wait()
    fetch_taps.wait()

    sum_ref[...] = jnp.zeros_like(sum_ref)
    weight_ref[...] = jnp.zeros_like(weight_ref)
    inverse_ramp = 1.0 / ramp_ref[...].astype(F32)
    lane = iota((angles_here, window), 1)
    for tile in range(tiles):
        base = tile * step_cols
        shift = jnp.broadcast_to(
            offset_ref[:, tile : tile + 1] - (base - LANES), (angles_here, window)
        )
        piece = jnp.concatenate(
            [
                grid_ref[tile * angles_here : (tile + 1) * angles_here, :],
                jnp.zeros((angles_here, 2 * LANES), F32),
            ],
            axis=1,
        )
        for bit in range(8):
            moved = pltpu.roll(piece, 1 << bit, 1)
            piece = jnp.where((shift & (1 << bit)) != 0, moved, piece)
        x = lane - shift
        edge = (jnp.minimum(x, tile_width - 1 - x) + 1).astype(F32)
        feather = jnp.minimum(1.0, edge * inverse_ramp[:, tile : tile + 1])
        feather = jnp.maximum(feather, 0.0)
        sum_ref[:, base : base + window] += feather * piece
        weight_ref[:, base : base + window] += feather

    wide = width_ref[...].astype(F32)
    upper = iota((mods, wide.shape[1]), 1)
    lower = iota((mods, wide.shape[1]), 0)
    bounds = jnp.sum(jnp.where(upper <= lower, wide, 0.0), axis=1, keepdims=True)
    starts = jnp.sum(jnp.where(upper < lower, wide, 0.0), axis=1, keepdims=True)
    on_diagonal = iota((mods, mods), 0) == iota((mods, mods), 1)
    safe_wide = jnp.sum(jnp.where(on_diagonal, bounds - starts, 0.0), axis=0, keepdims=True)
    safe_wide = jnp.maximum(safe_wide, 1.0)

    def member(first, count):
        c = (iota((mods, count), 1) + first).astype(F32)
        inside = (c >= starts) & (c < bounds)
        return jnp.where(inside, 1.0, 0.0).astype(BF16)

    def project(step, total):
        at = step * SPAN
        behind = at + LANES
        blended = sum_ref[:, pl.ds(behind, SPAN)] / weight_ref[:, pl.ds(behind, SPAN)]
        projection = -jnp.log(blended)
        proj_ref[:, pl.ds(at, SPAN)] = projection
        return total + dot_nt(thirds(projection), member(at, SPAN))

    total = jnp.zeros((4 * angles_here, mods), F32)
    for step in range(W // SPAN):
        total = project(step, total)

    def gather_thirds(stack):
        a = angles_here
        return stack[0:a] + stack[a : 2 * a] + stack[2 * a : 3 * a]

    mean = thirds(gather_thirds(total) / safe_wide)

    def centered_slab(owner):
        at = pl.multiple_of(owner * cols, LANES)
        flat = proj_ref[:, pl.ds(at, cols)] - gather_thirds(dot(mean, member(at, cols)))
        if fold > 1:
            flat = jnp.concatenate([flat[:, i * half : (i + 1) * half] for i in range(fold)], axis=0)
        return flat.astype(cent_send.dtype)

    def send_centered(step):
        peer = peer_at(step + 1)
        cent_send[peer] = centered_slab(peer)
        remote(1, cent_send.at[peer], cent_recv.at[me], me, peer).start()

    loop(devices - 1, send_centered)
    cent_send[me] = centered_slab(me)
    cent_recv[me] = cent_send[me]

    if fold > 1:
        shared_row = iota((fold * angles_here, fold * angles_here), 0)
        shared_col = iota((fold * angles_here, fold * angles_here), 1)
        same = (shared_row // angles_here) == (shared_col // angles_here)
        shared_table = jnp.where(same, SHARED / angles_here, 0.0).astype(BF16)

        def take_shared(owner):
            at = pl.multiple_of(owner * cols, LANES)
            shared = dot(shared_table, cent_send[owner])
            shared = jnp.concatenate(
                [shared[i * angles_here : (i + 1) * angles_here] for i in range(fold)], axis=1
            )
            proj_ref[:, pl.ds(at, cols)] = proj_ref[:, pl.ds(at, cols)] - shared

        loop(devices, take_shared)

    finish(1, lambda p: cent_send.at[p], lambda p: cent_recv.at[p])

    signal = cent_recv[...].reshape(devices * fold * angles_here, half).astype(BF16)
    k = iota((rows, 1), 0)
    count_of = jnp.where((k == 0) | (2 * k == angles), 1.0, 2.0)
    count_of = jnp.where(2 * k <= angles, count_of, 0.0)
    mine = pl.multiple_of(me * cols, LANES)
    sums = jnp.zeros((4 * 8, mods), F32)
    for part in range(fold):
        wide_spec = dot(fwd_ref[part], signal)
        spectrum = wide_spec[: 2 * rows] + wide_spec[2 * rows :]
        spec_ref[part] = spectrum
        magnitude = jnp.sqrt(
            spectrum[:rows] * spectrum[:rows] + spectrum[rows:] * spectrum[rows:]
        )
        over_k = jnp.sum(magnitude * count_of, axis=0, keepdims=True)
        first_row = jnp.where(iota((8, half), 0) == 0, over_k, 0.0)
        sums = sums + dot_nt(thirds(first_row), member(mine + part * half, half))
    level_send[...] = jnp.zeros_like(level_send)
    level_send[:, 0:mods] = sums[0:8] + sums[8:16] + sums[16:24]

    def send_level(step):
        peer = peer_at(step + 1)
        remote(2, level_send, level_recv.at[me], me, peer).start()

    loop(devices - 1, send_level)
    level_recv[me] = level_send[...]
    finish(2, lambda p: level_send, lambda p: level_recv.at[p])
    everything = jnp.sum(level_recv[...], axis=0)[:, 0:mods]
    level = SHRINK_SCALE * (everything / (angles * safe_wide) + EPSILON)
    level_parts = thirds(jnp.where(iota((8, mods), 0) == 0, level, 0.0))

    residual = []
    for part in range(fold):
        spread = dot(level_parts, member(mine + part * half, half))
        level_col = spread[0:1] + spread[8:9] + spread[16:17]
        spectrum = spec_ref[part]
        magnitude = jnp.sqrt(
            spectrum[:rows] * spectrum[:rows] + spectrum[rows:] * spectrum[rows:]
        )
        factor = jnp.maximum(magnitude - level_col, 0.0) / jnp.maximum(magnitude, level_col)
        shrunk = jnp.concatenate([spectrum[:rows] * factor, spectrum[rows:] * factor], axis=0)
        high, low = halves(shrunk)
        parts = [high, low, high] + ([signal] if fold > 1 else [])
        stripe = dot(inv_ref[part], jnp.concatenate(parts, axis=0))
        residual.append(stripe.reshape(devices, angles_here, half))
    stripe_send[...] = jnp.concatenate(residual, axis=1).astype(stripe_send.dtype)

    def send_stripe(step):
        peer = ring_at(step + 1)
        remote(3, stripe_send.at[peer], stripe_recv.at[me], me, peer).start()

    loop(devices - 1, send_stripe)
    stripe_recv[me] = stripe_send[me]

    sum_ref[:, 0:LANES] = jnp.zeros((angles_here, LANES), F32)
    sum_ref[:, W + LANES :] = jnp.zeros((angles_here, LANES), F32)
    lane_blocks = cols // LANES

    def clean(owner):
        at = pl.multiple_of(owner * cols, LANES)
        behind = pl.multiple_of(owner * cols + LANES, LANES)
        rest = stripe_recv[owner].astype(F32)
        rest = jnp.concatenate(
            [rest[i * angles_here : (i + 1) * angles_here] for i in range(fold)], axis=1
        )
        sum_ref[:, pl.ds(behind, cols)] = proj_ref[:, pl.ds(at, cols)] - rest

    def ramp(group):
        at = pl.multiple_of(group * cols, LANES)
        flat = sum_ref[:, pl.ds(at, cols + 2 * LANES)]
        stack = jnp.concatenate(
            [flat[:, b * LANES : (b + 1) * LANES] for b in range(lane_blocks + 2)], axis=0
        )
        n = lane_blocks * angles_here
        near = jnp.concatenate(
            [stack[s * angles_here : s * angles_here + n] for s in range(3)], axis=1
        )
        high, low = halves(near)
        done = dot(high, taps_ref[0]) + dot(low, taps_ref[0]) + dot(high, taps_ref[1])
        out_ref[:, pl.ds(at, cols)] = jnp.concatenate(
            [done[b * angles_here : (b + 1) * angles_here] for b in range(lane_blocks)], axis=1
        )

    clean(me)

    def below(hop):
        return lax.rem(me + devices - hop, devices)

    def take(hop):
        owner = below(hop)
        remote(3, stripe_send.at[owner], stripe_recv.at[owner], owner, owner).wait_recv()
        clean(owner)

    take(1)

    def advance(step):
        take(step + 2)
        ramp(below(step + 1))

    loop(devices - 2, advance)
    ramp(below(devices - 1))
    ramp(me)

    def sent(step):
        peer = ring_at(step + 1)
        remote(3, stripe_send.at[peer], stripe_recv.at[peer], peer, peer).wait_send()

    loop(devices - 1, sent)


def pack_plan(cap, chunks, first, need):
    split = next(
        (n for n in range(1, cap) if n + (chunks - cap) * n // cap >= need), 0
    )
    run = list(range(first, first + need))
    others = [b for b in range(chunks) if b not in run]
    direct = run[:split] + others[: cap - split]
    cells = {}
    n = 0
    early = (chunks - cap) * split
    for block in run[split:] + others[cap - split :]:
        for rank in range(cap):
            if n < early:
                cells[cap + n // split, n % split] = (rank, block)
            else:
                late = n - early
                cells[cap + late // (cap - split), split + late % (cap - split)] = (rank, block)
            n += 1
    return split, direct, cells


def fast_plan(devices, angles_here, tiles, tile_width, mods, modules):
    cols = W // devices
    step_cols = (W - tile_width) // (tiles - 1)
    cap = -(-angles_here * tiles // devices)
    chunks = tile_width // LANES
    if cols % (4 * LANES) or step_cols % LANES or tile_width % LANES:
        return None
    mine = cols // (2 * LANES)
    per_step = step_cols // LANES
    first = -(-(tile_width - step_cols + JITTER) // LANES) + 1
    back = per_step - first - mine
    fits = (
        tiles == devices + 1
        and angles_here == 8
        and angles_here * mods == LANES
        and modules <= 8
        and chunks == 16
        and devices * chunks == LANES
        and 1 < cap < chunks
        and back >= 1
        and tile_width < 2 * step_cols - 2 * JITTER
        and (first + mine) * LANES <= step_cols - JITTER
    )
    if not fits:
        return None
    split, direct, cells = pack_plan(cap, chunks, first - 1, mine + 2)
    if not split:
        return None
    alone = {t * per_step + first + i for t in range(tiles) for i in range(mine)}
    early, late = [], []
    for p in range(devices):
        window = range(2 * p * mine, 2 * (p + 1) * mine)
        early.append([b for b in window if b in alone][:mine])
        late.append([b for b in window if b not in early[p]])
    if any(len(run) != mine for run in early):
        return None
    reach = -(-2 * W // modules // cols)
    return cap, split, direct, cells, first, back, mine, early, late, reach


def fast_kernel(
    cfg,
    plan,
    raw_hbm,
    dest_hbm,
    offset_hbm,
    ramp_hbm,
    width_hbm,
    fwd_hbm,
    inv_hbm,
    taps_hbm,
    shared_hbm,
    out_ref,
    raw_ref,
    dest_ref,
    offset_ref,
    ramp_ref,
    width_ref,
    rows_send_a,
    rows_recv_a,
    rows_send_b,
    rows_recv_b,
    ids_send,
    ids_recv,
    grid_ref,
    clean_ref,
    proj_ref,
    hot_ref,
    weight_ref,
    member_ref,
    member_own_ref,
    inside_ref,
    inside_own_ref,
    cent_send_a,
    cent_recv_a,
    cent_send_b,
    cent_recv_b,
    diff_send,
    diff_recv,
    spec_ref,
    size_ref,
    level_send,
    level_recv,
    stripe_send_a,
    stripe_recv_a,
    stripe_send_b,
    stripe_recv_b,
    known_ref,
    fwd_ref,
    inv_ref,
    taps_ref,
    shared_ref,
    table_sem,
    send_sem,
    recv_sem,
):
    devices, angles_here, tiles, tile_width, mods, fold = cfg
    cap, split, direct_blocks, cells, first, back, mine, early, late, reach = plan
    angles = devices * angles_here
    rows = freq_rows(angles)
    step_cols = (W - tile_width) // (tiles - 1)
    blocks = angles_here * tiles
    chunks = tile_width // LANES
    slab = chunks
    slots = devices * slab
    width = mine * LANES
    half = width // 2
    me = lax.axis_index("ang")
    ROWS_A, ROWS_B, IDS, CENT_A, CENT_B, DIFF, LEVEL, STRIPE_A, STRIPE_B = range(9)

    def peer_at(hop):
        mask = devices - hop
        peer = 0
        bit = 1
        while bit < devices:
            peer = peer + bit * lax.rem(lax.div(me, bit) + mask // bit, 2)
            bit *= 2
        return peer

    peers = [peer_at(hop) for hop in range(1, devices)]
    barrier = pltpu.get_barrier_semaphore()
    for peer in peers:
        pl.semaphore_signal(
            barrier, inc=1, device_id={"ang": peer}, device_id_type=pl.DeviceIdType.MESH
        )
    fetched = [
        (dest_hbm, dest_ref),
        (raw_hbm, raw_ref),
        (width_hbm, width_ref),
        (offset_hbm, offset_ref),
        (ramp_hbm, ramp_ref),
        (fwd_hbm, fwd_ref),
        (inv_hbm, inv_ref),
        (taps_hbm, taps_ref),
        (shared_hbm, shared_ref),
    ]
    fetches = [
        pltpu.make_async_copy(src, dst, table_sem.at[i]) for i, (src, dst) in enumerate(fetched)
    ]
    for fetch in fetches:
        fetch.start()

    def remote(phase, src, dst, slot, peer):
        return pltpu.make_async_remote_copy(
            src_ref=src,
            dst_ref=dst,
            send_sem=send_sem.at[phase, peer],
            recv_sem=recv_sem.at[phase, slot],
            device_id={"ang": peer},
            device_id_type=pl.DeviceIdType.MESH,
        )

    def send_all(phase, send_ref, recv_ref):
        for peer in peers:
            remote(phase, send_ref.at[peer], recv_ref.at[me], me, peer).start()

    def wait_recv(phase, send_ref, recv_ref):
        for peer in peers:
            remote(phase, send_ref.at[peer], recv_ref.at[peer], peer, peer).wait_recv()

    def wait_send(phase, send_ref, recv_ref):
        for peer in peers:
            remote(phase, send_ref.at[peer], recv_ref.at[peer], peer, peer).wait_send()

    fetches[0].wait()
    dest_row = dest_ref[...].astype(F32)
    source_row = iota((blocks, blocks), 1)
    source_col = iota((blocks, blocks), 0)

    def turned(values):
        return jnp.sum(jnp.where(source_row == source_col, values, 0.0), axis=1, keepdims=True)

    owner_row = jnp.floor((dest_row + 0.5) * (1.0 / blocks))
    owner_col = turned(owner_row)
    earlier = (owner_col == owner_row) & (source_col < source_row)
    rank_row = jnp.sum(jnp.where(earlier, 1.0, 0.0), axis=0, keepdims=True)
    rank_col = turned(rank_row)
    place_row = dest_row - owner_row * blocks + 1.0
    slot = iota((slots, 1), 0).astype(F32)

    def one_hot(left, right):
        return jnp.where(left == right, 1.0, 0.0).astype(BF16)

    direct = one_hot(slot, owner_row * slab + rank_row)
    keeps = [
        jnp.where(jnp.broadcast_to(rank_col, (blocks, LANES)) == j, 1.0, 0.0).astype(BF16)
        for j in range(cap)
    ]

    def lane_block(b):
        return raw_ref[:, b * LANES : (b + 1) * LANES]

    def pack(columns):
        packed = dot(direct, jnp.concatenate([lane_block(direct_blocks[k]) for k in columns], axis=1))
        for r in range(cap, slab):
            masked = jnp.concatenate(
                [lane_block(cells[r, k][1]) * keeps[cells[r, k][0]] for k in columns], axis=1
            )
            packed = packed + dot(one_hot(slot, owner_row * slab + r), masked)
        return packed.astype(BF16).reshape(devices, slab, len(columns) * LANES)

    columns_a = range(split)
    columns_b = range(split, cap)
    lane_at = iota((blocks, LANES), 1).astype(F32)
    first_lane = (me * slab).astype(F32)
    at_rank = one_hot(lane_at, rank_col + first_lane)
    to_owner = jnp.where(iota((devices, blocks), 0).astype(F32) == owner_row, place_row, 0.0)
    ids_send[...] = dot(to_owner.astype(BF16), at_rank).reshape(devices, 1, LANES)
    fetches[1].wait()
    rows_send_a[...] = pack(columns_a)

    pl.semaphore_wait(barrier, devices - 1)

    send_all(IDS, ids_send, ids_recv)
    send_all(ROWS_A, rows_send_a, rows_recv_a)
    rows_send_b[...] = pack(columns_b)
    send_all(ROWS_B, rows_send_b, rows_recv_b)
    rows_recv_a[me] = rows_send_a[me]
    rows_recv_b[me] = rows_send_b[me]
    ids_recv[me] = ids_send[me]

    for fetch in fetches[2:5]:
        fetch.wait()
    wide = width_ref[...].astype(F32)
    upper = iota((mods, wide.shape[1]), 1)
    lower = iota((mods, wide.shape[1]), 0)
    bounds = jnp.sum(jnp.where(upper <= lower, wide, 0.0), axis=1, keepdims=True)
    starts = jnp.sum(jnp.where(upper < lower, wide, 0.0), axis=1, keepdims=True)
    wide_column = jnp.maximum((bounds - starts)[0:8], 1.0)
    bounds = jnp.broadcast_to(bounds, (mods, LANES))
    starts = jnp.broadcast_to(starts, (mods, LANES))
    lane = iota((mods, LANES), 1).astype(F32)
    for b in range(W // LANES):
        c = lane + float(b * LANES)
        inside = (c >= starts) & (c < bounds)
        inside = jnp.where(inside, 1.0, 0.0)
        member_ref[:, b * LANES : (b + 1) * LANES] = inside.astype(BF16)
        inside_ref[:, b * LANES : (b + 1) * LANES] = inside[0:8]
    for p in range(devices):
        for i, b in enumerate(early[p] + late[p]):
            at = i * LANES
            member_own_ref[p, :, at : at + LANES] = member_ref[:, b * LANES : (b + 1) * LANES]
            inside_own_ref[p, :, at : at + LANES] = inside_ref[:, b * LANES : (b + 1) * LANES]
    held = range(width_ref.shape[1])

    def inside_early(m, p):
        return inside_own_ref[p, m : m + 1, :width]

    def inside_late(m, p):
        return inside_own_ref[p, m : m + 1, width:]

    def narrowed(x):
        pieces = [x[:, i * LANES : (i + 1) * LANES] for i in range(mine)]
        while len(pieces) > 1:
            odd = pieces[len(pieces) // 2 * 2 :]
            pieces = [x + y for x, y in zip(pieces[::2], pieces[1::2])] + odd
        return pieces[0]

    def module_sums(flats, inside_of):
        sums = []
        for m in held:
            total = narrowed(flats[0] * inside_of(m, 0))
            for p in range(1, devices):
                total = total + narrowed(flats[p] * inside_of(m, p))
            sums.append(jnp.sum(total, axis=1, keepdims=True))
        return sums

    def less_mean(flat, means, inside_of, p):
        for m in held:
            flat = flat - means[m] * inside_of(m, p)
        flat = jnp.concatenate([flat[:, :half], flat[:, half:]], axis=0)
        return flat.astype(BF16)

    blank_row = jnp.ones((1, width), F32)
    counts = module_sums([blank_row] * devices, inside_early)
    scales_a = [1.0 / jnp.maximum(count, 1.0) for count in counts]
    scales = [
        1.0 / jnp.maximum(jnp.sum(width_ref[0:1, m : m + 1], axis=1, keepdims=True).astype(F32), 1.0)
        for m in held
    ]

    row = iota((blocks, 1), 0).astype(F32)
    tile_of = jnp.floor((row + 0.5) * (1.0 / angles_here))
    wanted = (row - tile_of * angles_here) * tiles + tile_of + 1.0
    wanted = jnp.broadcast_to(wanted, (blocks, LANES))
    within = iota((8, slots), 1) & (slab - 1)

    wait_recv(IDS, ids_send, ids_recv)
    ids = jnp.broadcast_to(jnp.sum(ids_recv[...], axis=0), (8, slots))
    turns = [pltpu.roll(ids, n, 1) if n else ids for n in range(slab)]

    def match(ids_row):
        return jnp.where(wanted == jnp.broadcast_to(ids_row[0:1], (blocks, LANES)), 1.0, 0.0)

    held_in = {k: sorted({cells[r, k][1] for r in range(cap, slab)}) for k in range(cap)}
    padded = -(-blocks // 16) * 16
    direct_ref = hot_ref.at[:blocks]
    direct_ref[...] = match(ids).astype(BF16)
    hot_at = {}
    top = padded
    for k in range(cap):
        hot = []
        for b in held_in[k]:
            ids_b = jnp.zeros((8, slots), F32)
            for r in range(cap, slab):
                if cells[r, k][1] == b:
                    ids_b = jnp.where(within == r, turns[r - cells[r, k][0]], ids_b)
            hot.append(match(ids_b))
        count = len(hot) * blocks
        hot_at[k] = (top, count)
        hot_ref[top : top + count] = jnp.concatenate(hot, axis=0).astype(BF16)
        top += -(-count // 16) * 16

    begun = set()

    def unpack(columns, recv_ref):
        lead = recv_ref[...].reshape(slots, len(columns) * LANES)
        flat = dot(direct_ref[...], lead)
        for at, k in enumerate(columns):
            b = direct_blocks[k]
            grid_ref[:, b * LANES : (b + 1) * LANES] = flat[:, at * LANES : (at + 1) * LANES]
        sums = {}
        for at, k in enumerate(columns):
            start, count = hot_at[k]
            part = dot(hot_ref[start : start + count], lead[:, at * LANES : (at + 1) * LANES])
            for i, b in enumerate(held_in[k]):
                piece = part[i * blocks : (i + 1) * blocks]
                sums[b] = sums[b] + piece if b in sums else piece
        for b, value in sums.items():
            at = b * LANES
            if b in begun:
                value = value + grid_ref[:, at : at + LANES]
            begun.add(b)
            grid_ref[:, at : at + LANES] = value

    def shift_of(tile):
        ahead = LANES - (offset_ref[:, tile : tile + 1] - tile * step_cols)
        return jnp.broadcast_to(ahead, (angles_here, LANES))

    lane_here = iota((angles_here, LANES), 1)

    def shifted(pieces, ahead, wanted_blocks):
        far = (ahead & LANES) != 0
        steps = [1 << n for n in range(LANES.bit_length() - 1)]
        masks = [(ahead & step) != 0 for step in steps]
        stay = lane_here < LANES - (ahead & (LANES - 1))
        blank = jnp.zeros((angles_here, LANES), F32)
        turned_at = {}
        for i in sorted({i + n for i in wanted_blocks for n in (0, 1)}):
            near_piece, far_piece = pieces.get(i), pieces.get(i + 1)
            if near_piece is None and far_piece is None:
                turned_at[i] = blank
                continue
            x = jnp.where(
                far,
                blank if far_piece is None else far_piece,
                blank if near_piece is None else near_piece,
            )
            for step, mask in zip(steps, masks):
                x = jnp.where(mask, pltpu.roll(x, LANES - step, 1), x)
            turned_at[i] = x
        return {i: jnp.where(stay, turned_at[i], turned_at[i + 1]) for i in wanted_blocks}

    def tile_block(tile, b):
        return grid_ref[tile * angles_here : (tile + 1) * angles_here, b * LANES : (b + 1) * LANES]

    def tile_blocks(tile, start, stop, at):
        return {at + b - start: tile_block(tile, b) for b in range(start, stop)}

    shifts = [shift_of(t) for t in range(tiles)]
    gap = back + first
    inverse_ramp = 1.0 / ramp_ref[...].astype(F32)
    left_at = step_cols // LANES - back - 1
    per_step = step_cols // LANES
    left_end = back - (-(tile_width - step_cols + JITTER) // LANES)
    right_start = back - 1 - (JITTER - 1) // LANES
    lane_float = lane_here.astype(F32)
    shared_blocks = range(right_start, left_end)
    for g in range(1, tiles):
        ahead_left = lane_float + shifts[g - 1].astype(F32)
        ahead_right = lane_float + shifts[g].astype(F32)
        for n, i in enumerate(shared_blocks):
            till = float(tile_width - (left_at + i) * LANES)
            since = float((i - back - 1) * LANES + 1)
            feather_left = (till - ahead_left) * inverse_ramp[:, g - 1 : g]
            feather_right = (ahead_right + since) * inverse_ramp[:, g : g + 1]
            feather_left = jnp.maximum(jnp.minimum(1.0, feather_left), 0.0)
            feather_right = jnp.maximum(jnp.minimum(1.0, feather_right), 0.0)
            both = 1.0 / (feather_left + feather_right)
            weight_ref[0, g - 1, :, n * LANES : (n + 1) * LANES] = feather_left * both
            weight_ref[1, g - 1, :, n * LANES : (n + 1) * LANES] = feather_right * both

    wait_recv(ROWS_A, rows_send_a, rows_recv_a)
    unpack(columns_a, rows_recv_a)
    values = {}
    for t in range(tiles):
        if t in (0, tiles - 1):
            value = {i: tile_block(t, first + i) for i in range(mine)}
        else:
            pieces = tile_blocks(t, first - 1, first + mine + 1, 0)
            value = shifted(pieces, shifts[t], range(mine))
        for i in range(mine):
            values[t * (step_cols // LANES) + first + i] = value[i]

    def project(block_lists):
        flats = []
        for block_list in block_lists:
            flat = -jnp.log(jnp.concatenate([values[b] for b in block_list], axis=1))
            flats.append(flat)
            for i, b in enumerate(block_list):
                proj_ref[:, b * LANES : (b + 1) * LANES] = flat[:, i * LANES : (i + 1) * LANES]
        return flats

    flats_a = project(early)
    sums_a = module_sums(flats_a, inside_early)
    means_a = [sums_a[m] * scales_a[m] for m in held]
    for p in range(devices):
        cent_send_a[p] = less_mean(flats_a[p], means_a, inside_early, p)
    level_recv[...] = jnp.zeros_like(level_recv)
    send_all(CENT_A, cent_send_a, cent_recv_a)
    cent_recv_a[me] = cent_send_a[me]

    wait_recv(ROWS_B, rows_send_b, rows_recv_b)
    unpack(columns_b, rows_recv_b)
    for b in range(first):
        values[b] = tile_block(0, b)
    for g in range(1, tiles):
        left_pieces = tile_blocks(g - 1, left_at, chunks, 0)
        right_pieces = tile_blocks(g, 0, gap + 1 - back, back + 1)
        if g == 1:
            left = {i: left_pieces[i + 1] for i in range(left_end) if i + 1 in left_pieces}
        else:
            left = shifted(left_pieces, shifts[g - 1], range(left_end))
        if g == tiles - 1:
            right = {i: right_pieces[i + 1] for i in range(back, gap)}
        else:
            right = shifted(right_pieces, shifts[g], range(right_start, gap))
        for i in range(gap):
            if i not in left or i not in right:
                values[g * per_step - back + i] = left[i] if i in left else right[i]
                continue
            at = (i - right_start) * LANES
            values[g * per_step - back + i] = (
                weight_ref[0, g - 1, :, at : at + LANES] * left[i]
                + weight_ref[1, g - 1, :, at : at + LANES] * right[i]
            )
    for b in range(first + mine, chunks):
        values[(tiles - 1) * per_step + b] = tile_block(tiles - 1, b)
    flats = project(late)
    sums_b = module_sums(flats, inside_late)
    means = [(sums_a[m] + sums_b[m]) * scales[m] for m in held]
    lane_of = iota((angles_here, LANES), 1)
    own = (lane_of // mods) == iota((angles_here, LANES), 0)
    diff = jnp.zeros((angles_here, LANES), F32)
    for m in held:
        diff = jnp.where(lane_of % mods == m, means_a[m] - means[m], diff)
    diff_row = jnp.sum(jnp.where(own, diff, 0.0), axis=0, keepdims=True)
    diff_send[...] = diff_row
    for peer in peers:
        remote(DIFF, diff_send, diff_recv.at[me], me, peer).start()
    diff_recv[me] = diff_row
    for p in range(devices):
        cent_send_b[p] = less_mean(flats[p], means, inside_late, p)
    send_all(CENT_B, cent_send_b, cent_recv_b)
    cent_recv_b[me] = cent_send_b[me]

    shared_row = iota((fold * angles_here, fold * angles_here), 0)
    shared_col = iota((fold * angles_here, fold * angles_here), 1)
    same = (shared_row // angles_here) == (shared_col // angles_here)
    shared_table = jnp.where(same, SHARED / angles_here, 0.0).astype(BF16)
    for p in range(devices):
        for send_ref, block_list in ((cent_send_a, early[p]), (cent_send_b, late[p])):
            shared = dot(shared_table, send_ref[p])
            for i, b in enumerate(block_list):
                part, at = divmod(i, mine // 2)
                piece = shared[
                    part * angles_here : (part + 1) * angles_here, at * LANES : (at + 1) * LANES
                ]
                clean_ref[:, (b + 1) * LANES : (b + 2) * LANES] = (
                    proj_ref[:, b * LANES : (b + 1) * LANES] - piece
                )
    clean_ref[:, 0:LANES] = jnp.zeros((angles_here, LANES), F32)
    clean_ref[:, W + LANES :] = jnp.zeros((angles_here, LANES), F32)
    for fetch in fetches[5:]:
        fetch.wait()

    def near_of(block_list):
        return jnp.concatenate(
            [clean_ref[:, b * LANES : (b + 3) * LANES] for b in block_list], axis=0
        )

    def ramp_known(block_list):
        high, low = halves(near_of(block_list))
        done = dot(high, taps_ref[...])
        done = done[:, :LANES] + done[:, LANES:] + dot(low, taps_ref[:, :LANES])
        for i, b in enumerate(block_list):
            out_ref[:, b * LANES : (b + 1) * LANES] = done[i * angles_here : (i + 1) * angles_here]

    def ramp_less(block_list):
        done = dot(near_of(block_list).astype(BF16), taps_ref[...])
        done = done[:, :LANES] + done[:, LANES:]
        for i, b in enumerate(block_list):
            at = b * LANES
            out_ref[:, at : at + LANES] = (
                out_ref[:, at : at + LANES] - done[i * angles_here : (i + 1) * angles_here]
            )

    for at in range(0, W // LANES, 16):
        ramp_known(range(at, at + 16))

    k = iota((rows, 1), 0)
    count_of = jnp.where((k == 0) | (2 * k == angles), 1.0, 2.0)
    count_of = jnp.where(2 * k <= angles, count_of, 0.0)

    def magnitude_of(spectrum):
        return jnp.sqrt(spectrum[:rows] * spectrum[:rows] + spectrum[rows:] * spectrum[rows:])

    def inside_mine(at):
        return inside_own_ref[me, :, at * half : (at + 1) * half]

    def summed(at, spectrum):
        magnitude = magnitude_of(spectrum)
        spec_ref[at] = spectrum
        size_ref[at] = magnitude
        over_k = jnp.sum(magnitude * count_of, axis=0, keepdims=True)
        spread = over_k * inside_mine(at)
        pieces = [spread[:, i * LANES : (i + 1) * LANES] for i in range(half // LANES)]
        return functools.reduce(jnp.add, pieces)

    member_own = [
        member_own_ref[me][:, i * half : (i + 1) * half] for i in range(2 * fold)
    ]

    wait_recv(CENT_A, cent_send_a, cent_recv_a)
    signal_a = cent_recv_a[...].reshape(devices * fold * angles_here, half)
    sums = jnp.zeros((8, LANES), F32)
    found = []
    for part in range(fold):
        spread = dot(fwd_ref[part], signal_a)
        found.append(spread[: 2 * rows] + spread[2 * rows :])
    for peer in peers:
        remote(DIFF, diff_send, diff_recv.at[peer], peer, peer).wait_recv()
    diffs = []
    for p in range(devices):
        spread = jnp.where(own, jnp.broadcast_to(diff_recv[p], (angles_here, LANES)), 0.0)
        diffs += [spread] * fold
    high, low = halves(jnp.concatenate(diffs, axis=0))
    shift = dot(fwd_ref[0], jnp.concatenate([high, low], axis=1))
    shift = shift[: 2 * rows] + shift[2 * rows :]
    high, low = halves(shift[:, :LANES] + shift[:, LANES:])
    shift = jnp.concatenate([high, low], axis=1)
    for part in range(fold):
        inside = jnp.concatenate([member_own[part]] * (2 * LANES // mods), axis=0)
        spectrum = found[part] + dot(shift, inside)
        sums = sums + summed(part, spectrum)

    wait_recv(CENT_B, cent_send_b, cent_recv_b)
    signal_b = cent_recv_b[...].reshape(devices * fold * angles_here, half)
    for part in range(fold):
        spread = dot(fwd_ref[part], signal_b)
        spectrum = spread[: 2 * rows] + spread[2 * rows :]
        sums = sums + summed(fold + part, spectrum)
    level_send[...] = sums
    hops = [hop for n in range(reach, 0, -1) for hop in (n, -n)]

    def near(hop, body):
        inside = me + hop < devices if hop > 0 else me + hop >= 0

        @pl.when(inside)
        def _():
            body(me + hop)

    for hop in hops:
        near(hop, lambda peer: remote(LEVEL, level_send, level_recv.at[me], me, peer).start())
    level_recv[me] = level_send[...]
    for at in range(2 * fold):
        size_ref[at] = 1.0 / size_ref[at]
        known_ref[at] = dot(shared_ref[at % fold], signal_a if at < fold else signal_b)
    wait_send(IDS, ids_send, ids_recv)
    wait_send(ROWS_A, rows_send_a, rows_recv_a)
    wait_send(ROWS_B, rows_send_b, rows_recv_b)
    for hop in hops:
        near(
            hop,
            lambda peer: remote(LEVEL, level_send, level_recv.at[peer], peer, peer).wait_recv(),
        )
    everything = jnp.sum(jnp.sum(level_recv[...], axis=0), axis=1, keepdims=True)
    level = SHRINK_SCALE * (everything / (angles * wide_column) + EPSILON)

    def inverse(at):
        level_col = jnp.sum(level * inside_mine(at), axis=0, keepdims=True)
        spectrum = spec_ref[at]
        factor = jnp.maximum(1.0 - level_col * size_ref[at], 0.0)
        shrunk = jnp.concatenate([spectrum[:rows] * factor, spectrum[rows:] * factor], axis=0)
        high, low = halves(shrunk)
        stripe = dot(inv_ref[...], jnp.concatenate([high, low, high], axis=0)) + known_ref[at]
        return stripe.reshape(devices, angles_here, half)

    both = [inverse(part) for part in range(fold)]
    stripe_send_a[...] = jnp.concatenate(both, axis=1).astype(BF16)
    send_all(STRIPE_A, stripe_send_a, stripe_recv_a)
    both = [inverse(fold + part) for part in range(fold)]
    stripe_send_b[...] = jnp.concatenate(both, axis=1).astype(BF16)
    send_all(STRIPE_B, stripe_send_b, stripe_recv_b)
    stripe_recv_a[me] = stripe_send_a[me]
    stripe_recv_b[me] = stripe_send_b[me]
    wait_send(CENT_A, cent_send_a, cent_recv_a)
    wait_send(CENT_B, cent_send_b, cent_recv_b)
    for peer in peers:
        remote(DIFF, diff_send, diff_recv.at[peer], peer, peer).wait_send()
    for hop in hops:
        near(
            hop,
            lambda peer: remote(LEVEL, level_send, level_recv.at[peer], peer, peer).wait_send(),
        )

    def spread_stripe(recv_ref, block_lists):
        for p in range(devices):
            rest = recv_ref[p].astype(F32)
            for i, b in enumerate(block_lists[p]):
                part, at = divmod(i, mine // 2)
                piece = rest[
                    part * angles_here : (part + 1) * angles_here, at * LANES : (at + 1) * LANES
                ]
                clean_ref[:, (b + 1) * LANES : (b + 2) * LANES] = piece

    wait_recv(STRIPE_A, stripe_send_a, stripe_recv_a)
    spread_stripe(stripe_recv_a, early)
    found_early = {b for run in early for b in run}
    inner = [b for b in sorted(found_early) if b - 1 in found_early and b + 1 in found_early]
    outer = [b for b in range(W // LANES) if b not in set(inner)]
    for at in range(0, len(inner), 16):
        ramp_less(inner[at : at + 16])
    wait_recv(STRIPE_B, stripe_send_b, stripe_recv_b)
    spread_stripe(stripe_recv_b, late)
    for at in range(0, len(outer), 16):
        ramp_less(outer[at : at + 16])
    wait_send(STRIPE_A, stripe_send_a, stripe_recv_a)
    wait_send(STRIPE_B, stripe_send_b, stripe_recv_b)


def fast_call(cfg, plan, tables, args):
    devices, angles_here, tiles, tile_width, mods, fold = cfg
    cap, split, mine = plan[0], plan[1], plan[6]
    rows = freq_rows(devices * angles_here)
    half = mine * LANES // 2
    cells = plan[3]
    blocks = angles_here * tiles
    hot_rows = blocks + 16
    for k in range(cap):
        hot_rows += len({block for (_, at), (_, block) in cells.items() if at == k}) * blocks + 16
    hot_rows = -(-hot_rows // 16) * 16
    vmem = pl.BlockSpec(memory_space=pltpu.VMEM)
    message = pltpu.VMEM((devices, fold * angles_here, half), BF16)
    line = pltpu.VMEM((1, LANES), F32)
    lines = pltpu.VMEM((devices, 1, LANES), F32)
    rows_a = pltpu.VMEM((devices, 16, split * LANES), BF16)
    rows_b = pltpu.VMEM((devices, 16, (cap - split) * LANES), BF16)
    return pl.pallas_call(
        functools.partial(fast_kernel, cfg, plan),
        out_shape=pltpu.VMEM((angles_here, W), F32),
        in_specs=[pl.BlockSpec(memory_space=pl.ANY)] * 9,
        out_specs=vmem,
        scratch_shapes=[
            *[pltpu.VMEM(arg.shape, arg.dtype) for arg in args],
            rows_a,
            rows_a,
            rows_b,
            rows_b,
            lines,
            lines,
            pltpu.VMEM((angles_here * tiles, tile_width), F32),
            pltpu.VMEM((angles_here, W + 2 * LANES), F32),
            pltpu.VMEM((angles_here, W), F32),
            pltpu.VMEM((hot_rows, LANES), BF16),
            pltpu.VMEM((2, tiles - 1, angles_here, (plan[5] + plan[4]) * LANES), F32),
            pltpu.VMEM((mods, W), BF16),
            pltpu.VMEM((devices, mods, 2 * mine * LANES), BF16),
            pltpu.VMEM((8, W), F32),
            pltpu.VMEM((devices, 8, 2 * mine * LANES), F32),
            message,
            message,
            message,
            message,
            line,
            lines,
            pltpu.VMEM((2 * fold, 2 * rows, half), F32),
            pltpu.VMEM((2 * fold, rows, half), F32),
            pltpu.VMEM((8, LANES), F32),
            pltpu.VMEM((devices, 8, LANES), F32),
            message,
            message,
            message,
            message,
            pltpu.VMEM((2 * fold, devices * angles_here, half), F32),
            *[pltpu.VMEM(table.shape, BF16) for table in tables],
            pltpu.SemaphoreType.DMA((9,)),
            pltpu.SemaphoreType.DMA((9, devices)),
            pltpu.SemaphoreType.DMA((9, devices)),
        ],
        compiler_params=pltpu.CompilerParams(
            collective_id=0, has_side_effects=True, vmem_limit_bytes=60 << 20
        ),
    )(*args, *[jnp.asarray(table) for table in tables])


def per_device(raw, block_dest, section_offset, ramp_length, module_width):
    devices = lax.axis_size("ang")
    blocks_here = raw.shape[0]
    tile_width = raw.shape[1]
    angles_here, tiles = section_offset.shape
    angles = angles_here * devices
    capacity = (blocks_here + devices - 1) // devices
    cols = W // devices
    fold = 2 if cols % (2 * LANES) == 0 else 1
    wire = BF16 if fold == 2 else F32
    mods = -(-module_width.shape[0] // 16) * 16
    half = cols // fold
    rows = freq_rows(angles)
    cfg = (devices, angles_here, tiles, tile_width, mods, fold)
    forward = forward_table(angles, devices, fold)
    inverse = inverse_table(angles, devices, fold)
    taps = ramp_table()
    plan = fast_plan(devices, angles_here, tiles, tile_width, mods, module_width.shape[0])
    if fold == 2 and plan:
        args = (
            raw,
            block_dest[None, :],
            section_offset,
            ramp_length[None, :],
            module_width[None, :],
        )
        depth = 3 * 2 * rows
        tables = (
            forward,
            inverse[0][:, :depth],
            np.concatenate(list(taps), axis=1),
            inverse[:, :, depth:],
        )
        return fast_call(cfg, plan, tables, args)
    vmem = pl.BlockSpec(memory_space=pltpu.VMEM)
    return pl.pallas_call(
        functools.partial(kernel, cfg),
        out_shape=pltpu.VMEM((angles_here, W), F32),
        in_specs=[vmem] * 5 + [pl.BlockSpec(memory_space=pl.ANY)] * 3,
        out_specs=vmem,
        scratch_shapes=[
            pltpu.VMEM((devices, 16, capacity * LANES), BF16),
            pltpu.VMEM((devices, 16, capacity * LANES), BF16),
            pltpu.VMEM((angles_here * tiles, tile_width), F32),
            pltpu.VMEM((angles_here, W + 2 * LANES), F32),
            pltpu.VMEM((angles_here, W + 2 * LANES), F32),
            pltpu.VMEM((angles_here, W), F32),
            pltpu.VMEM((devices, angles_here * fold, half), wire),
            pltpu.VMEM((devices, angles_here * fold, half), wire),
            pltpu.VMEM((fold, 2 * rows, half), F32),
            pltpu.VMEM((8, max(mods, LANES)), F32),
            pltpu.VMEM((devices, 8, max(mods, LANES)), F32),
            pltpu.VMEM((devices, angles_here * fold, half), wire),
            pltpu.VMEM((devices, angles_here * fold, half), wire),
            pltpu.VMEM((devices, 1, LANES), F32),
            pltpu.VMEM((devices, 1, LANES), F32),
            pltpu.VMEM(forward.shape, BF16),
            pltpu.VMEM(inverse.shape, BF16),
            pltpu.VMEM(taps.shape, BF16),
            pltpu.SemaphoreType.DMA((3,)),
            pltpu.SemaphoreType.DMA((5, devices)),
            pltpu.SemaphoreType.DMA((5, devices)),
        ],
        compiler_params=pltpu.CompilerParams(
            collective_id=0, has_side_effects=True, vmem_limit_bytes=60 << 20
        ),
    )(
        raw,
        block_dest[None, :],
        section_offset,
        ramp_length[None, :],
        module_width[None, :],
        jnp.asarray(forward),
        jnp.asarray(inverse),
        jnp.asarray(taps),
    )


def solution(mesh):
    in_specs = (P(("row", "ang"), None), P("ang"), P("ang", None), P(), P())
    out_specs = P(("row", "ang"), None)
    return jax.shard_map(
        per_device, mesh=mesh, in_specs=in_specs, out_specs=out_specs, check_vma=False
    )
```
